32 devices in a mesh: fsdp: 4 (over x, core), context: 4 (over z), tensor: 2 (over y).
Axes of the slice: x: 2, y: 2, z: 4, core: 2. Of those that a mesh axis runs over, the one named last changes fastest.
Arguments:
- tokens: bfloat16 [4096, 1536], P(('fsdp', 'context')), may hold values from -6 to 6
- cotangent: bfloat16 [4096, 1536], P(('fsdp', 'context')), may hold values from -6 to 6
- lengths: int32 [4, 3], P('fsdp'), may hold values from 256 to 384, as said below
- span_order: int32 [4, 4, 4], P('fsdp'), may hold values from 0 to 3, each once within a row
- attn_gain: float32 [1536], P('fsdp'), may hold values from 0.5 to 1.5
- w_q: float32 [1536, 1536], P('fsdp', 'tensor'), may hold values from -0.15625 to 0.15625
- b_q: float32 [12, 128], P('tensor', 'fsdp'), may hold values from -3 to 3
- w_k: float32 [1536, 256], P('fsdp', 'tensor'), may hold values from -0.15625 to 0.15625
- b_k: float32 [2, 128], P('tensor', 'fsdp'), may hold values from -3 to 3
- w_v: float32 [1536, 256], P('fsdp', 'tensor'), may hold values from -0.15625 to 0.15625
- b_v: float32 [2, 128], P('tensor', 'fsdp'), may hold values from -3 to 3
- w_o: float32 [1536, 1536], P('tensor', 'fsdp'), may hold values from -1.75 to 1.75
- mlp_gain: float32 [1536], P('fsdp'), may hold values from 0.5 to 1.5
- w_gate: float32 [1536, 8960], P('fsdp', 'tensor'), may hold values from -0.15625 to 0.15625
- w_up: float32 [1536, 8960], P('fsdp', 'tensor'), may hold values from -0.15625 to 0.15625
- w_down: float32 [8960, 1536], P('tensor', 'fsdp'), may hold values from -0.0625 to 0.0625
Outputs:
- out: float32 [4096, 1536], P(('fsdp', 'context'))
- grad_tokens: float32 [4096, 1536], P(('fsdp', 'context'))
- grad_attn_gain: float32 [1536], P('fsdp')
- grad_w_q: float32 [1536, 1536], P('fsdp', 'tensor')
- grad_b_q: float32 [12, 128], P('tensor', 'fsdp')
- grad_w_k: float32 [1536, 256], P('fsdp', 'tensor')
- grad_b_k: float32 [2, 128], P('tensor', 'fsdp')
- grad_w_v: float32 [1536, 256], P('fsdp', 'tensor')
- grad_b_v: float32 [2, 128], P('tensor', 'fsdp')
- grad_w_o: float32 [1536, 1536], P('tensor', 'fsdp')
- grad_mlp_gain: float32 [1536], P('fsdp')
- grad_w_gate: float32 [1536, 8960], P('fsdp', 'tensor')
- grad_w_up: float32 [1536, 8960], P('fsdp', 'tensor')
- grad_w_down: float32 [8960, 1536], P('tensor', 'fsdp')
The draws below stay inside these ranges and needn't reach their ends.
Inputs may be any that keep to these rules, and one draw needn't show every extreme that they name: Row f lists the lengths of the 3 sequences packed in order into the 1024 rows of group f; they sum to 1024, and one of them is exactly 384 long. Each row span_order[f, c] is a permutation of 0 to 3.
All inputs are finite; a program needn't handle non-finite values.
Results may differ from the reference program's by a relative error of at most 0.018.
Values may be sent and summed in bfloat16 or wider, within the bound.
No kernel may reach another device: no remote copies, remote signals or barrier semaphores. Data moves between devices by JAX's collectives and lax.ppermute only.
A program may use at most 256 MiB of HBM per device.

```python
import jax
import jax.numpy as jnp
from jax import lax

D = 1536
HEADS = 12
KV_HEADS = 2
HD = 128
FF = 8960
TOK_DEV = 256
GROUP_TOK = 1024
MOST = 384
SHORTEST = 256
TOKENS = 4096
N_FSDP = 4
N_CONTEXT = 4


def draw_lengths(key, part):
    key_len, key_order = jax.random.split(jax.random.fold_in(key, 17))
    middle_len = jax.random.randint(key_len, (N_FSDP,), SHORTEST, MOST + 1, dtype=jnp.int32)
    last_len = (GROUP_TOK - MOST - middle_len).astype(jnp.int32)
    length_rows = jnp.stack([jnp.full((N_FSDP,), MOST, jnp.int32), middle_len, last_len], axis=1)
    scores = jax.random.randint(key_order, (N_FSDP, 3), 0, 1000, dtype=jnp.int32) * 3 + jnp.arange(3, dtype=jnp.int32)[None, :]
    placing_order = jnp.argsort(scores, axis=1, stable=True).astype(jnp.int32)
    return jnp.take_along_axis(length_rows, placing_order, axis=1)


def block_scale(own_key, shape, cuts, low, largest):
    def one(dim, shards_of):
        heights = jax.random.uniform(jax.random.fold_in(jax.random.fold_in(own_key, 6), dim), (shards_of,), jnp.float32, low / len(cuts), largest / len(cuts))
        return jnp.repeat(jnp.exp(heights), shape[dim] // shards_of).reshape((-1,) + (1,) * (len(shape) - dim - 1))

    factor_of = one(*cuts[0])
    for cut in cuts[1:]:
        factor_of = factor_of * one(*cut)
    return factor_of


def bell_draw(own_key, extent, deviation, bound, pieces=(), held_as=jnp.bfloat16):
    values = deviation * jax.random.normal(own_key, extent, jnp.float32)
    if pieces:
        values = values * block_scale(own_key, extent, pieces, -0.22, 0.18)
    return jnp.clip(values, -bound, bound).astype(held_as)


def setup_inputs(seed: int = 0) -> dict:
    arg_keys = jax.random.split(jax.random.key(seed), 17)
    return {
        "tokens": bell_draw(arg_keys[0], (TOKENS, D), 1.0, 6.0, ((0, 16),)),
        "cotangent": bell_draw(arg_keys[1], (TOKENS, D), 1.0, 6.0, ((0, 16),)),
        "lengths": draw_lengths(jax.random.fold_in(arg_keys[16], 71), 0),
        "span_order": jax.vmap(lambda own: jax.random.permutation(own, N_CONTEXT))(jax.random.split(arg_keys[3], N_FSDP * N_CONTEXT)).reshape((N_FSDP, N_CONTEXT, N_CONTEXT)).astype(jnp.int32),
        "attn_gain": jnp.clip(1.0 + 0.1 * jax.random.normal(arg_keys[4], (D,), jnp.float32), 0.5, 1.5),
        "w_q": bell_draw(arg_keys[5], (D, HEADS * HD), D ** -0.5, 0.15625, ((0, 4), (1, 2)), jnp.float32),
        "b_q": bell_draw(arg_keys[6], (HEADS, HD), 0.5, 3.0, ((0, 2), (1, 4)), jnp.float32),
        "w_k": bell_draw(arg_keys[7], (D, KV_HEADS * HD), D ** -0.5, 0.15625, ((0, 4), (1, 2)), jnp.float32),
        "b_k": bell_draw(arg_keys[8], (KV_HEADS, HD), 0.5, 3.0, ((0, 2), (1, 4)), jnp.float32),
        "w_v": bell_draw(arg_keys[9], (D, KV_HEADS * HD), D ** -0.5, 0.15625, ((0, 4), (1, 2)), jnp.float32),
        "b_v": bell_draw(arg_keys[10], (KV_HEADS, HD), 0.5, 3.0, ((0, 2), (1, 4)), jnp.float32),
        "w_o": bell_draw(arg_keys[11], (HEADS * HD, D), (HEADS * HD // 128) ** -0.5, 1.75, ((0, 2), (1, 4)), jnp.float32),
        "mlp_gain": jnp.clip(1.0 + 0.1 * jax.random.normal(arg_keys[12], (D,), jnp.float32), 0.5, 1.5),
        "w_gate": bell_draw(arg_keys[13], (D, FF), D ** -0.5, 0.15625, ((0, 4), (1, 2)), jnp.float32),
        "w_up": bell_draw(arg_keys[14], (D, FF), D ** -0.5, 0.15625, ((0, 4), (1, 2)), jnp.float32),
        "w_down": bell_draw(arg_keys[15], (FF, D), FF ** -0.5, 0.0625, ((0, 2), (1, 4)), jnp.float32),
    }


@jax.custom_vjp
def low(v):
    return lax.optimization_barrier(v.astype(jnp.bfloat16)).astype(jnp.float32)

@jax.custom_vjp
def low_back(v):
    return v

def low_keep(v):
    return (low(v), None)

def low_pass(kept, grad):
    return (grad,)

def back_keep(v):
    return (v, None)

def back_low(kept, grad):
    return (low(grad),)
low.defvjp(low_keep, low_pass)
low_back.defvjp(back_keep, back_low)
epsilon = 1e-06
rope_base = 10000.0
neg_big = -1e+30

def matmul(left_op, right_op):
    return jnp.dot(left_op, right_op, precision=lax.Precision.HIGHEST, preferred_element_type=jnp.float32)

def rms_scale(values):
    return lax.rsqrt(lax.optimization_barrier(jnp.mean(values * values, axis=-1, keepdims=True)) + epsilon)

def rotary_tables(position):
    half_dim = HD // 2
    frequency = rope_base ** (-(jnp.arange(half_dim, dtype=jnp.float32) * 2.0) / HD)
    angles = position.astype(jnp.float32)[:, None] * frequency[None, :]
    angles = jnp.concatenate([angles, angles], axis=1)
    return (jnp.cos(angles), jnp.sin(angles))

def rotate(values, cos_table, sin_table):
    half_dim = HD // 2
    turned = jnp.concatenate([-values[..., half_dim:], values[..., :half_dim]], axis=-1)
    return values * cos_table[:, None, :] + turned * sin_table[:, None, :]

def locate(packed, seq_lengths):
    seq_ends = jnp.cumsum(seq_lengths).astype(jnp.int32)
    seq_starts = (seq_ends - seq_lengths).astype(jnp.int32)
    segment = lax.optimization_barrier(jnp.sum((packed[:, None] >= seq_ends[None, :]).astype(jnp.int32), axis=1)).astype(jnp.int32)
    inside = segment[:, None] == jnp.arange(seq_lengths.shape[0], dtype=jnp.int32)[None, :]
    offset = lax.optimization_barrier(jnp.sum(jnp.where(inside, seq_starts[None, :], 0), axis=1)).astype(jnp.int32)
    return (segment, (packed - offset).astype(jnp.int32))

def decoder_layer(params, inputs, seq_lengths):
    attn_gain, w_q, b_q, w_k, b_k, w_v, b_v, w_o, mlp_gain, w_gate, w_up, w_down = params
    group_tok = inputs.shape[0]
    packed = jnp.arange(group_tok, dtype=jnp.int32)
    segment, position = locate(packed, seq_lengths)
    cos_table, sin_table = rotary_tables(position)
    normed = low(inputs * rms_scale(inputs) * low(attn_gain))
    query_proj = low_back(matmul(normed, low(w_q)) + low(b_q).reshape(-1))
    key_proj = low_back(matmul(normed, low(w_k)) + low(b_k).reshape(-1))
    value_proj = low(low_back(matmul(normed, low(w_v)) + low(b_v).reshape(-1)))
    query_rot = low(rotate(query_proj.reshape(group_tok, HEADS, HD), cos_table, sin_table))
    key_rot = low(rotate(key_proj.reshape(group_tok, KV_HEADS, HD), cos_table, sin_table))
    group_size = HEADS // KV_HEADS
    key_all = jnp.repeat(key_rot, group_size, axis=1)
    value_all = jnp.repeat(value_proj.reshape(group_tok, KV_HEADS, HD), group_size, axis=1)
    block_rows = min(512, group_tok)
    block_count = group_tok // block_rows

    def attend(block_args):
        q_block, q_seg, q_pack = block_args
        scores = jnp.einsum('qhd,khd->hqk', q_block, key_all, precision=lax.Precision.HIGHEST) * HD ** (-0.5)
        scores = low_back(scores)
        allowed = (q_seg[:, None] == segment[None, :]) & (packed[None, :] <= q_pack[:, None])
        scores = jnp.where(allowed[None], scores, neg_big)
        row_top = lax.optimization_barrier(jnp.max(scores, axis=-1, keepdims=True))
        log_sum = row_top + jnp.log(lax.optimization_barrier(jnp.sum(jnp.exp(scores - row_top), axis=-1, keepdims=True)))
        weights = low(jnp.exp(scores - log_sum))
        return jnp.einsum('hqk,khd->qhd', weights, value_all, precision=lax.Precision.HIGHEST)
    blocks = lax.map(jax.checkpoint(attend), (query_rot.reshape(block_count, block_rows, HEADS, HD), segment.reshape(block_count, block_rows), packed.reshape(block_count, block_rows)))
    attended = low(low_back(blocks.reshape(group_tok, HEADS * HD)))
    middle = inputs + low_back(matmul(attended, low(w_o)))
    normed_two = low(middle * rms_scale(middle) * low(mlp_gain))
    gate_proj = low_back(matmul(normed_two, low(w_gate)))
    up_proj = low_back(matmul(normed_two, low(w_up)))
    hidden = low(jax.nn.silu(gate_proj) * up_proj)
    return middle + low_back(matmul(hidden, low(w_down)))

def reference(tokens, cotangent, lengths, span_order, attn_gain, w_q, b_q, w_k, b_k, w_v, b_v, w_o, mlp_gain, w_gate, w_up, w_down):
    params = (attn_gain, w_q, b_q, w_k, b_k, w_v, b_v, w_o, mlp_gain, w_gate, w_up, w_down)
    span_rows = TOK_DEV // N_CONTEXT
    order_index = span_order.astype(jnp.int32)[:, :, :, None, None]
    inverse_index = jnp.argsort(span_order, axis=-1).astype(jnp.int32)[:, :, :, None, None]

    def to_packed(values):
        stored = values.astype(jnp.float32).reshape(N_FSDP, N_CONTEXT, N_CONTEXT, span_rows, D)
        packed = jnp.take_along_axis(stored, inverse_index, axis=2)
        return packed.reshape(N_FSDP, N_CONTEXT * TOK_DEV, D)

    def to_stored(values):
        packed = values.reshape(N_FSDP, N_CONTEXT, N_CONTEXT, span_rows, D)
        stored = jnp.take_along_axis(packed, order_index, axis=2)
        return stored.reshape(N_FSDP * N_CONTEXT * TOK_DEV, D)

    def one_group(grad_total, group_args):
        values, grads_out, seq_lengths = group_args
        result, pull_back = jax.vjp(lambda weights, inputs: decoder_layer(weights, inputs, seq_lengths), params, values)
        grad_params, grad_values = pull_back(grads_out)
        grad_total = jax.tree.map(lambda first, second: first + second, grad_total, grad_params)
        return (grad_total, (result, grad_values))
    zero_grads = jax.tree.map(jnp.zeros_like, params)
    grad_total, outputs = lax.scan(one_group, zero_grads, (to_packed(tokens), to_packed(cotangent), lengths))
    return (to_stored(outputs[0]), to_stored(outputs[1]), grad_total[0], grad_total[1], grad_total[2], grad_total[3], grad_total[4], grad_total[5], grad_total[6], grad_total[7], grad_total[8], grad_total[9], grad_total[10], grad_total[11])
```

```python
import functools

import jax
import jax.numpy as jnp
from jax import lax
from jax.experimental import pallas as pl
from jax.experimental.pallas import tpu as pltpu
from jax.sharding import PartitionSpec as P

D = 1536
HD = 128
LANES = 128
TEAM = 2
PARTS = 2

epsilon = 1e-06
rope_base = 10000.0
neg_big = -1e30
far_away = 1 << 29
bf16 = jnp.bfloat16
f32 = jnp.float32


def dot_plain(left_op, right_op):
    return jnp.dot(left_op, right_op, preferred_element_type=f32)


def dot_rows(left_op, right_op):
    return lax.dot_general(
        left_op, right_op, (((0,), (0,)), ((), ())), preferred_element_type=f32
    )


def dot_cols(left_op, right_op):
    return lax.dot_general(
        left_op, right_op, (((1,), (1,)), ((), ())), preferred_element_type=f32
    )


def swap(values, axis_name, bit):
    size = lax.axis_size(axis_name)
    return lax.ppermute(values, axis_name, [(i, i ^ bit) for i in range(size)])


def shift(values, axis_name, step):
    size = lax.axis_size(axis_name)
    pairs = [(i, i + step) for i in range(size) if 0 <= i + step < size]
    return lax.ppermute(values, axis_name, pairs)


def bits_of(size):
    found = []
    bit = 1
    while bit < size:
        found.append(bit)
        bit *= 2
    return found


def fsdp_order(size):
    order = [0]
    for bit in reversed(bits_of(size)):
        order = order + [held ^ bit for held in order]
    return order


def gather_pieces(piece):
    pieces = [piece]
    for bit in reversed(bits_of(lax.axis_size("fsdp"))):
        pieces = pieces + [swap(held, "fsdp", bit) for held in pieces]
    return pieces


def xor_blocks(blocks, index, size):
    for bit in bits_of(size):
        on = (index & bit) != 0
        blocks = [jnp.where(on, blocks[i ^ bit], blocks[i]) for i in range(size)]
    return blocks


def to_relative(values, index, size):
    width = values.shape[-1] // size
    blocks = [values[..., i * width : (i + 1) * width] for i in range(size)]
    blocks = xor_blocks(blocks, index, size)
    return jnp.concatenate([blocks[i] for i in fsdp_order(size)], axis=-1)


def from_relative(values, index, size):
    width = values.shape[-1] // size
    order = fsdp_order(size)
    blocks = [None] * size
    for place, i in enumerate(order):
        blocks[i] = values[..., place * width : (place + 1) * width]
    return jnp.concatenate(xor_blocks(blocks, index, size), axis=-1)


def reduce_fsdp(values, axis):
    for bit in bits_of(lax.axis_size("fsdp")):
        half = values.shape[axis] // 2
        kept = lax.slice_in_dim(values, 0, half, axis=axis)
        sent = lax.slice_in_dim(values, half, 2 * half, axis=axis).astype(bf16)
        values = kept.astype(f32) + swap(sent, "fsdp", bit).astype(f32)
    return values


def sum_context(values):
    index = lax.axis_index("context")
    bits = bits_of(lax.axis_size("context"))
    for bit in bits:
        half = values.shape[0] // 2
        on = (index & bit) != 0
        kept = jnp.where(on, values[half:], values[:half])
        sent = jnp.where(on, values[:half], values[half:]).astype(bf16)
        values = kept + swap(sent, "context", bit).astype(f32)
    values = values.astype(bf16)
    for bit in reversed(bits):
        on = (index & bit) != 0
        other = swap(values, "context", bit)
        values = jnp.concatenate(
            [jnp.where(on, other, values), jnp.where(on, values, other)], axis=0
        )
    return values.astype(f32)


def turn_sign(shape):
    lane = lax.broadcasted_iota(jnp.int32, shape, 1)
    return jnp.where(lane < HD // 2, -1.0, 1.0)


def attend_body(q_ref, kv_ref, low_ref, high_ref, key_ref, o_ref):
    scores = dot_cols(q_ref[...], kv_ref[:, :HD]) * HD ** (-0.5)
    key_at = key_ref[...]
    allowed = (key_at >= low_ref[...]) & (key_at <= high_ref[...])
    scores = jnp.where(allowed, scores, neg_big)
    top = jnp.max(scores, axis=-1, keepdims=True)
    raised = jnp.exp(scores - top)
    weights = raised * (1.0 / jnp.sum(raised, axis=-1, keepdims=True))
    o_ref[...] = dot_plain(weights.astype(bf16), kv_ref[:, HD:]).astype(bf16)


def attend_back_body(
    q_ref, g_ref, kv_ref, low_ref, high_ref, key_ref, cos_ref, sin_ref, dq_ref, dkv_ref
):
    scale = HD ** (-0.5)
    queries = q_ref[...]
    grad = g_ref[...]
    keys = kv_ref[:, :HD]
    scores = dot_cols(queries, keys) * scale
    key_at = key_ref[...]
    allowed = (key_at >= low_ref[...]) & (key_at <= high_ref[...])
    scores = jnp.where(allowed, scores, neg_big)
    top = jnp.max(scores, axis=-1, keepdims=True)
    raised = jnp.exp(scores - top)
    weights = raised * (1.0 / jnp.sum(raised, axis=-1, keepdims=True))
    dweights = dot_cols(grad, kv_ref[:, HD:])
    delta = jnp.sum(weights * dweights, axis=-1, keepdims=True)
    dscores = (weights * (dweights - delta)).astype(bf16)
    dq_rot = dot_plain(dscores, keys) * scale
    turned = pltpu.roll(dq_rot, HD // 2, 1)
    dq_ref[...] = (dq_rot * cos_ref[...] - turned * sin_ref[...]).astype(bf16)
    dkeys = dot_rows(dscores, queries) * scale
    dvalues = dot_rows(weights.astype(bf16), grad)

    @pl.when(pl.program_id(0) == 0)
    def _():
        dkv_ref[:, :HD] = dkeys
        dkv_ref[:, HD:] = dvalues

    @pl.when(pl.program_id(0) != 0)
    def _():
        dkv_ref[:, :HD] += dkeys
        dkv_ref[:, HD:] += dvalues


def whole_spec(array):
    return pl.BlockSpec(array.shape, lambda h: (0,) * array.ndim)


def attend(queries, kv_all, low, high, key_at):
    rows, width = queries.shape
    head = pl.BlockSpec((rows, HD), lambda h: (0, h))
    keys = kv_all.shape[0]
    return pl.pallas_call(
        attend_body,
        out_shape=jax.ShapeDtypeStruct(queries.shape, bf16),
        grid=(width // HD,),
        in_specs=[head] + [whole_spec(a) for a in (kv_all, low, high, key_at)],
        out_specs=head,
        compiler_params=pltpu.CompilerParams(vmem_limit_bytes=32 << 20),
        cost_estimate=pl.CostEstimate(
            flops=4 * rows * width * keys,
            transcendentals=rows * keys * (width // HD),
            bytes_accessed=4 * rows * width + 4 * keys * HD,
        ),
    )(queries, kv_all, low, high, key_at)


def attend_back(queries, grad, kv_all, low, high, key_at, cos_table, sin_table):
    rows, width = queries.shape
    head = pl.BlockSpec((rows, HD), lambda h: (0, h))
    keys = kv_all.shape[0]
    rest = (kv_all, low, high, key_at, cos_table, sin_table)
    return pl.pallas_call(
        attend_back_body,
        out_shape=(
            jax.ShapeDtypeStruct(queries.shape, bf16),
            jax.ShapeDtypeStruct(kv_all.shape, f32),
        ),
        grid=(width // HD,),
        in_specs=[head, head] + [whole_spec(a) for a in rest],
        out_specs=(head, whole_spec(kv_all)),
        compiler_params=pltpu.CompilerParams(vmem_limit_bytes=48 << 20),
        cost_estimate=pl.CostEstimate(
            flops=10 * rows * width * keys,
            transcendentals=rows * keys * (width // HD),
            bytes_accessed=6 * rows * width + 12 * keys * HD,
        ),
    )(queries, grad, *rest)


def swiglu_grads(gate_proj, up_proj, d_hidden, shown):
    gate_sig = jax.nn.sigmoid(gate_proj)
    activated = gate_proj * gate_sig
    hidden = activated * up_proj
    d_gate = d_hidden * up_proj * gate_sig * (1.0 + gate_proj * (1.0 - gate_sig))
    d_up = d_hidden * activated
    if shown is not None:
        hidden, d_gate, d_up = (jnp.where(shown, v, 0.0) for v in (hidden, d_gate, d_up))
    return hidden.astype(bf16), d_gate.astype(bf16), d_up.astype(bf16)


def rms_scale(values):
    return lax.rsqrt(jnp.mean(values * values, axis=-1, keepdims=True) + epsilon)


def per_device(
    tokens,
    cotangent,
    lengths,
    span_order,
    attn_gain,
    w_q,
    b_q,
    w_k,
    b_k,
    w_v,
    b_v,
    w_o,
    mlp_gain,
    w_gate,
    w_up,
    w_down,
):
    n_fsdp = lax.axis_size("fsdp")
    n_ctx = lax.axis_size("context")
    my_fsdp = lax.axis_index("fsdp")
    my_ctx = lax.axis_index("context")
    my_tensor = lax.axis_index("tensor")
    member = my_ctx % TEAM
    rows = tokens.shape[0]
    half = rows // 2
    piece_rows = rows // n_ctx
    shard = D // n_fsdp
    q_width = w_q.shape[1]
    kv_width = w_k.shape[1]
    qkv_width = q_width + 2 * kv_width
    heads_local = q_width // HD
    all_heads = qkv_width // HD
    flipped = my_tensor != 0

    def mine_first(values):
        first, second = values[:half], values[half:]
        return jnp.concatenate(
            [jnp.where(flipped, second, first), jnp.where(flipped, first, second)], axis=0
        )

    extras = jnp.concatenate(
        [
            attn_gain.astype(bf16),
            mlp_gain.astype(bf16),
            jnp.concatenate([b_q, b_k, b_v], axis=0).astype(bf16).reshape(-1),
        ]
    )
    extras = jnp.pad(extras, (0, qkv_width - extras.shape[0]))
    extra_rows = jnp.pad(extras[None, :], ((0, 15), (0, 0)))
    qkv_pack = jnp.concatenate(
        [jnp.concatenate([w_q, w_k, w_v], axis=1).astype(bf16), extra_rows], axis=0
    )
    qkv_pieces = gather_pieces(qkv_pack)
    qkv_w = jnp.concatenate([p[:shard] for p in qkv_pieces], axis=0)
    gain_one = jnp.concatenate([p[shard, :shard] for p in qkv_pieces]).astype(f32)[None, :]
    gain_two = (
        jnp.concatenate([p[shard, shard : 2 * shard] for p in qkv_pieces]).astype(f32)[None, :]
    )
    bias_cols = HD // n_fsdp
    bias_size = all_heads * bias_cols
    order = fsdp_order(n_fsdp)
    bias_blocks = [None] * n_fsdp
    for place, i in enumerate(order):
        bias_blocks[i] = (
            qkv_pieces[place][shard, 2 * shard : 2 * shard + bias_size]
            .astype(f32)
            .reshape(all_heads, bias_cols)
        )
    bias = jnp.concatenate(xor_blocks(bias_blocks, my_fsdp, n_fsdp), axis=1).reshape(1, -1)
    out_w = jnp.concatenate(gather_pieces(w_o.astype(bf16)), axis=1)

    ff_local = w_gate.shape[1]
    tiles = ff_local // LANES
    slice_tiles = -(-tiles // (TEAM * PARTS)) * PARTS
    part = slice_tiles // PARTS * LANES
    starts = [min(s * slice_tiles, tiles - slice_tiles) * LANES for s in range(TEAM)]
    fresh = [s * slice_tiles * LANES - starts[s] for s in range(TEAM)]

    def own_part(values, axis, index):
        chosen = lax.slice_in_dim(values, starts[0] + index * part, starts[0] + (index + 1) * part, axis=axis)
        for s in range(1, TEAM):
            other = lax.slice_in_dim(values, starts[s] + index * part, starts[s] + (index + 1) * part, axis=axis)
            chosen = jnp.where(member == s, other, chosen)
        return chosen.astype(bf16)

    up_gate_w, down_w = [], []
    for index in range(PARTS):
        both = jnp.concatenate([own_part(w_gate, 1, index), own_part(w_up, 1, index)], axis=1)
        up_gate_w.append(jnp.concatenate(gather_pieces(both), axis=0))
        down_w.append(jnp.concatenate(gather_pieces(own_part(w_down, 0, index)), axis=1))

    own_tokens = to_relative(mine_first(tokens), my_fsdp, n_fsdp)
    own_grad = to_relative(mine_first(cotangent), my_fsdp, n_fsdp)

    def gather_rows(mine):
        held = jnp.concatenate([mine, swap(mine, "context", 1)], axis=0)
        team = jnp.concatenate([held, swap(held, "tensor", 1)], axis=0)
        others = []
        for bit in bits_of(n_ctx)[1:]:
            arrived = swap(held, "context", bit)
            others.append(arrived)
            held = jnp.concatenate([held, arrived], axis=0)
        remote = jnp.concatenate(others, axis=0)
        return team, jnp.concatenate([remote, swap(remote, "tensor", 1)], axis=0)

    grad_team, grad_remote = gather_rows(own_grad[:half])

    seq_lengths = lengths[0]
    seq_ends = jnp.cumsum(seq_lengths)
    seq_starts = seq_ends - seq_lengths
    row = jnp.arange(rows, dtype=jnp.int32)
    stored = jnp.where(flipped, (row + half) % rows, row)

    def packed_of(context):
        owner = lax.dynamic_index_in_dim(span_order[0], context, 0, keepdims=False)
        span = stored // piece_rows
        hot = span[:, None] == jnp.arange(n_ctx, dtype=jnp.int32)[None, :]
        place = jnp.sum(jnp.where(hot, owner[None, :], 0), axis=1)
        return context * rows + place * piece_rows + stored % piece_rows

    own_at = packed_of(my_ctx)
    passed = own_at[:, None] >= seq_ends[None, :]
    begin = jnp.max(jnp.where(passed, seq_ends[None, :], 0), axis=1)
    position = own_at - begin
    longest = 3 * n_ctx * rows // 8
    behind = min(n_ctx - 1, (longest - 1 + rows - 1) // rows)
    key_at = [own_at]
    for step in range(1, behind + 1):
        there = packed_of(jnp.maximum(my_ctx - step, 0))
        key_at.append(jnp.where(my_ctx >= step, there, far_away))
    key_at = jnp.concatenate(key_at)[None, :]
    low, high = begin[:, None], own_at[:, None]

    half_dim = HD // 2
    frequency = rope_base ** (-(jnp.arange(half_dim, dtype=f32) * 2.0) / HD)
    angles = position.astype(f32)[:, None] * frequency[None, :]
    cosine, sine = jnp.cos(angles), jnp.sin(angles)
    cos_table = jnp.concatenate([cosine, cosine], axis=1)
    sin_table = jnp.concatenate([-sine, sine], axis=1)

    def rotate(values):
        count = values.shape[1] // HD
        shaped = values.reshape(rows, count, HD)
        turned = jnp.concatenate([shaped[..., half_dim:], shaped[..., :half_dim]], axis=-1)
        return (shaped * cos_table[:, None, :] + turned * sin_table[:, None, :]).reshape(
            values.shape
        )

    inputs = own_tokens.astype(f32)
    scale_one = rms_scale(inputs)
    normed = (inputs * scale_one * gain_one).astype(bf16)
    qkv = dot_plain(normed, qkv_w) + bias
    rotated = rotate(qkv[:, : q_width + kv_width]).astype(bf16)
    queries = rotated[:, :q_width]
    kv_own = jnp.concatenate([rotated[:, q_width:], qkv[:, q_width + kv_width :].astype(bf16)], axis=1)
    kv_all = jnp.concatenate(
        [kv_own] + [shift(kv_own, "context", step) for step in range(1, behind + 1)], axis=0
    )
    attended = attend(queries, kv_all, low, high, key_at)
    branch = dot_plain(attended, out_w)
    middle = (
        inputs[:half]
        + branch[:half]
        + swap(branch[half:].astype(bf16), "tensor", 1).astype(f32)
    )
    middle_scale = rms_scale(middle)
    normed_two = (middle * middle_scale * gain_two).astype(bf16)
    team_rows, remote_rows = gather_rows(normed_two)

    def feed(index, rows_in, grads_in):
        both = dot_plain(rows_in, up_gate_w[index])
        d_hidden = dot_cols(grads_in, down_w[index])
        shown = None
        overlap = max(fresh)
        if index == 0 and overlap:
            column = jnp.arange(part, dtype=jnp.int32)[None, :]
            limit = jnp.int32(0)
            for s in range(TEAM):
                limit = jnp.where(member == s, fresh[s], limit)
            shown = column >= limit
        hidden, d_gate, d_up = swiglu_grads(both[:, :part], both[:, part:], d_hidden, shown)
        return hidden, jnp.concatenate([d_gate, d_up], axis=1)

    team_out, remote_out = [], []
    d_rows, out_rows = 0.0, 0.0
    for index in range(PARTS):
        hidden, d_both = feed(index, team_rows, grad_team)
        team_out.append((hidden, d_both))
        d_rows = d_rows + dot_cols(d_both, up_gate_w[index])
        out_rows = out_rows + dot_plain(hidden, down_w[index])
    for index in range(PARTS):
        remote_out.append(feed(index, remote_rows, grad_remote))

    def give_back(partial):
        mid_rows = partial.shape[0] // 2
        mine = partial[:mid_rows] + swap(partial[mid_rows:].astype(bf16), "tensor", 1).astype(f32)
        return mine[:half] + swap(mine[half:].astype(bf16), "context", 1).astype(f32)

    d_normed_two = give_back(d_rows)
    branch_out = give_back(out_rows)

    all_rows = jnp.concatenate([team_rows, remote_rows], axis=0)
    all_grads = jnp.concatenate([grad_team, grad_remote], axis=0)
    both_parts, down_parts = [], []
    for index in range(PARTS):
        hidden = jnp.concatenate([team_out[index][0], remote_out[index][0]], axis=0)
        d_both = jnp.concatenate([team_out[index][1], remote_out[index][1]], axis=0)
        grad_both = dot_rows(all_rows, d_both).astype(bf16)
        grad_down = dot_rows(hidden, all_grads).astype(bf16)
        both_own = reduce_fsdp(grad_both, 0).astype(bf16)
        down_own = reduce_fsdp(grad_down, 1).astype(bf16)
        both_parts.append((both_own, swap(both_own, "context", 1)))
        down_parts.append((down_own, swap(down_own, "context", 1)))

    def assemble(parts, axis):
        own = jnp.concatenate([p[0] for p in parts], axis=axis)
        other = jnp.concatenate([p[1] for p in parts], axis=axis)
        pieces = []
        for s in range(TEAM):
            full = jnp.where(member == s, own, other)
            pieces.append(lax.slice_in_dim(full, fresh[s], full.shape[axis], axis=axis))
        return jnp.concatenate(pieces, axis=axis).astype(f32)

    grad_gate = assemble([(a[:, :part], b[:, :part]) for a, b in both_parts], 1)
    grad_up = assemble([(a[:, part:], b[:, part:]) for a, b in both_parts], 1)
    grad_down = assemble(down_parts, 0)

    grad_gain_two = jnp.sum(d_normed_two * middle * middle_scale, axis=0)
    weighted_two = d_normed_two * gain_two
    d_middle = (
        own_grad[:half].astype(f32)
        + middle_scale * weighted_two
        - middle * middle_scale**3 * jnp.mean(weighted_two * middle, axis=-1, keepdims=True)
    )
    d_branch_half = d_middle.astype(bf16)
    d_branch = jnp.concatenate([d_branch_half, swap(d_branch_half, "tensor", 1)], axis=0)
    d_attended = dot_cols(d_branch, out_w).astype(bf16)
    dq_low, dkv_all = attend_back(
        queries, d_attended, kv_all, low, high, key_at, cos_table, sin_table
    )
    dkv = dkv_all[:rows]
    for step in range(1, behind + 1):
        sent = dkv_all[step * rows : (step + 1) * rows].astype(bf16)
        dkv = dkv + shift(sent, "context", -step).astype(f32)
    dk = dkv[:, :HD]
    dk_turned = jnp.concatenate([dk[:, half_dim:], dk[:, :half_dim]], axis=1)
    dk = dk * cos_table - dk_turned * sin_table
    d_qkv = jnp.concatenate([dq_low, dk.astype(bf16), dkv[:, HD:].astype(bf16)], axis=1)
    d_normed_part = dot_cols(d_qkv, qkv_w)
    d_normed = d_normed_part[:half] + swap(
        d_normed_part[half:].astype(bf16), "tensor", 1
    ).astype(f32)
    grad_gain_one = jnp.sum(d_normed * inputs[:half] * scale_one[:half], axis=0)
    weighted_one = d_normed * gain_one
    d_inputs = (
        d_middle
        + scale_one[:half] * weighted_one
        - inputs[:half]
        * scale_one[:half] ** 3
        * jnp.mean(weighted_one * inputs[:half], axis=-1, keepdims=True)
    )

    grad_o = sum_context(reduce_fsdp(dot_rows(attended, d_branch).astype(bf16), 1))
    grad_qkv = sum_context(reduce_fsdp(dot_rows(normed, d_qkv).astype(bf16), 0))

    gains = jnp.stack([grad_gain_one, grad_gain_two])
    gains = gains + swap(gains, "tensor", 1)
    grad_bias = jnp.sum(d_qkv.astype(f32), axis=0).reshape(all_heads, n_fsdp, bias_cols)
    bias_rel = xor_blocks([grad_bias[:, i] for i in range(n_fsdp)], my_fsdp, n_fsdp)
    small = jnp.stack(
        [
            jnp.concatenate(
                [gains[:, place * shard : (place + 1) * shard].reshape(-1), bias_rel[i].reshape(-1)]
            )
            for place, i in enumerate(order)
        ]
    )
    for bit in bits_of(n_fsdp):
        kept = small.shape[0] // 2
        small = small[:kept] + swap(small[kept:], "fsdp", bit)
    for bit in bits_of(n_ctx):
        small = small + swap(small, "context", bit)
    small = small[0]
    grad_biases = small[2 * shard :].reshape(all_heads, bias_cols)

    def restore(mine):
        low_half = mine.astype(bf16)
        both = mine_first(jnp.concatenate([low_half, swap(low_half, "tensor", 1)], axis=0))
        return from_relative(both, my_fsdp, n_fsdp).astype(f32)

    return (
        restore(middle + branch_out),
        restore(d_inputs),
        small[:shard],
        grad_qkv[:, :q_width],
        grad_biases[:heads_local],
        grad_qkv[:, q_width : q_width + kv_width],
        grad_biases[heads_local : heads_local + 1],
        grad_qkv[:, q_width + kv_width :],
        grad_biases[heads_local + 1 :],
        grad_o,
        small[shard : 2 * shard],
        grad_gate,
        grad_up,
        grad_down,
    )


def solution(mesh):
    in_specs = (
        P(("fsdp", "context"), None),
        P(("fsdp", "context"), None),
        P("fsdp", None),
        P("fsdp", None, None),
        P("fsdp"),
        P("fsdp", "tensor"),
        P("tensor", "fsdp"),
        P("fsdp", "tensor"),
        P("tensor", "fsdp"),
        P("fsdp", "tensor"),
        P("tensor", "fsdp"),
        P("tensor", "fsdp"),
        P("fsdp"),
        P("fsdp", "tensor"),
        P("fsdp", "tensor"),
        P("tensor", "fsdp"),
    )
    out_specs = (
        P(("fsdp", "context"), None),
        P(("fsdp", "context"), None),
        P("fsdp"),
        P("fsdp", "tensor"),
        P("tensor", "fsdp"),
        P("fsdp", "tensor"),
        P("tensor", "fsdp"),
        P("fsdp", "tensor"),
        P("tensor", "fsdp"),
        P("tensor", "fsdp"),
        P("fsdp"),
        P("fsdp", "tensor"),
        P("fsdp", "tensor"),
        P("tensor", "fsdp"),
    )
    return jax.shard_map(
        per_device, mesh=mesh, in_specs=in_specs, out_specs=out_specs, check_vma=False
    )
```

```python
import functools

import jax
import jax.numpy as jnp
from jax import lax
from jax.experimental import pallas as pl
from jax.experimental.pallas import tpu as pltpu
from jax.sharding import PartitionSpec as P

D = 1536
HD = 128
LANES = 128
TEAM = 2
PARTS = 3
WIDE = 256
SHARED_PARTS = 1

epsilon = 1e-06
rope_base = 10000.0
neg_big = -1e30
far_away = 1 << 29
bf16 = jnp.bfloat16
f32 = jnp.float32


def dot_plain(left_op, right_op):
    return jnp.dot(left_op, right_op, preferred_element_type=f32)


def dot_rows(left_op, right_op):
    return lax.dot_general(
        left_op, right_op, (((0,), (0,)), ((), ())), preferred_element_type=f32
    )


def dot_cols(left_op, right_op):
    return lax.dot_general(
        left_op, right_op, (((1,), (1,)), ((), ())), preferred_element_type=f32
    )


def swap(values, axis_name, bit):
    size = lax.axis_size(axis_name)
    return lax.ppermute(values, axis_name, [(i, i ^ bit) for i in range(size)])


def shift(values, axis_name, step):
    size = lax.axis_size(axis_name)
    pairs = [(i, i + step) for i in range(size) if 0 <= i + step < size]
    return lax.ppermute(values, axis_name, pairs)


def bits_of(size):
    found = []
    bit = 1
    while bit < size:
        found.append(bit)
        bit *= 2
    return found


def fsdp_order(size):
    order = [0]
    for bit in reversed(bits_of(size)):
        order = order + [held ^ bit for held in order]
    return order


def gather_pieces(piece):
    pieces = [piece]
    for bit in reversed(bits_of(lax.axis_size("fsdp"))):
        pieces = pieces + [swap(held, "fsdp", bit) for held in pieces]
    return pieces


def xor_blocks(blocks, index, size):
    for bit in bits_of(size):
        on = (index & bit) != 0
        blocks = [jnp.where(on, blocks[i ^ bit], blocks[i]) for i in range(size)]
    return blocks


def to_relative(values, index, size):
    width = values.shape[-1] // size
    blocks = [values[..., i * width : (i + 1) * width] for i in range(size)]
    blocks = xor_blocks(blocks, index, size)
    return jnp.concatenate([blocks[i] for i in fsdp_order(size)], axis=-1)


def from_relative(values, index, size):
    width = values.shape[-1] // size
    order = fsdp_order(size)
    blocks = [None] * size
    for place, i in enumerate(order):
        blocks[i] = values[..., place * width : (place + 1) * width]
    return jnp.concatenate(xor_blocks(blocks, index, size), axis=-1)


def reduce_fsdp(values, axis):
    for bit in bits_of(lax.axis_size("fsdp")):
        half = values.shape[axis] // 2
        kept = lax.slice_in_dim(values, 0, half, axis=axis)
        sent = lax.slice_in_dim(values, half, 2 * half, axis=axis).astype(bf16)
        values = kept.astype(f32) + swap(sent, "fsdp", bit).astype(f32)
    return values


def sum_context(values):
    index = lax.axis_index("context")
    bits = bits_of(lax.axis_size("context"))
    for bit in bits:
        half = values.shape[0] // 2
        on = (index & bit) != 0
        kept = jnp.where(on, values[half:], values[:half])
        sent = jnp.where(on, values[:half], values[half:]).astype(bf16)
        values = kept + swap(sent, "context", bit).astype(f32)
    values = values.astype(bf16)
    for bit in reversed(bits):
        on = (index & bit) != 0
        other = swap(values, "context", bit)
        values = jnp.concatenate(
            [jnp.where(on, other, values), jnp.where(on, values, other)], axis=0
        )
    return values.astype(f32)


def whole(array):
    return pl.BlockSpec(array.shape, lambda *ids: (0,) * array.ndim)


def wide_enough(pieces, axis):
    if pieces[0].shape[axis] % LANES:
        return [jnp.concatenate(pieces, axis=axis)]
    return pieces


def cost(us=1):
    return pl.CostEstimate(
        flops=int(us * 0.55e9), bytes_accessed=int(us * 1.8e6), transcendentals=0
    )


def joined(refs, index_ref, axis, cut=None):
    blocks = [r[...] if cut is None else r[cut] for r in refs]
    if len(blocks) > 1:
        order = fsdp_order(len(blocks))
        blocks = [blocks[order.index(i)] for i in range(len(blocks))]
        blocks = xor_blocks(blocks, index_ref[0], len(blocks))
    return jnp.concatenate(blocks, axis=axis)


def params(mib):
    return pltpu.CompilerParams(vmem_limit_bytes=mib << 20)


def pack_body(count, start_ref, *refs):
    out_ref = refs[-1]
    for i in range(count):
        at = slice(i * LANES, (i + 1) * LANES)
        out_ref[0, :, at] = refs[i][...].astype(bf16)
        out_ref[1, :, at] = refs[count + i][...].astype(bf16)
        out_ref[2, :, at] = refs[2 * count + i][...].T.astype(bf16)


def pack(w_gate, w_up, w_down, start, width):
    shard = w_gate.shape[0]
    count = width // LANES
    columns = [pl.BlockSpec((shard, LANES), lambda j, s, i=i: (0, s[0] + i)) for i in range(count)]
    lines = [pl.BlockSpec((LANES, shard), lambda j, s, i=i: (s[0] + i, 0)) for i in range(count)]
    spec = pltpu.PrefetchScalarGridSpec(
        num_scalar_prefetch=1,
        grid=(1,),
        in_specs=columns + columns + lines,
        out_specs=pl.BlockSpec((3, shard, width), lambda j, s: (0, 0, 0)),
    )
    return pl.pallas_call(
        functools.partial(pack_body, count),
        out_shape=jax.ShapeDtypeStruct((3, shard, width), bf16),
        grid_spec=spec,
        cost_estimate=cost(),
        compiler_params=params(60),
    )(start, *[w_gate] * count, *[w_up] * count, *[w_down] * count)


def vectors_body(count, heads, index_ref, *refs):
    gain_ref, bias_ref = refs[count:]
    width = D // count
    gain_ref[...] = joined(refs[:count], index_ref, 1, (slice(0, 2), slice(0, width)))
    bias_ref[...] = sum(r[8 : 8 + heads, :HD].astype(f32) for r in refs[:count])


def vectors(index, pieces, heads):
    shard = D // len(pieces)
    if shard % LANES:
        order = fsdp_order(len(pieces))
        blocks = [pieces[order.index(i)][shard : shard + 2, :shard] for i in range(len(pieces))]
        gains = jnp.concatenate(xor_blocks(blocks, index[0], len(pieces)), axis=1)
        return gains, sum(p[shard + 8 : shard + 8 + heads, :HD].astype(f32) for p in pieces)
    rows = pl.BlockSpec((16, pieces[0].shape[1]), lambda i: (shard // 16, 0))
    outs = (jax.ShapeDtypeStruct((2, D), bf16), jax.ShapeDtypeStruct((heads, HD), f32))
    return pl.pallas_call(
        functools.partial(vectors_body, len(pieces), heads),
        out_shape=outs,
        grid=(1,),
        in_specs=[pl.BlockSpec(memory_space=pltpu.SMEM)] + [rows] * len(pieces),
        out_specs=tuple(whole(a) for a in outs),
        cost_estimate=cost(),
        compiler_params=params(60),
    )(index, *pieces)


def project_body(count, q_width, index_ref, a_ref, b_ref, gain_ref, bias_ref, cos_ref, sin_ref, *refs):
    w_refs, (q_ref, kv_ref, h_ref) = refs[:count], refs[count:]
    x = jnp.concatenate([a_ref[...], b_ref[...]], axis=0).astype(f32)
    scale = lax.rsqrt(jnp.mean(x * x, axis=-1, keepdims=True) + epsilon)
    normed = (x * scale * gain_ref[0:1].astype(f32)).astype(bf16)
    h_ref[...] = normed
    total = w_refs[0].shape[1]
    depth = D // count
    for at in range(0, total, WIDE):
        weights = joined(w_refs, index_ref, 0, (slice(0, depth), slice(at, at + WIDE)))
        both = dot_plain(normed, weights)
        for inner in range(0, WIDE, HD):
            place = at + inner
            head = place // HD
            values = both[:, inner : inner + HD] + bias_ref[head : head + 1]
            if place < total - HD:
                turned = pltpu.roll(values, HD // 2, 1)
                values = values * cos_ref[...] + turned * sin_ref[...]
            if place < q_width:
                q_ref[:, place : place + HD] = values.astype(bf16)
            else:
                kv_ref[:, place - q_width : place - q_width + HD] = values.astype(bf16)


def project(index, first, second, gain, bias, cos_table, sin_table, weights, q_width):
    rows = 2 * first.shape[0]
    total = weights[0].shape[1]
    return pl.pallas_call(
        functools.partial(project_body, len(weights), q_width),
        out_shape=(
            jax.ShapeDtypeStruct((rows, q_width), bf16),
            jax.ShapeDtypeStruct((rows, total - q_width), bf16),
            jax.ShapeDtypeStruct((rows, D), bf16),
        ),
        in_specs=[pl.BlockSpec(memory_space=pltpu.SMEM)] + [pl.BlockSpec(memory_space=pltpu.VMEM)] * (6 + len(weights)),
        cost_estimate=cost(4),
        compiler_params=params(60),
    )(index, first, second, gain, bias, cos_table, sin_table, *weights)


def masked_weights(queries, keys, low_ref, high_ref, key_ref):
    scores = dot_cols(queries, keys) * HD ** (-0.5)
    key_at = key_ref[...]
    allowed = (key_at >= low_ref[...]) & (key_at <= high_ref[...])
    scores = jnp.where(allowed, scores, neg_big)
    top = jnp.max(scores, axis=-1, keepdims=True)
    raised = jnp.exp(scores - top)
    return raised * (1.0 / jnp.sum(raised, axis=-1, keepdims=True))


def attend_body(count, ahead, index_ref, q_ref, low_ref, high_ref, key_ref, *refs):
    w_refs, kv_refs = refs[:count], refs[count : count + ahead]
    o_ref, mine_ref, other_ref = refs[count + ahead :]
    keys = jnp.concatenate([kv[:, :HD] for kv in kv_refs], axis=0)
    values = jnp.concatenate([kv[:, HD:] for kv in kv_refs], axis=0)
    weights = masked_weights(q_ref[...], keys, low_ref, high_ref, key_ref)
    head = pl.program_id(0)
    out = dot_plain(weights.astype(bf16), values).astype(bf16)
    o_ref[:, pl.ds(pl.multiple_of(head * HD, HD), HD)] = out

    @pl.when(head == pl.num_programs(0) - 1)
    def _():
        half = mine_ref.shape[0]
        out_w = joined(w_refs, index_ref, 1)
        branch = dot_plain(o_ref[...], out_w)
        mine_ref[...] = branch[:half]
        other_ref[...] = branch[half:].astype(bf16)


def attend(index, queries, low, high, key_at, weights, kv_parts):
    rows, width = queries.shape
    head = pl.BlockSpec((rows, HD), lambda h: (0, h))
    keys = key_at.shape[1]
    rest = (low, high, key_at, *weights, *kv_parts)
    outs = (
        jax.ShapeDtypeStruct(queries.shape, bf16),
        jax.ShapeDtypeStruct((rows // 2, D), f32),
        jax.ShapeDtypeStruct((rows // 2, D), bf16),
    )
    return pl.pallas_call(
        functools.partial(attend_body, len(weights), len(kv_parts)),
        out_shape=outs,
        grid=(width // HD,),
        in_specs=[pl.BlockSpec(memory_space=pltpu.SMEM), head] + [whole(a) for a in rest],
        out_specs=tuple(whole(a) for a in outs),
        compiler_params=params(60),
        cost_estimate=cost(8),
    )(index, queries, *rest)


def middle_body(x_ref, mine_ref, other_ref, gain_ref, mid_ref, h_ref):
    middle = x_ref[...].astype(f32) + mine_ref[...] + other_ref[...].astype(f32)
    scale = lax.rsqrt(jnp.mean(middle * middle, axis=-1, keepdims=True) + epsilon)
    mid_ref[...] = middle
    h_ref[...] = (middle * scale * gain_ref[1:2].astype(f32)).astype(bf16)


def middle_norm(x, mine, other, gain):
    return pl.pallas_call(
        middle_body,
        out_shape=(jax.ShapeDtypeStruct(mine.shape, f32), jax.ShapeDtypeStruct(mine.shape, bf16)),
        cost_estimate=cost(),
        compiler_params=params(60),
    )(x, mine, other, gain)


def feed_body(count, base, back, carried, last, filled, at_row, limit_ref, ctx_ref, *refs):
    (h_own, h_across, g_own, g_across, w_ref), refs = refs[:5], refs[5:]
    carry, refs = refs[: 2 * carried], refs[2 * carried + filled :]
    outs, (act_ref, sem) = refs[:-2], refs[-2:]
    gate_w, up_w, down_w = (
        jnp.concatenate([w_ref[i, k] for i in range(count)], axis=0) for k in range(3)
    )
    rows = act_ref.shape[1]
    lane = lax.broadcasted_iota(jnp.int32, (1, act_ref.shape[2]), 1)
    shown = lane >= limit_ref[0]
    half = g_own.shape[1]
    chunk = 2 * half
    at = 0
    for h_ref, g_ref in ((h_own, g_own), (h_across, g_across)):
        for j in range(h_ref.shape[0] // chunk):
            rows_in = h_ref[j * chunk : (j + 1) * chunk]
            grads_in = jnp.concatenate(
                [g_ref[ctx_ref[0] ^ (base + 2 * j + k)] for k in range(2)], axis=0
            )
            gate = dot_plain(rows_in, gate_w)
            up = dot_plain(rows_in, up_w)
            d_hidden = dot_plain(grads_in, down_w)
            gate_sig = jax.nn.sigmoid(gate)
            activated = gate * gate_sig
            hidden = activated * up
            d_gate = d_hidden * up * gate_sig * (1.0 + gate * (1.0 - gate_sig))
            d_up = d_hidden * activated
            act_ref[0, at : at + chunk] = jnp.where(shown, d_gate, 0.0).astype(bf16)
            act_ref[1, at : at + chunk] = jnp.where(shown, d_up, 0.0).astype(bf16)
            act_ref[2, at : at + chunk] = jnp.where(shown, hidden, 0.0).astype(bf16)
            at += chunk
    copy = pltpu.make_async_copy(act_ref, outs[0].at[:, pl.ds(at_row, rows), :], sem)
    copy.start()
    if back:
        d_rows = dot_cols(act_ref[0], gate_w) + dot_cols(act_ref[1], up_w)
        out_rows = dot_cols(act_ref[2], down_w)
        if carried:
            d_rows = d_rows + carry[0][...]
            out_rows = out_rows + carry[1][...]
        if last:
            cuts = [(i * half, (i + 1) * half) for i in range(4)]
            for ref, (low, high) in zip(outs[1:5], cuts):
                ref[...] = d_rows[low:high].astype(ref.dtype)
            cuts = cuts[:2] + [(2 * half, 4 * half)]
            for ref, (low, high) in zip(outs[5:], cuts):
                ref[...] = out_rows[low:high].astype(ref.dtype)
        else:
            outs[1][...] = d_rows
            outs[2][...] = out_rows
    copy.wait()


def feed(limit, ctx, rows_in, grads_in, weights, total, back, carry=(), last=False, act=None):
    some = sum(r.shape[0] for r in rows_in)
    width = weights.shape[3]
    outs = [jax.ShapeDtypeStruct((3, total, width), bf16)]
    half = grads_in[0].shape[1]
    if back and last:
        outs += [jax.ShapeDtypeStruct((half, D), f32)] * 2
        outs += [jax.ShapeDtypeStruct((half, D), bf16)] * 2
        outs += [jax.ShapeDtypeStruct((half, D), f32)] * 2
        outs += [jax.ShapeDtypeStruct((2 * half, D), bf16)]
    elif back:
        outs += [jax.ShapeDtypeStruct((some, D), f32)] * 2
    vmem = pl.BlockSpec(memory_space=pltpu.VMEM)
    smem = pl.BlockSpec(memory_space=pltpu.SMEM)
    hbm = pl.BlockSpec(memory_space=pl.ANY)
    inputs = (*rows_in, *grads_in, weights, *carry)
    filled = () if act is None else (act,)
    return pl.pallas_call(
        functools.partial(
            feed_body, weights.shape[0], 0 if back else TEAM, back, len(carry) // 2, last,
            len(filled), 0 if back else total - some,
        ),
        out_shape=tuple(outs),
        in_specs=[smem, smem] + [vmem] * len(inputs) + [hbm] * len(filled),
        out_specs=tuple([hbm] + [vmem] * (len(outs) - 1)),
        scratch_shapes=[pltpu.VMEM((3, some, width), bf16), pltpu.SemaphoreType.DMA],
        input_output_aliases={2 + len(inputs): 0} if filled else {},
        compiler_params=params(60),
        cost_estimate=cost((6 if back else 0) + 9 * some / 512),
    )(limit, ctx, *inputs, *filled)


def turn_body(contexts, blocks, index_ref, ctx_ref, *refs):
    lines, (g_own, g_across, kept_ref, sent_ref) = refs[:-4], refs[-4:]
    width = D // blocks
    order = fsdp_order(blocks)
    half = g_own.shape[1]

    def put(which, at, value):
        here = slice(at, at + value.shape[0])
        parts = [value[:, i * width : (i + 1) * width] for i in range(blocks)]
        if blocks > 2:
            parts = xor_blocks(parts, index_ref[0], blocks)
            parts = [parts[i] for i in order]
        for spot in range(blocks // 2):
            lines_at = slice(spot * width, (spot + 1) * width)
            kept_ref[which, lines_at, here] = parts[spot].T
            sent_ref[which, lines_at, here] = parts[blocks // 2 + spot].T

    at = 0
    for ref in lines:
        put(0, at, ref[...])
        at += ref.shape[0]
    at = 0
    for group in (range(TEAM), range(TEAM, contexts)):
        for ref in (g_own, g_across):
            for k in group:
                put(1, at, ref[ctx_ref[0] ^ k])
                at += half


def turn_rows(index, ctx, rows, grads, n_fsdp):
    total = sum(r.shape[0] for r in rows)
    blocks = n_fsdp
    if D // n_fsdp % LANES:
        blocks = 2
        rows, grads = (
            [to_relative(v, index[0], n_fsdp) for v in some] for some in (rows, grads)
        )
    smem = pl.BlockSpec(memory_space=pltpu.SMEM)
    return pl.pallas_call(
        functools.partial(turn_body, grads[0].shape[0], blocks),
        out_shape=(jax.ShapeDtypeStruct((2, D // 2, total), bf16),) * 2,
        in_specs=[smem, smem] + [pl.BlockSpec(memory_space=pltpu.VMEM)] * (len(rows) + 2),
        cost_estimate=cost(7),
        compiler_params=params(60),
    )(index, ctx, *rows, *grads)


def weight_body(own_ref, beside_ref, act_ref, act_beside_ref, near_ref, far_ref):
    cut = near_ref.shape[1]
    value = dot_plain(own_ref[0], act_ref[0]) + dot_plain(beside_ref[0], act_beside_ref[0])
    near_ref[0] = value[:cut].astype(bf16)
    far_ref[0] = value[cut:].astype(bf16)


def weight_grads(own, beside, act, act_beside):
    total, width = act.shape[1:]
    cut = D // 4
    left = pl.BlockSpec((1, D // 2, total), lambda k: (k // 2, 0, 0))
    right = pl.BlockSpec((1, total, width), lambda k: (k, 0, 0))
    out = pl.BlockSpec((1, cut, width), lambda k: (k, 0, 0))
    return pl.pallas_call(
        weight_body,
        out_shape=(jax.ShapeDtypeStruct((3, cut, width), bf16),) * 2,
        grid=(3,),
        in_specs=[left, left, right, right],
        out_specs=(out, out),
        compiler_params=params(60),
        cost_estimate=cost(12),
    )(own, beside, act, act_beside)


def middle_back_body(
    near_ref, across_ref, far_ref, mid_ref, gain_ref, g_ref, d_ref, low_ref, gain_out
):
    d_normed = near_ref[...] + across_ref[...].astype(f32) + far_ref[...].astype(f32)
    middle = mid_ref[...]
    scale = lax.rsqrt(jnp.mean(middle * middle, axis=-1, keepdims=True) + epsilon)
    gain_out[...] = jnp.sum(d_normed * middle * scale, axis=0, keepdims=True)
    weighted = d_normed * gain_ref[1:2].astype(f32)
    inner = jnp.mean(weighted * middle, axis=-1, keepdims=True)
    d_middle = g_ref[...].astype(f32) + scale * weighted - middle * scale**3 * inner
    d_ref[...] = d_middle
    low_ref[...] = d_middle.astype(bf16)


def middle_back(near, across, far, middle, gain, grads):
    return pl.pallas_call(
        middle_back_body,
        out_shape=(
            jax.ShapeDtypeStruct(near.shape, f32),
            jax.ShapeDtypeStruct(near.shape, bf16),
            jax.ShapeDtypeStruct((1, D), f32),
        ),
        cost_estimate=cost(),
        compiler_params=params(60),
    )(near, across, far, middle, gain, grads)


def attend_back_body(count, ahead, index_ref, q_ref, low_ref, high_ref, key_ref, cos_ref, sin_ref, *refs):
    scale = HD ** (-0.5)
    mine_ref, other_ref = refs[:2]
    w_refs, kv_refs = refs[2 : 2 + count], refs[2 + count : 2 + count + ahead]
    outs = refs[2 + count + ahead :]
    dq_ref, dkv_refs, (d_o, sums) = outs[0], outs[1 : 1 + ahead], outs[1 + ahead :]
    head = pl.program_id(0)

    @pl.when(head == 0)
    def _():
        d_branch = jnp.concatenate([mine_ref[...], other_ref[...]], axis=0)
        out_w = joined(w_refs, index_ref, 1)
        d_o[...] = dot_cols(d_branch, out_w).astype(bf16)
        sums[...] = jnp.zeros_like(sums)

    queries = q_ref[...]
    grad = d_o[:, pl.ds(pl.multiple_of(head * HD, HD), HD)]
    keys = jnp.concatenate([kv[:, :HD] for kv in kv_refs], axis=0)
    values = jnp.concatenate([kv[:, HD:] for kv in kv_refs], axis=0)
    weights = masked_weights(queries, keys, low_ref, high_ref, key_ref)
    dweights = dot_cols(grad, values)
    delta = jnp.sum(weights * dweights, axis=-1, keepdims=True)
    dscores = (weights * (dweights - delta)).astype(bf16)
    dq_rot = dot_plain(dscores, keys) * scale
    turned = pltpu.roll(dq_rot, HD // 2, 1)
    dq_ref[...] = (dq_rot * cos_ref[...] - turned * sin_ref[...]).astype(bf16)
    sums[:, :HD] += dot_rows(dscores, queries) * scale
    sums[:, HD:] += dot_rows(weights.astype(bf16), grad)

    @pl.when(head == pl.num_programs(0) - 1)
    def _():
        rows = q_ref.shape[0]
        for i, out in enumerate(dkv_refs):
            out[...] = sums[i * rows : (i + 1) * rows].astype(out.dtype)


def attend_back(index, queries, low, high, key_at, cos_table, sin_table, grads, weights, kv_parts):
    rows, width = queries.shape
    head = pl.BlockSpec((rows, HD), lambda h: (0, h))
    keys = key_at.shape[1]
    rest = (low, high, key_at, cos_table, sin_table, *grads, *weights, *kv_parts)
    outs = [jax.ShapeDtypeStruct(queries.shape, bf16)]
    outs += [
        jax.ShapeDtypeStruct(kv.shape, bf16 if i else f32) for i, kv in enumerate(kv_parts)
    ]
    return pl.pallas_call(
        functools.partial(attend_back_body, len(weights), len(kv_parts)),
        out_shape=tuple(outs),
        grid=(width // HD,),
        in_specs=[pl.BlockSpec(memory_space=pltpu.SMEM), head] + [whole(a) for a in rest],
        out_specs=tuple([head] + [whole(a) for a in outs[1:]]),
        scratch_shapes=[pltpu.VMEM((rows, width), bf16), pltpu.VMEM((keys, 2 * HD), f32)],
        compiler_params=params(60),
        cost_estimate=cost(10),
    )(index, queries, *rest)


def project_back_body(count, ahead, index_ref, dq_ref, cos_ref, sin_ref, *refs):
    w_refs, dkv_refs = refs[:count], refs[count : count + ahead]
    d_ref, mine_ref, other_ref, bias_ref = refs[count + ahead :]
    total = dkv_refs[0][...]
    for extra in dkv_refs[1:]:
        total = total + extra[...].astype(f32)
    dk = total[:, :HD]
    dk = dk * cos_ref[...] - pltpu.roll(dk, HD // 2, 1) * sin_ref[...]
    d_low = jnp.concatenate([dq_ref[...], dk.astype(bf16), total[:, HD:].astype(bf16)], axis=1)
    d_ref[...] = d_low
    bias_ref[...] = jnp.sum(d_low.astype(f32), axis=0, keepdims=True)
    weights = joined(w_refs, index_ref, 0, slice(0, D // count))
    d_normed = dot_cols(d_low, weights)
    half = mine_ref.shape[0]
    mine_ref[...] = d_normed[:half]
    other_ref[...] = d_normed[half:].astype(bf16)


def project_back(index, dq, cos_table, sin_table, weights, dkv_parts):
    rows = dq.shape[0]
    total = weights[0].shape[1]
    return pl.pallas_call(
        functools.partial(project_back_body, len(weights), len(dkv_parts)),
        out_shape=(
            jax.ShapeDtypeStruct((rows, total), bf16),
            jax.ShapeDtypeStruct((rows // 2, D), f32),
            jax.ShapeDtypeStruct((rows // 2, D), bf16),
            jax.ShapeDtypeStruct((1, total), f32),
        ),
        in_specs=[pl.BlockSpec(memory_space=pltpu.SMEM)] + [pl.BlockSpec(memory_space=pltpu.VMEM)] * (3 + len(weights) + len(dkv_parts)),
        cost_estimate=cost(4),
        compiler_params=params(60),
    )(index, dq, cos_table, sin_table, *weights, *dkv_parts)


def input_back_body(mine_ref, other_ref, x_ref, gain_ref, mid_ref, d_ref, gain_out):
    d_normed = mine_ref[...] + other_ref[...].astype(f32)
    x = x_ref[...].astype(f32)
    scale = lax.rsqrt(jnp.mean(x * x, axis=-1, keepdims=True) + epsilon)
    gain_out[...] = jnp.sum(d_normed * x * scale, axis=0, keepdims=True)
    weighted = d_normed * gain_ref[0:1].astype(f32)
    inner = jnp.mean(weighted * x, axis=-1, keepdims=True)
    d_ref[...] = (mid_ref[...] + scale * weighted - x * scale**3 * inner).astype(bf16)


def input_back(mine, other, x, gain, d_middle):
    return pl.pallas_call(
        input_back_body,
        out_shape=(jax.ShapeDtypeStruct(mine.shape, bf16), jax.ShapeDtypeStruct((1, D), f32)),
        cost_estimate=cost(),
        compiler_params=params(60),
    )(mine, other, x, gain, d_middle)


def place_body(plan, carried, member_ref, *refs):
    own_ref, other_ref, refs = refs[0], refs[1], refs[2:]
    outs = refs[carried : carried + 3]
    wide_buf, tall_buf, sems = refs[carried + 3 :]
    width = own_ref.shape[2]

    def copies(team):
        skip, at = plan[team]
        size = width - skip
        for k in range(2):
            yield pltpu.make_async_copy(
                wide_buf.at[team, k, :, pl.ds(skip, size)],
                outs[k].at[:, pl.ds(at + skip, size)],
                sems.at[team, k],
            )
        yield pltpu.make_async_copy(
            tall_buf.at[team, pl.ds(skip, size)],
            outs[2].at[pl.ds(at + skip, size)],
            sems.at[team, 2],
        )

    for team in range(len(plan)):
        def put(ref, team=team):
            wide_buf[team, 0] = ref[0].astype(f32)
            wide_buf[team, 1] = ref[1].astype(f32)
            tall_buf[team] = ref[2].astype(f32).T

        @pl.when(member_ref[0] == team)
        def _():
            put(own_ref)

        @pl.when(member_ref[0] != team)
        def _():
            put(other_ref)

        for copy in copies(team):
            copy.start()
    for team in range(len(plan)):
        for copy in copies(team):
            copy.wait()


def place(member, own, other, index, starts, fresh, ff_local, carry):
    shard, width = own.shape[1:]
    plan = tuple(
        (min(max(fresh[s] - index * width, 0), width), starts[s] + index * width)
        for s in range(TEAM)
    )
    hbm = pl.BlockSpec(memory_space=pl.ANY)
    vmem = pl.BlockSpec(memory_space=pltpu.VMEM)
    return pl.pallas_call(
        functools.partial(place_body, plan, len(carry)),
        out_shape=(
            jax.ShapeDtypeStruct((shard, ff_local), f32),
            jax.ShapeDtypeStruct((shard, ff_local), f32),
            jax.ShapeDtypeStruct((ff_local, shard), f32),
        ),
        in_specs=[pl.BlockSpec(memory_space=pltpu.SMEM)] + [vmem] * 2 + [hbm] * len(carry),
        out_specs=(hbm, hbm, hbm),
        scratch_shapes=[
            pltpu.VMEM((TEAM, 2, shard, width), f32),
            pltpu.VMEM((TEAM, width, shard), f32),
            pltpu.SemaphoreType.DMA((TEAM, 3)),
        ],
        input_output_aliases={3 + i: i for i in range(len(carry))},
        cost_estimate=cost(),
        compiler_params=params(60),
    )(member, own, other, *carry)


def after(values, *first):
    return lax.optimization_barrier((values, first))[0]


class Order:
    def __init__(self):
        self.last = ()

    def __call__(self, step, *args):
        args, _ = lax.optimization_barrier((args, self.last))
        result = step(*args)
        self.last = (jax.tree.leaves(result)[0],)
        return result

    def pin(self, values):
        values, _ = lax.optimization_barrier((values, self.last))
        self.last = (jax.tree.leaves(values)[0],)
        return values


def stack(*pieces):
    return jnp.concatenate(pieces, axis=0)


class Pieces:
    def __init__(self, run, full, *first):
        bits = list(reversed(bits_of(lax.axis_size("fsdp"))))
        self.run, self.near = run, bits[-1]
        self.held = [full]
        gate = after(full, *first)
        for bit in bits[:-1]:
            self.held = self.held + [swap(p, "fsdp", bit) for p in [gate] + self.held[1:]]

    def turn(self):
        self.held = self.held[:1] + list(self.run.pin(tuple(self.held[1:])))
        self.sent = swap(self.run(lambda *a: jnp.stack(a), *self.held), "fsdp", self.near)
        return self.held[-1]

    def finish(self):
        self.sent = self.run.pin(self.sent)

    def pieces(self):
        return self.held + [self.sent[i] for i in range(len(self.held))]


def per_device(
    tokens,
    cotangent,
    lengths,
    span_order,
    attn_gain,
    w_q,
    b_q,
    w_k,
    b_k,
    w_v,
    b_v,
    w_o,
    mlp_gain,
    w_gate,
    w_up,
    w_down,
):
    n_fsdp = lax.axis_size("fsdp")
    n_ctx = lax.axis_size("context")
    my_fsdp = lax.axis_index("fsdp")
    my_ctx = lax.axis_index("context")
    my_tensor = lax.axis_index("tensor")
    member = my_ctx % TEAM
    rows = tokens.shape[0]
    half = rows // 2
    piece_rows = rows // n_ctx
    shard = D // n_fsdp
    q_width = w_q.shape[1]
    kv_width = w_k.shape[1]
    qkv_width = q_width + 2 * kv_width
    heads_local = q_width // HD
    all_heads = qkv_width // HD
    flipped = my_tensor != 0
    run = Order()
    sharing = n_fsdp == 4 and n_ctx % 2 == 0

    def mine_first(values):
        first, second = values[:half], values[half:]
        return stack(jnp.where(flipped, second, first), jnp.where(flipped, first, second))

    bias_cols = HD // n_fsdp

    def qkv_pack(g1, g2, b_q, b_k, b_v, *w):
        biases = jnp.concatenate([b_q, b_k, b_v], axis=0).astype(bf16)
        spread = jnp.concatenate([biases] * n_fsdp, axis=1)
        lane = jnp.arange(HD, dtype=jnp.int32)[None, :] // bias_cols
        spread = jnp.where(lane == my_fsdp, spread, jnp.zeros_like(spread))
        gains = jnp.pad(jnp.stack([g1, g2]).astype(bf16), ((0, 6), (0, qkv_width - shard)))
        spread = jnp.pad(spread, ((0, 8 - all_heads), (0, qkv_width - HD)))
        return stack(jnp.concatenate(w, axis=1).astype(bf16), gains, spread)

    qkv_h = Pieces(run, run(qkv_pack, attn_gain, mlp_gain, b_q, b_k, b_v, w_q, w_k, w_v))
    out_cast = run(lambda w: w.astype(bf16), w_o)

    def arrange(values):
        both = mine_first(values)
        return both[:half], both[half:]

    pair = n_ctx == 4

    class Rows:
        def __init__(self, mine):
            self.mine = mine
            self.beside = swap(mine, "context", 1)

        def early(self):
            if pair:
                self.remote_mine = swap(self.mine, "context", 2)

        def turn(self):
            self.beside = run.pin(self.beside)

        def across_team(self):
            self.held = run(stack, self.mine, self.beside)
            self.held_across = swap(self.held, "tensor", 1)

        def pin_early(self):
            if pair:
                self.remote_mine = run.pin(self.remote_mine)

        def late(self):
            if pair:
                self.remote_beside = swap(self.beside, "context", 2)
                return
            held, others = self.held, []
            for bit in bits_of(n_ctx)[1:]:
                there = swap(held, "context", bit)
                others.append(there)
                held = stack(held, there)
            self.remote = stack(*others)

        def across_rest(self):
            if pair:
                self.remote = run(stack, self.remote_mine, self.remote_beside)
            self.remote_across = swap(self.remote, "tensor", 1)

        def pin_team(self):
            self.held_across = run.pin(self.held_across)

        def pin_rest(self):
            self.remote_across = run.pin(self.remote_across)

        def team(self):
            return (self.held, self.held_across)

        def rest(self):
            return (self.remote, self.remote_across)

    grad_mine, _ = run(arrange, cotangent)
    grads_own = run(lambda v: jnp.broadcast_to(v[None], (n_ctx,) + v.shape), grad_mine)
    grads_own = lax.all_to_all(grads_own, "context", split_axis=0, concat_axis=0)

    ff_local = w_gate.shape[1]
    tiles = ff_local // LANES
    unit = PARTS * WIDE // LANES
    slice_tiles = -(-tiles // (TEAM * unit)) * unit
    part = slice_tiles // PARTS * LANES
    starts = [min(s * slice_tiles, tiles - slice_tiles) * LANES for s in range(TEAM)]
    fresh = [s * slice_tiles * LANES - starts[s] for s in range(TEAM)]
    my_start = jnp.int32(starts[0] // LANES)
    limit = jnp.int32(fresh[0])
    for s in range(1, TEAM):
        my_start = jnp.where(member == s, starts[s] // LANES, my_start)
        limit = jnp.where(member == s, fresh[s], limit)

    def packed(index):
        start = (my_start + index * (part // LANES)).reshape(1)
        return run(lambda *a: pack(*a, part), w_gate, w_up, w_down, start)

    longest = 3 * n_ctx * rows // 8
    behind = min(n_ctx - 1, (longest - 1 + rows - 1) // rows)
    half_dim = HD // 2

    def places(lengths, span_order):
        seq_ends = jnp.cumsum(lengths[0])
        row = jnp.arange(rows, dtype=jnp.int32)
        stored = jnp.where(flipped, (row + half) % rows, row)

        def packed_of(context):
            owner = lax.dynamic_index_in_dim(span_order[0], context, 0, keepdims=False)
            span = stored // piece_rows
            hot = span[:, None] == jnp.arange(n_ctx, dtype=jnp.int32)[None, :]
            spot = jnp.sum(jnp.where(hot, owner[None, :], 0), axis=1)
            return context * rows + spot * piece_rows + stored % piece_rows

        own_at = packed_of(my_ctx)
        passed = own_at[:, None] >= seq_ends[None, :]
        begin = jnp.max(jnp.where(passed, seq_ends[None, :], 0), axis=1)
        position = own_at - begin
        key_at = [own_at]
        for step in range(1, behind + 1):
            there = packed_of(jnp.maximum(my_ctx - step, 0))
            key_at.append(jnp.where(my_ctx >= step, there, far_away))
        frequency = rope_base ** (-(jnp.arange(half_dim, dtype=f32) * 2.0) / HD)
        angles = position.astype(f32)[:, None] * frequency[None, :]
        cosine, sine = jnp.cos(angles), jnp.sin(angles)
        return (
            begin[:, None],
            own_at[:, None],
            jnp.concatenate(key_at)[None, :],
            jnp.concatenate([cosine, cosine], axis=1),
            jnp.concatenate([-sine, sine], axis=1),
        )

    index = my_fsdp.astype(jnp.int32).reshape(1)
    ctx = my_ctx.astype(jnp.int32).reshape(1)
    feed_in = [packed(0)]
    mine_tokens, other_tokens = run(arrange, tokens)
    feed_in.append(packed(1))
    far = qkv_h.turn()
    out_h = Pieces(run, out_cast, far)
    feed_in += [packed(i) for i in range(2, PARTS)]
    low, high, key_at, cos_table, sin_table = run(places, lengths, span_order)
    qkv_h.finish()

    def in_order(pieces, axis, cut=None):
        if shard % LANES == 0:
            return pieces
        order = fsdp_order(n_fsdp)
        blocks = [pieces[order.index(i)] for i in range(n_fsdp)]
        blocks = [b if cut is None else b[:cut] for b in blocks]
        return [jnp.concatenate(xor_blocks(blocks, my_fsdp, n_fsdp), axis=axis)]

    gains, bias = run(lambda i, p: vectors(i, p, all_heads), index, qkv_h.pieces())
    qkv_w = in_order(qkv_h.pieces(), 0, shard)

    queries, kv_own, normed = run(
        lambda *a: project(*a, q_width),
        index, mine_tokens, other_tokens, gains, bias, cos_table, sin_table, qkv_w,
    )
    kv_parts = [kv_own] + [shift(kv_own, "context", step) for step in range(1, behind + 1)]
    normed_rel = run(lambda v: to_relative(v, my_fsdp, n_fsdp), normed)
    grads_own = run.pin(grads_own)
    grads = (grads_own, swap(grads_own, "tensor", 1))
    far = out_h.turn()
    feed_w = [lax.all_gather(after(v, far), "fsdp") for v in feed_in]
    kv_parts = [kv_own] + list(run.pin(tuple(kv_parts[1:])))
    out_h.finish()
    out_w = in_order(out_h.pieces(), 1)
    branch_mine, attended, branch_other = run(
        lambda *a: (lambda o, m, s: (m, o, s))(*attend(*a)),
        index, queries, low, high, key_at, out_w, kv_parts,
    )
    branch_other = swap(branch_other, "tensor", 1)
    sent = run(lambda a, b: jnp.concatenate([a, b[:, D // 2 :]], axis=1), attended, normed_rel)
    early_beside = swap(sent, "fsdp", 1)
    grads = run.pin(grads)
    middle, normed_two = run(
        middle_norm, mine_tokens, branch_mine, branch_other, gains
    )
    lines = Rows(normed_two)
    lines.early()
    early_beside = run.pin(early_beside)
    attended_beside, normed_beside = early_beside[:, :q_width], early_beside[:, q_width:]
    lines.turn()
    lines.across_team()
    lines.pin_early()
    lines.late()
    lines.pin_team()
    lines.across_rest()

    limits = [limit.reshape(1)] + [jnp.zeros((1,), jnp.int32)] * (PARTS - 1)
    acts, acts_beside = {}, {}
    total_rows = n_ctx * rows

    def feed_team(index, carry, last=False):
        acts[index], *carry = run(
            lambda *a: feed(*a[:5], total_rows, True, a[5], last),
            limits[index], ctx, lines.team(), grads, feed_w[index], carry,
        )
        return tuple(carry)

    def feed_rest(index):
        (acts[index],) = run(
            lambda *a: feed(*a[:5], total_rows, False, act=a[5]),
            limits[index], ctx, lines.rest(), grads, feed_w[index], acts[index],
        )
        acts_beside[index] = swap(acts[index], "fsdp", 1)

    waiting, reduced, other_parts = {}, {}, {}

    def grads_of(index):
        far, near = run(
            lambda *a: weight_grads(*a)[::-1],
            turned, turned_beside, acts[index], acts_beside[index],
        )
        bits = bits_of(n_fsdp)[1:]
        for bit in bits[:-1]:
            total = near.astype(f32) + swap(far, "fsdp", bit).astype(f32)
            cut = total.shape[1] // 2
            far, near = total[:, cut:].astype(bf16), total[:, :cut].astype(bf16)
        waiting[index] = (near, swap(far, "fsdp", bits[-1]))

    def give(near, arrived):
        return (near.astype(f32) + arrived.astype(f32)).astype(bf16)

    def add_far(index):
        reduced[index] = run(give, *waiting[index])
        other_parts[index] = swap(reduced[index], "context", 1)

    carry = feed_team(0, ())
    lines.pin_rest()
    turned, turned_sent = run(
        lambda *a: turn_rows(*a, n_fsdp), index, ctx, lines.team() + lines.rest(), grads
    )
    turned_beside = swap(turned_sent, "fsdp", 1)
    feed_rest(0)
    carry = feed_team(1, carry)
    grads_of(0)
    feed_rest(1)
    given = feed_team(2, carry, True)
    d_near, d_beside, d_far, d_far_beside = given[:4]
    out_near, out_beside, out_far = given[4:]
    d_far_beside, d_far = swap(d_far_beside, "tensor", 1), swap(d_far, "tensor", 1)
    feed_rest(2)
    d_beside = swap(run(give, d_beside, d_far_beside), "context", 1)
    d_far = run.pin(d_far)
    grads_of(1)
    add_far(0)
    d_middle, d_branch, grad_gain_two = run(
        middle_back, d_near, d_far, d_beside, middle, gains, grad_mine
    )
    d_branch_other = swap(d_branch, "tensor", 1)
    grads_of(2)
    d_branch_other = run.pin(d_branch_other)
    d_all = run(lambda *a: to_relative(stack(*a), my_fsdp, n_fsdp), d_branch, d_branch_other)
    d_all_beside = swap(d_all[:, D // 2 :], "fsdp", 1)
    d_all_beside = run.pin(d_all_beside)
    dq_low, *dkv_parts = run(
        attend_back,
        index, queries, low, high, key_at, cos_table, sin_table,
        (d_branch, d_branch_other), out_w, kv_parts,
    )
    dkv_parts = [dkv_parts[0]] + [
        shift(p, "context", -step - 1) for step, p in enumerate(dkv_parts[1:])
    ]
    add_far(1)
    other_parts[0] = run.pin(other_parts[0])

    def halves(values, axis):
        cut = values.shape[axis] // 2
        return (
            lax.slice_in_dim(values, 0, cut, axis=axis),
            lax.slice_in_dim(values, cut, 2 * cut, axis=axis),
        )

    class Reduce:
        def __init__(self, axis, full, full_beside, split, split_beside):
            self.axis, self.other = axis, 1 - axis
            self.full, self.full_beside = full, full_beside
            self.kept, self.kept_beside = split[:, : D // 2], split_beside
            self.todo = [("fsdp", bit) for bit in bits_of(n_fsdp)[1:]]
            self.todo += [("context", bit) for bit in bits_of(n_ctx)]
            self.back = [bit for bit in reversed(bits_of(n_ctx))]
            self.value = None

        def cut(self, total):
            name, bit = self.todo[0]
            if name == "fsdp":
                keep, send = halves(total, self.axis)
                return keep, send.astype(bf16)
            first, second = halves(total, self.other)
            on = (my_ctx & bit) != 0
            return jnp.where(on, second, first), jnp.where(on, first, second).astype(bf16)

        def send(self, pair):
            name, bit = self.todo.pop(0)
            self.keep, sent = pair
            self.sent = swap(sent, name, bit)

        def first(self):
            def product(full, kept, full_beside, kept_beside):
                left, right = stack(kept, kept_beside), stack(full, full_beside)
                if self.axis == 1:
                    left, right = right, left
                return self.cut(dot_rows(left, right))

            self.send(run(product, self.full, self.kept, self.full_beside, self.kept_beside))

        def step(self):
            if self.todo:
                self.send(run(lambda a, b: self.cut(a + b.astype(f32)), self.keep, self.sent))
                return
            if self.value is None:
                self.value = run(give, self.keep, self.sent)
            else:
                self.value = self.join()
            self.bit = self.back.pop(0)
            self.sent = swap(self.value, "context", self.bit)

        def join(self):
            on = (my_ctx & self.bit) != 0

            def both(mine, other):
                return jnp.concatenate(
                    [jnp.where(on, other, mine), jnp.where(on, mine, other)], axis=self.other
                )

            return run(both, self.value, self.sent)

    reduce_o = Reduce(1, attended, attended_beside, d_all, d_all_beside)
    reduce_o.first()
    d_qkv, dn_mine, dn_other, grad_bias = run(
        project_back, index, dq_low, cos_table, sin_table, qkv_w, dkv_parts
    )
    d_qkv_beside = swap(d_qkv, "fsdp", 1)
    dn_other = swap(dn_other, "tensor", 1)
    placed = ()

    def place_part(index, placed):
        return run(
            lambda m, a, b, c: place(m, a, b, index, starts, fresh, ff_local, c),
            member.reshape(1), reduced[index], other_parts[index], placed,
        )

    placed = place_part(0, placed)
    reduce_qkv = Reduce(0, d_qkv, d_qkv_beside, normed_rel, normed_beside)
    reduce_qkv.first()
    d_inputs, grad_gain_one = run(
        input_back, dn_mine, dn_other, mine_tokens, gains, d_middle
    )
    reduce_o.step()
    add_far(2)
    d_inputs_other = swap(d_inputs, "tensor", 1)
    reduce_qkv.step()
    d_inputs_other = run.pin(d_inputs_other)
    out_far = swap(out_far, "tensor", 1)
    reduce_o.step()
    other_parts[1] = run.pin(other_parts[1])
    reduce_qkv.step()
    out_mine, out_beside = run(
        lambda a, b, c: (a + c[:half].astype(f32), give(b, c[half:])), out_near, out_beside, out_far
    )
    out_beside = swap(out_beside, "context", 1)
    reduce_o.step()
    reduce_qkv.step()
    placed = place_part(1, placed)
    out_half = run(
        lambda a, b, c: (a + b + c.astype(f32)).astype(bf16), middle, out_mine, out_beside
    )
    out_half_other = swap(out_half, "tensor", 1)

    gain_rows = run(stack, grad_gain_one, grad_gain_two)
    gain_other = swap(gain_rows, "tensor", 1)

    def smalls(gain_rows, gain_other, grad_bias):
        gain_rows = jnp.pad(gain_rows + gain_other, ((0, 6), (0, 0)))
        biases = jnp.pad(grad_bias.reshape(all_heads, HD), ((0, 0), (0, D - HD)))
        return stack(gain_rows, biases)

    reduce_o.step()
    reduce_qkv.step()
    small = run(smalls, gain_rows, gain_other, grad_bias)
    steps = [("fsdp", bit) for bit in bits_of(n_fsdp)] + [("context", bit) for bit in bits_of(n_ctx)]

    def small_step(small):
        name, bit = steps.pop(0)
        return run(jnp.add, small, swap(small, name, bit))

    small = small_step(small)
    while reduce_o.back:
        reduce_o.step()
        reduce_qkv.step()
        small = small_step(small)
    while steps:
        small = small_step(small)
    grad_o = reduce_o.join().astype(f32)
    grad_qkv = reduce_qkv.join().astype(f32)
    grad_gate, grad_up, grad_down = place_part(2, placed)
    grad_biases = small[8 : 8 + all_heads, :bias_cols]
    small_gains = small[:2, :shard]
    for f in range(1, n_fsdp):
        there = small[8 : 8 + all_heads, f * bias_cols : (f + 1) * bias_cols]
        grad_biases = jnp.where(my_fsdp == f, there, grad_biases)
        small_gains = jnp.where(my_fsdp == f, small[:2, f * shard : (f + 1) * shard], small_gains)
    def restore(low_half, other_half):
        both = mine_first(stack(low_half, other_half))
        return both.astype(f32)

    return (
        restore(out_half, out_half_other),
        restore(d_inputs, d_inputs_other),
        small_gains[0],
        grad_qkv[:, :q_width],
        grad_biases[:heads_local],
        grad_qkv[:, q_width : q_width + kv_width],
        grad_biases[heads_local : heads_local + 1],
        grad_qkv[:, q_width + kv_width :],
        grad_biases[heads_local + 1 :],
        grad_o,
        small_gains[1],
        grad_gate,
        grad_up,
        grad_down,
    )


def solution(mesh):
    in_specs = (
        P(("fsdp", "context"), None),
        P(("fsdp", "context"), None),
        P("fsdp", None),
        P("fsdp", None, None),
        P("fsdp"),
        P("fsdp", "tensor"),
        P("tensor", "fsdp"),
        P("fsdp", "tensor"),
        P("tensor", "fsdp"),
        P("fsdp", "tensor"),
        P("tensor", "fsdp"),
        P("tensor", "fsdp"),
        P("fsdp"),
        P("fsdp", "tensor"),
        P("fsdp", "tensor"),
        P("tensor", "fsdp"),
    )
    out_specs = (
        P(("fsdp", "context"), None),
        P(("fsdp", "context"), None),
        P("fsdp"),
        P("fsdp", "tensor"),
        P("tensor", "fsdp"),
        P("fsdp", "tensor"),
        P("tensor", "fsdp"),
        P("fsdp", "tensor"),
        P("tensor", "fsdp"),
        P("tensor", "fsdp"),
        P("fsdp"),
        P("fsdp", "tensor"),
        P("fsdp", "tensor"),
        P("tensor", "fsdp"),
    )
    return jax.shard_map(
        per_device, mesh=mesh, in_specs=in_specs, out_specs=out_specs, check_vma=False
    )
```

```python
import functools

import jax
import jax.numpy as jnp
from jax import lax
from jax.experimental import pallas as pl
from jax.experimental.pallas import tpu as pltpu
from jax.sharding import PartitionSpec as P

D = 1536
HD = 128
LANES = 128
TEAM = 2
PARTS = 3
WIDE = 256
SHARED_PARTS = 1

epsilon = 1e-06
rope_base = 10000.0
neg_big = -1e30
far_away = 1 << 29
bf16 = jnp.bfloat16
f32 = jnp.float32


def dot_plain(left_op, right_op):
    return jnp.dot(left_op, right_op, preferred_element_type=f32)


def dot_rows(left_op, right_op):
    return lax.dot_general(
        left_op, right_op, (((0,), (0,)), ((), ())), preferred_element_type=f32
    )


def dot_cols(left_op, right_op):
    return lax.dot_general(
        left_op, right_op, (((1,), (1,)), ((), ())), preferred_element_type=f32
    )


def swap(values, axis_name, bit):
    size = lax.axis_size(axis_name)
    return lax.ppermute(values, axis_name, [(i, i ^ bit) for i in range(size)])


def shift(values, axis_name, step):
    size = lax.axis_size(axis_name)
    pairs = [(i, i + step) for i in range(size) if 0 <= i + step < size]
    return lax.ppermute(values, axis_name, pairs)


def bits_of(size):
    found = []
    bit = 1
    while bit < size:
        found.append(bit)
        bit *= 2
    return found


def fsdp_order(size):
    order = [0]
    for bit in reversed(bits_of(size)):
        order = order + [held ^ bit for held in order]
    return order


def gather_pieces(piece):
    pieces = [piece]
    for bit in reversed(bits_of(lax.axis_size("fsdp"))):
        pieces = pieces + [swap(held, "fsdp", bit) for held in pieces]
    return pieces


def xor_blocks(blocks, index, size):
    for bit in bits_of(size):
        on = (index & bit) != 0
        blocks = [jnp.where(on, blocks[i ^ bit], blocks[i]) for i in range(size)]
    return blocks


def to_relative(values, index, size):
    width = values.shape[-1] // size
    blocks = [values[..., i * width : (i + 1) * width] for i in range(size)]
    blocks = xor_blocks(blocks, index, size)
    return jnp.concatenate([blocks[i] for i in fsdp_order(size)], axis=-1)


def from_relative(values, index, size):
    width = values.shape[-1] // size
    order = fsdp_order(size)
    blocks = [None] * size
    for place, i in enumerate(order):
        blocks[i] = values[..., place * width : (place + 1) * width]
    return jnp.concatenate(xor_blocks(blocks, index, size), axis=-1)


def reduce_fsdp(values, axis):
    for bit in bits_of(lax.axis_size("fsdp")):
        half = values.shape[axis] // 2
        kept = lax.slice_in_dim(values, 0, half, axis=axis)
        sent = lax.slice_in_dim(values, half, 2 * half, axis=axis).astype(bf16)
        values = kept.astype(f32) + swap(sent, "fsdp", bit).astype(f32)
    return values


def sum_context(values):
    index = lax.axis_index("context")
    bits = bits_of(lax.axis_size("context"))
    for bit in bits:
        half = values.shape[0] // 2
        on = (index & bit) != 0
        kept = jnp.where(on, values[half:], values[:half])
        sent = jnp.where(on, values[:half], values[half:]).astype(bf16)
        values = kept + swap(sent, "context", bit).astype(f32)
    values = values.astype(bf16)
    for bit in reversed(bits):
        on = (index & bit) != 0
        other = swap(values, "context", bit)
        values = jnp.concatenate(
            [jnp.where(on, other, values), jnp.where(on, values, other)], axis=0
        )
    return values.astype(f32)


def whole(array):
    return pl.BlockSpec(array.shape, lambda *ids: (0,) * array.ndim)


def wide_enough(pieces, axis):
    if pieces[0].shape[axis] % LANES:
        return [jnp.concatenate(pieces, axis=axis)]
    return pieces


SCALE = 0.5


def cost(us=1):
    return pl.CostEstimate(
        flops=int(us * SCALE * 1.1e9), bytes_accessed=int(us * SCALE * 3.6e6), transcendentals=0
    )


def joined(refs, index_ref, axis, cut=None):
    blocks = [r[...] if cut is None else r[cut] for r in refs]
    if len(blocks) > 1:
        order = fsdp_order(len(blocks))
        blocks = [blocks[order.index(i)] for i in range(len(blocks))]
        blocks = xor_blocks(blocks, index_ref[0], len(blocks))
    return jnp.concatenate(blocks, axis=axis)


def params(mib):
    return pltpu.CompilerParams(vmem_limit_bytes=mib << 20)


def pack_body(count, start_ref, *refs):
    out_ref = refs[-1]
    for i in range(count):
        at = slice(i * LANES, (i + 1) * LANES)
        out_ref[0, :, at] = refs[i][...].astype(bf16)
        out_ref[1, :, at] = refs[count + i][...].astype(bf16)
        out_ref[2, :, at] = refs[2 * count + i][...].T.astype(bf16)


def pack(w_gate, w_up, w_down, start, width):
    shard = w_gate.shape[0]
    count = width // LANES
    columns = [pl.BlockSpec((shard, LANES), lambda j, s, i=i: (0, s[0] + i)) for i in range(count)]
    lines = [pl.BlockSpec((LANES, shard), lambda j, s, i=i: (s[0] + i, 0)) for i in range(count)]
    spec = pltpu.PrefetchScalarGridSpec(
        num_scalar_prefetch=1,
        grid=(1,),
        in_specs=columns + columns + lines,
        out_specs=pl.BlockSpec((3, shard, width), lambda j, s: (0, 0, 0)),
    )
    return pl.pallas_call(
        functools.partial(pack_body, count),
        out_shape=jax.ShapeDtypeStruct((3, shard, width), bf16),
        grid_spec=spec,
        cost_estimate=cost(),
        compiler_params=params(60),
    )(start, *[w_gate] * count, *[w_up] * count, *[w_down] * count)


def vectors_body(count, heads, index_ref, *refs):
    gain_ref, bias_ref = refs[count:]
    width = D // count
    gain_ref[...] = joined(refs[:count], index_ref, 1, (slice(0, 2), slice(0, width)))
    bias_ref[...] = sum(r[8 : 8 + heads, :HD].astype(f32) for r in refs[:count])


def vectors(index, pieces, heads):
    shard = D // len(pieces)
    if shard % LANES:
        order = fsdp_order(len(pieces))
        blocks = [pieces[order.index(i)][shard : shard + 2, :shard] for i in range(len(pieces))]
        gains = jnp.concatenate(xor_blocks(blocks, index[0], len(pieces)), axis=1)
        return gains, sum(p[shard + 8 : shard + 8 + heads, :HD].astype(f32) for p in pieces)
    rows = pl.BlockSpec((16, pieces[0].shape[1]), lambda i: (shard // 16, 0))
    outs = (jax.ShapeDtypeStruct((2, D), bf16), jax.ShapeDtypeStruct((heads, HD), f32))
    return pl.pallas_call(
        functools.partial(vectors_body, len(pieces), heads),
        out_shape=outs,
        grid=(1,),
        in_specs=[pl.BlockSpec(memory_space=pltpu.SMEM)] + [rows] * len(pieces),
        out_specs=tuple(whole(a) for a in outs),
        cost_estimate=cost(),
        compiler_params=params(60),
    )(index, *pieces)


def project_body(count, q_width, index_ref, a_ref, b_ref, gain_ref, bias_ref, cos_ref, sin_ref, *refs):
    w_refs, (q_ref, kv_ref, h_ref) = refs[:count], refs[count:]
    x = jnp.concatenate([a_ref[...], b_ref[...]], axis=0).astype(f32)
    scale = lax.rsqrt(jnp.mean(x * x, axis=-1, keepdims=True) + epsilon)
    normed = (x * scale * gain_ref[0:1].astype(f32)).astype(bf16)
    h_ref[...] = normed
    total = w_refs[0].shape[1]
    depth = D // count
    for at in range(0, total, WIDE):
        weights = joined(w_refs, index_ref, 0, (slice(0, depth), slice(at, at + WIDE)))
        both = dot_plain(normed, weights)
        for inner in range(0, WIDE, HD):
            place = at + inner
            head = place // HD
            values = both[:, inner : inner + HD] + bias_ref[head : head + 1]
            if place < total - HD:
                turned = pltpu.roll(values, HD // 2, 1)
                values = values * cos_ref[...] + turned * sin_ref[...]
            if place < q_width:
                q_ref[:, place : place + HD] = values.astype(bf16)
            else:
                kv_ref[:, place - q_width : place - q_width + HD] = values.astype(bf16)


def project(index, first, second, gain, bias, cos_table, sin_table, weights, q_width):
    rows = 2 * first.shape[0]
    total = weights[0].shape[1]
    return pl.pallas_call(
        functools.partial(project_body, len(weights), q_width),
        out_shape=(
            jax.ShapeDtypeStruct((rows, q_width), bf16),
            jax.ShapeDtypeStruct((rows, total - q_width), bf16),
            jax.ShapeDtypeStruct((rows, D), bf16),
        ),
        in_specs=[pl.BlockSpec(memory_space=pltpu.SMEM)] + [pl.BlockSpec(memory_space=pltpu.VMEM)] * (6 + len(weights)),
        cost_estimate=cost(4),
        compiler_params=params(60),
    )(index, first, second, gain, bias, cos_table, sin_table, *weights)


def masked_weights(queries, keys, low_ref, high_ref, key_ref):
    scores = dot_cols(queries, keys) * HD ** (-0.5)
    key_at = key_ref[...]
    allowed = (key_at >= low_ref[...]) & (key_at <= high_ref[...])
    scores = jnp.where(allowed, scores, neg_big)
    top = jnp.max(scores, axis=-1, keepdims=True)
    raised = jnp.exp(scores - top)
    return raised * (1.0 / jnp.sum(raised, axis=-1, keepdims=True))


def attend_body(count, ahead, index_ref, q_ref, low_ref, high_ref, key_ref, *refs):
    w_refs, kv_refs = refs[:count], refs[count : count + ahead]
    o_ref, mine_ref, other_ref = refs[count + ahead :]
    keys = jnp.concatenate([kv[:, :HD] for kv in kv_refs], axis=0)
    values = jnp.concatenate([kv[:, HD:] for kv in kv_refs], axis=0)
    weights = masked_weights(q_ref[...], keys, low_ref, high_ref, key_ref)
    head = pl.program_id(0)
    out = dot_plain(weights.astype(bf16), values).astype(bf16)
    o_ref[:, pl.ds(pl.multiple_of(head * HD, HD), HD)] = out

    @pl.when(head == pl.num_programs(0) - 1)
    def _():
        half = mine_ref.shape[0]
        out_w = joined(w_refs, index_ref, 1)
        branch = dot_plain(o_ref[...], out_w)
        mine_ref[...] = branch[:half]
        other_ref[...] = branch[half:].astype(bf16)


def attend(index, queries, low, high, key_at, weights, kv_parts):
    rows, width = queries.shape
    head = pl.BlockSpec((rows, HD), lambda h: (0, h))
    keys = key_at.shape[1]
    rest = (low, high, key_at, *weights, *kv_parts)
    outs = (
        jax.ShapeDtypeStruct(queries.shape, bf16),
        jax.ShapeDtypeStruct((rows // 2, D), f32),
        jax.ShapeDtypeStruct((rows // 2, D), bf16),
    )
    return pl.pallas_call(
        functools.partial(attend_body, len(weights), len(kv_parts)),
        out_shape=outs,
        grid=(width // HD,),
        in_specs=[pl.BlockSpec(memory_space=pltpu.SMEM), head] + [whole(a) for a in rest],
        out_specs=tuple(whole(a) for a in outs),
        compiler_params=params(60),
        cost_estimate=cost(8),
    )(index, queries, *rest)


def middle_body(x_ref, mine_ref, other_ref, gain_ref, mid_ref, h_ref):
    middle = x_ref[...].astype(f32) + mine_ref[...] + other_ref[...].astype(f32)
    scale = lax.rsqrt(jnp.mean(middle * middle, axis=-1, keepdims=True) + epsilon)
    mid_ref[...] = middle
    h_ref[...] = (middle * scale * gain_ref[1:2].astype(f32)).astype(bf16)


def middle_norm(x, mine, other, gain):
    return pl.pallas_call(
        middle_body,
        out_shape=(jax.ShapeDtypeStruct(mine.shape, f32), jax.ShapeDtypeStruct(mine.shape, bf16)),
        cost_estimate=cost(),
        compiler_params=params(60),
    )(x, mine, other, gain)


def feed_body(
    count, bases, back, carried, last, filled, at_row, limit_ref, ctx_ref, *refs
):
    h_refs, refs = refs[: 2 * len(bases)], refs[2 * len(bases) :]
    (g_own, g_across, w_ref), refs = refs[:3], refs[3:]
    carry, refs = refs[: 2 * carried], refs[2 * carried + filled :]
    outs, (act_ref, sems) = refs[:-2], refs[-2:]
    gate_w, up_w, down_w = (
        jnp.concatenate([w_ref[i, k] for i in range(count)], axis=0) for k in range(3)
    )
    rows = act_ref.shape[1]
    lane = lax.broadcasted_iota(jnp.int32, (1, act_ref.shape[2]), 1)
    shown = lane >= limit_ref[0]
    half = g_own.shape[1]
    chunk = 2 * half
    at = 0
    for which, h_ref in enumerate(h_refs):
        base, g_ref = bases[which // 2], (g_own, g_across)[which % 2]
        for j in range(h_ref.shape[0] // chunk):
            rows_in = h_ref[j * chunk : (j + 1) * chunk]
            grads_in = jnp.concatenate(
                [g_ref[ctx_ref[0] ^ (base + 2 * j + k)] for k in range(2)], axis=0
            )
            gate = dot_plain(rows_in, gate_w)
            up = dot_plain(rows_in, up_w)
            d_hidden = dot_plain(grads_in, down_w)
            gate_sig = jax.nn.sigmoid(gate)
            activated = gate * gate_sig
            hidden = activated * up
            d_gate = d_hidden * up * gate_sig * (1.0 + gate * (1.0 - gate_sig))
            d_up = d_hidden * activated
            act_ref[0, at : at + chunk] = jnp.where(shown, d_gate, 0.0).astype(bf16)
            act_ref[1, at : at + chunk] = jnp.where(shown, d_up, 0.0).astype(bf16)
            act_ref[2, at : at + chunk] = jnp.where(shown, hidden, 0.0).astype(bf16)
            at += chunk
    copies = [
        pltpu.make_async_copy(act_ref.at[k], outs[k].at[pl.ds(at_row, rows)], sems.at[k])
        for k in range(3)
    ]
    for copy in copies:
        copy.start()
    if back:
        team = slice(0, 2 * chunk)
        d_rows = dot_cols(act_ref[0, team], gate_w) + dot_cols(act_ref[1, team], up_w)
        out_rows = dot_cols(act_ref[2, team], down_w)
        if carried:
            d_rows = d_rows + carry[0][...]
            out_rows = out_rows + carry[1][...]
        if last:
            cuts = ((0, half), (half, 2 * half), (2 * half, 4 * half))
            for group, total in ((outs[3:6], d_rows), (outs[6:], out_rows)):
                for ref, (low, high) in zip(group, cuts):
                    ref[...] = total[low:high].astype(ref.dtype)
        else:
            outs[3][...] = d_rows
            outs[4][...] = out_rows
    for copy in copies:
        copy.wait()


def feed(limit, ctx, rows_in, grads_in, weights, total, back, carry=(), last=False, act=None):
    some = sum(r.shape[0] for r in rows_in)
    width = weights.shape[3]
    outs = [jax.ShapeDtypeStruct((total, width), bf16)] * 3
    half = grads_in[0].shape[1]
    if back and last:
        group = [jax.ShapeDtypeStruct((half, D), f32)] * 2
        outs += (group + [jax.ShapeDtypeStruct((2 * half, D), bf16)]) * 2
    elif back:
        outs += [jax.ShapeDtypeStruct((4 * half, D), f32)] * 2
    vmem = pl.BlockSpec(memory_space=pltpu.VMEM)
    smem = pl.BlockSpec(memory_space=pltpu.SMEM)
    hbm = pl.BlockSpec(memory_space=pl.ANY)
    inputs = (*rows_in, *grads_in, weights, *carry)
    filled = () if act is None else tuple(act)
    return pl.pallas_call(
        functools.partial(
            feed_body, weights.shape[0],
            ((0,) if back else ()) + ((TEAM,) if some == total or not back else ()),
            back, len(carry) // 2, last, len(filled), 0 if back else total - some,
        ),
        out_shape=tuple(outs),
        in_specs=[smem, smem] + [vmem] * len(inputs) + [hbm] * len(filled),
        out_specs=tuple([hbm] * 3 + [vmem] * (len(outs) - 3)),
        scratch_shapes=[pltpu.VMEM((3, some, width), bf16), pltpu.SemaphoreType.DMA((3,))],
        input_output_aliases={2 + len(inputs) + k: k for k in range(len(filled))},
        compiler_params=params(60),
        cost_estimate=cost((6 if back else 0) + 9 * some / 512),
    )(limit, ctx, *inputs, *filled)


def turn_body(contexts, blocks, index_ref, ctx_ref, *refs):
    lines, (g_own, g_across, kept_ref, sent_ref) = refs[:-4], refs[-4:]
    width = D // blocks
    order = fsdp_order(blocks)
    half = g_own.shape[1]

    def put(which, at, value):
        here = slice(at, at + value.shape[0])
        parts = [value[:, i * width : (i + 1) * width] for i in range(blocks)]
        if blocks > 2:
            parts = xor_blocks(parts, index_ref[0], blocks)
            parts = [parts[i] for i in order]
        for spot in range(blocks // 2):
            lines_at = slice(spot * width, (spot + 1) * width)
            kept_ref[which, lines_at, here] = parts[spot].T
            sent_ref[which, lines_at, here] = parts[blocks // 2 + spot].T

    at = 0
    for ref in lines:
        put(0, at, ref[...])
        at += ref.shape[0]
    at = 0
    for group in (range(TEAM), range(TEAM, contexts)):
        for ref in (g_own, g_across):
            for k in group:
                put(1, at, ref[ctx_ref[0] ^ k])
                at += half


def turn_rows(index, ctx, rows, grads, n_fsdp):
    total = sum(r.shape[0] for r in rows)
    blocks = n_fsdp
    if D // n_fsdp % LANES:
        blocks = 2
        rows, grads = (
            [to_relative(v, index[0], n_fsdp) for v in some] for some in (rows, grads)
        )
    smem = pl.BlockSpec(memory_space=pltpu.SMEM)
    return pl.pallas_call(
        functools.partial(turn_body, grads[0].shape[0], blocks),
        out_shape=(jax.ShapeDtypeStruct((2, D // 2, total), bf16),) * 2,
        in_specs=[smem, smem] + [pl.BlockSpec(memory_space=pltpu.VMEM)] * (len(rows) + 2),
        cost_estimate=cost(7),
        compiler_params=params(60),
    )(index, ctx, *rows, *grads)


def weight_body(own_ref, beside_ref, *refs):
    acts, acts_beside, (near_ref, far_ref) = refs[:3], refs[3:6], refs[6:]
    cut = near_ref.shape[1]
    for k in range(3):
        value = dot_plain(own_ref[k // 2], acts[k][...])
        value = value + dot_plain(beside_ref[k // 2], acts_beside[k][...])
        near_ref[k] = value[:cut].astype(bf16)
        far_ref[k] = value[cut:].astype(bf16)


def weight_grads(own, beside, acts, acts_beside):
    total, width = acts[0].shape
    left = pl.BlockSpec(own.shape, lambda j: (0, 0, 0), pipeline_mode=pl.Buffered(1))
    right = pl.BlockSpec((total, WIDE), lambda j: (0, j))
    out = pl.BlockSpec((3, D // 4, WIDE), lambda j: (0, 0, j))
    return pl.pallas_call(
        weight_body,
        out_shape=(jax.ShapeDtypeStruct((3, D // 4, width), bf16),) * 2,
        grid=(width // WIDE,),
        in_specs=[left, left] + [right] * 6,
        out_specs=(out, out),
        compiler_params=params(60),
        cost_estimate=cost(12),
    )(own, beside, *acts, *acts_beside)


def middle_back_body(
    near_ref, across_ref, far_ref, mid_ref, gain_ref, g_ref, d_ref, low_ref, gain_out
):
    d_normed = near_ref[...] + across_ref[...].astype(f32) + far_ref[...].astype(f32)
    middle = mid_ref[...]
    scale = lax.rsqrt(jnp.mean(middle * middle, axis=-1, keepdims=True) + epsilon)
    gain_out[...] = jnp.sum(d_normed * middle * scale, axis=0, keepdims=True)
    weighted = d_normed * gain_ref[1:2].astype(f32)
    inner = jnp.mean(weighted * middle, axis=-1, keepdims=True)
    d_middle = g_ref[...].astype(f32) + scale * weighted - middle * scale**3 * inner
    d_ref[...] = d_middle
    low_ref[...] = d_middle.astype(bf16)


def middle_back(near, across, far, middle, gain, grads):
    return pl.pallas_call(
        middle_back_body,
        out_shape=(
            jax.ShapeDtypeStruct(near.shape, f32),
            jax.ShapeDtypeStruct(near.shape, bf16),
            jax.ShapeDtypeStruct((1, D), f32),
        ),
        cost_estimate=cost(),
        compiler_params=params(60),
    )(near, across, far, middle, gain, grads)


def attend_back_body(count, ahead, index_ref, q_ref, low_ref, high_ref, key_ref, cos_ref, sin_ref, *refs):
    scale = HD ** (-0.5)
    mine_ref, other_ref = refs[:2]
    w_refs, kv_refs = refs[2 : 2 + count], refs[2 + count : 2 + count + ahead]
    outs = refs[2 + count + ahead :]
    dq_ref, dkv_refs, (d_o, sums) = outs[0], outs[1 : 1 + ahead], outs[1 + ahead :]
    head = pl.program_id(0)

    @pl.when(head == 0)
    def _():
        d_branch = jnp.concatenate([mine_ref[...], other_ref[...]], axis=0)
        out_w = joined(w_refs, index_ref, 1)
        d_o[...] = dot_cols(d_branch, out_w).astype(bf16)
        sums[...] = jnp.zeros_like(sums)

    queries = q_ref[...]
    grad = d_o[:, pl.ds(pl.multiple_of(head * HD, HD), HD)]
    keys = jnp.concatenate([kv[:, :HD] for kv in kv_refs], axis=0)
    values = jnp.concatenate([kv[:, HD:] for kv in kv_refs], axis=0)
    weights = masked_weights(queries, keys, low_ref, high_ref, key_ref)
    dweights = dot_cols(grad, values)
    delta = jnp.sum(weights * dweights, axis=-1, keepdims=True)
    dscores = (weights * (dweights - delta)).astype(bf16)
    dq_rot = dot_plain(dscores, keys) * scale
    turned = pltpu.roll(dq_rot, HD // 2, 1)
    dq_ref[...] = (dq_rot * cos_ref[...] - turned * sin_ref[...]).astype(bf16)
    sums[:, :HD] += dot_rows(dscores, queries) * scale
    sums[:, HD:] += dot_rows(weights.astype(bf16), grad)

    @pl.when(head == pl.num_programs(0) - 1)
    def _():
        rows = q_ref.shape[0]
        for i, out in enumerate(dkv_refs):
            out[...] = sums[i * rows : (i + 1) * rows].astype(out.dtype)


def attend_back(index, queries, low, high, key_at, cos_table, sin_table, grads, weights, kv_parts):
    rows, width = queries.shape
    head = pl.BlockSpec((rows, HD), lambda h: (0, h))
    keys = key_at.shape[1]
    rest = (low, high, key_at, cos_table, sin_table, *grads, *weights, *kv_parts)
    outs = [jax.ShapeDtypeStruct(queries.shape, bf16)]
    outs += [
        jax.ShapeDtypeStruct(kv.shape, bf16 if i else f32) for i, kv in enumerate(kv_parts)
    ]
    return pl.pallas_call(
        functools.partial(attend_back_body, len(weights), len(kv_parts)),
        out_shape=tuple(outs),
        grid=(width // HD,),
        in_specs=[pl.BlockSpec(memory_space=pltpu.SMEM), head] + [whole(a) for a in rest],
        out_specs=tuple([head] + [whole(a) for a in outs[1:]]),
        scratch_shapes=[pltpu.VMEM((rows, width), bf16), pltpu.VMEM((keys, 2 * HD), f32)],
        compiler_params=params(60),
        cost_estimate=cost(10),
    )(index, queries, *rest)


def project_back_body(count, ahead, index_ref, dq_ref, cos_ref, sin_ref, *refs):
    w_refs, dkv_refs = refs[:count], refs[count : count + ahead]
    d_ref, mine_ref, other_ref, bias_ref = refs[count + ahead :]
    total = dkv_refs[0][...]
    for extra in dkv_refs[1:]:
        total = total + extra[...].astype(f32)
    dk = total[:, :HD]
    dk = dk * cos_ref[...] - pltpu.roll(dk, HD // 2, 1) * sin_ref[...]
    d_low = jnp.concatenate([dq_ref[...], dk.astype(bf16), total[:, HD:].astype(bf16)], axis=1)
    d_ref[...] = d_low
    bias_ref[...] = jnp.sum(d_low.astype(f32), axis=0, keepdims=True)
    weights = joined(w_refs, index_ref, 0, slice(0, D // count))
    d_normed = dot_cols(d_low, weights)
    half = mine_ref.shape[0]
    mine_ref[...] = d_normed[:half]
    other_ref[...] = d_normed[half:].astype(bf16)


def project_back(index, dq, cos_table, sin_table, weights, dkv_parts):
    rows = dq.shape[0]
    total = weights[0].shape[1]
    return pl.pallas_call(
        functools.partial(project_back_body, len(weights), len(dkv_parts)),
        out_shape=(
            jax.ShapeDtypeStruct((rows, total), bf16),
            jax.ShapeDtypeStruct((rows // 2, D), f32),
            jax.ShapeDtypeStruct((rows // 2, D), bf16),
            jax.ShapeDtypeStruct((1, total), f32),
        ),
        in_specs=[pl.BlockSpec(memory_space=pltpu.SMEM)] + [pl.BlockSpec(memory_space=pltpu.VMEM)] * (3 + len(weights) + len(dkv_parts)),
        cost_estimate=cost(4),
        compiler_params=params(60),
    )(index, dq, cos_table, sin_table, *weights, *dkv_parts)


def input_back_body(mine_ref, other_ref, x_ref, gain_ref, mid_ref, d_ref, gain_out):
    d_normed = mine_ref[...] + other_ref[...].astype(f32)
    x = x_ref[...].astype(f32)
    scale = lax.rsqrt(jnp.mean(x * x, axis=-1, keepdims=True) + epsilon)
    gain_out[...] = jnp.sum(d_normed * x * scale, axis=0, keepdims=True)
    weighted = d_normed * gain_ref[0:1].astype(f32)
    inner = jnp.mean(weighted * x, axis=-1, keepdims=True)
    d_ref[...] = (mid_ref[...] + scale * weighted - x * scale**3 * inner).astype(bf16)


def input_back(mine, other, x, gain, d_middle):
    return pl.pallas_call(
        input_back_body,
        out_shape=(jax.ShapeDtypeStruct(mine.shape, bf16), jax.ShapeDtypeStruct((1, D), f32)),
        cost_estimate=cost(),
        compiler_params=params(60),
    )(mine, other, x, gain, d_middle)


def place_body(plan, carried, member_ref, *refs):
    own_ref, other_ref, refs = refs[0], refs[1], refs[2:]
    outs = refs[carried : carried + 3]
    wide_buf, tall_buf, sems = refs[carried + 3 :]
    width = own_ref.shape[2]

    def copies(team):
        skip, at = plan[team]
        size = width - skip
        for k in range(2):
            yield pltpu.make_async_copy(
                wide_buf.at[team, k, :, pl.ds(skip, size)],
                outs[k].at[:, pl.ds(at + skip, size)],
                sems.at[team, k],
            )
        yield pltpu.make_async_copy(
            tall_buf.at[team, pl.ds(skip, size)],
            outs[2].at[pl.ds(at + skip, size)],
            sems.at[team, 2],
        )

    for team in range(len(plan)):
        def put(ref, team=team):
            wide_buf[team, 0] = ref[0].astype(f32)
            wide_buf[team, 1] = ref[1].astype(f32)
            tall_buf[team] = ref[2].astype(f32).T

        @pl.when(member_ref[0] == team)
        def _():
            put(own_ref)

        @pl.when(member_ref[0] != team)
        def _():
            put(other_ref)

        for copy in copies(team):
            copy.start()
    for team in range(len(plan)):
        for copy in copies(team):
            copy.wait()


def place(member, own, other, index, starts, fresh, ff_local, carry):
    shard, width = own.shape[1:]
    plan = tuple(
        (min(max(fresh[s] - index * width, 0), width), starts[s] + index * width)
        for s in range(TEAM)
    )
    hbm = pl.BlockSpec(memory_space=pl.ANY)
    vmem = pl.BlockSpec(memory_space=pltpu.VMEM)
    return pl.pallas_call(
        functools.partial(place_body, plan, len(carry)),
        out_shape=(
            jax.ShapeDtypeStruct((shard, ff_local), f32),
            jax.ShapeDtypeStruct((shard, ff_local), f32),
            jax.ShapeDtypeStruct((ff_local, shard), f32),
        ),
        in_specs=[pl.BlockSpec(memory_space=pltpu.SMEM)] + [vmem] * 2 + [hbm] * len(carry),
        out_specs=(hbm, hbm, hbm),
        scratch_shapes=[
            pltpu.VMEM((TEAM, 2, shard, width), f32),
            pltpu.VMEM((TEAM, width, shard), f32),
            pltpu.SemaphoreType.DMA((TEAM, 3)),
        ],
        input_output_aliases={3 + i: i for i in range(len(carry))},
        cost_estimate=cost(),
        compiler_params=params(60),
    )(member, own, other, *carry)


def after(values, *first):
    return lax.optimization_barrier((values, first))[0]


class Order:
    def __init__(self):
        self.last = ()

    def __call__(self, step, *args):
        args, _ = lax.optimization_barrier((args, self.last))
        result = step(*args)
        self.last = (jax.tree.leaves(result)[0],)
        return result

    def pin(self, values):
        values, _ = lax.optimization_barrier((values, self.last))
        self.last = (jax.tree.leaves(values)[0],)
        return values


def stack(*pieces):
    return jnp.concatenate(pieces, axis=0)


class Pieces:
    def __init__(self, run, full, *first):
        bits = list(reversed(bits_of(lax.axis_size("fsdp"))))
        self.run, self.near = run, bits[-1]
        self.held = [full]
        gate = after(full, *first)
        for bit in bits[:-1]:
            self.held = self.held + [swap(p, "fsdp", bit) for p in [gate] + self.held[1:]]

    def turn(self):
        self.held = self.held[:1] + list(self.run.pin(tuple(self.held[1:])))
        self.sent = swap(self.run(lambda *a: jnp.stack(a), *self.held), "fsdp", self.near)
        return self.held[-1]

    def finish(self):
        self.sent = self.run.pin(self.sent)

    def pieces(self):
        return self.held + [self.sent[i] for i in range(len(self.held))]


def per_device(
    tokens,
    cotangent,
    lengths,
    span_order,
    attn_gain,
    w_q,
    b_q,
    w_k,
    b_k,
    w_v,
    b_v,
    w_o,
    mlp_gain,
    w_gate,
    w_up,
    w_down,
):
    n_fsdp = lax.axis_size("fsdp")
    n_ctx = lax.axis_size("context")
    my_fsdp = lax.axis_index("fsdp")
    my_ctx = lax.axis_index("context")
    my_tensor = lax.axis_index("tensor")
    member = my_ctx % TEAM
    rows = tokens.shape[0]
    half = rows // 2
    piece_rows = rows // n_ctx
    shard = D // n_fsdp
    q_width = w_q.shape[1]
    kv_width = w_k.shape[1]
    qkv_width = q_width + 2 * kv_width
    heads_local = q_width // HD
    all_heads = qkv_width // HD
    flipped = my_tensor != 0
    run = Order()
    sharing = n_fsdp == 4 and n_ctx % 2 == 0

    def mine_first(values):
        first, second = values[:half], values[half:]
        return stack(jnp.where(flipped, second, first), jnp.where(flipped, first, second))

    bias_cols = HD // n_fsdp

    def qkv_pack(g1, g2, b_q, b_k, b_v, *w):
        biases = jnp.concatenate([b_q, b_k, b_v], axis=0).astype(bf16)
        spread = jnp.concatenate([biases] * n_fsdp, axis=1)
        lane = jnp.arange(HD, dtype=jnp.int32)[None, :] // bias_cols
        spread = jnp.where(lane == my_fsdp, spread, jnp.zeros_like(spread))
        gains = jnp.pad(jnp.stack([g1, g2]).astype(bf16), ((0, 6), (0, qkv_width - shard)))
        spread = jnp.pad(spread, ((0, 8 - all_heads), (0, qkv_width - HD)))
        return stack(jnp.concatenate(w, axis=1).astype(bf16), gains, spread)

    qkv_h = Pieces(run, run(qkv_pack, attn_gain, mlp_gain, b_q, b_k, b_v, w_q, w_k, w_v))
    out_cast = run(lambda w: w.astype(bf16), w_o)

    def arrange(values):
        both = mine_first(values)
        return both[:half], both[half:]

    class Rows:
        def __init__(self, mine):
            self.mine = mine
            self.beside = swap(mine, "context", 1)

        def turn(self):
            self.beside = run.pin(self.beside)
            self.held = run(stack, self.mine, self.beside)
            self.held_across = swap(self.held, "tensor", 1)
            held, others = self.held, []
            for bit in bits_of(n_ctx)[1:]:
                there = swap(held, "context", bit)
                others.append(there)
                held = stack(held, there)
            self.remote = others[0] if len(others) == 1 else stack(*others)

        def across_rest(self):
            self.remote = run.pin(self.remote)
            self.remote_across = swap(self.remote, "tensor", 1)

        def pin_team(self):
            self.held_across = run.pin(self.held_across)

        def pin_rest(self):
            self.remote_across = run.pin(self.remote_across)

        def team(self):
            return (self.held, self.held_across)

        def rest(self):
            return (self.remote, self.remote_across)

    grad_mine, _ = run(arrange, cotangent)
    grads_own = lax.all_gather(grad_mine, "context")

    ff_local = w_gate.shape[1]
    tiles = ff_local // LANES
    unit = PARTS * WIDE // LANES
    slice_tiles = -(-tiles // (TEAM * unit)) * unit
    part = slice_tiles // PARTS * LANES
    starts = [min(s * slice_tiles, tiles - slice_tiles) * LANES for s in range(TEAM)]
    fresh = [s * slice_tiles * LANES - starts[s] for s in range(TEAM)]
    my_start = jnp.int32(starts[0] // LANES)
    limit = jnp.int32(fresh[0])
    for s in range(1, TEAM):
        my_start = jnp.where(member == s, starts[s] // LANES, my_start)
        limit = jnp.where(member == s, fresh[s], limit)

    def packed(index):
        start = (my_start + index * (part // LANES)).reshape(1)
        return run(lambda *a: pack(*a, part), w_gate, w_up, w_down, start)

    longest = 3 * n_ctx * rows // 8
    behind = min(n_ctx - 1, (longest - 1 + rows - 1) // rows)
    half_dim = HD // 2

    def places(lengths, span_order):
        seq_ends = jnp.cumsum(lengths[0])
        row = jnp.arange(rows, dtype=jnp.int32)
        stored = jnp.where(flipped, (row + half) % rows, row)

        def packed_of(context):
            owner = lax.dynamic_index_in_dim(span_order[0], context, 0, keepdims=False)
            span = stored // piece_rows
            hot = span[:, None] == jnp.arange(n_ctx, dtype=jnp.int32)[None, :]
            spot = jnp.sum(jnp.where(hot, owner[None, :], 0), axis=1)
            return context * rows + spot * piece_rows + stored % piece_rows

        own_at = packed_of(my_ctx)
        passed = own_at[:, None] >= seq_ends[None, :]
        begin = jnp.max(jnp.where(passed, seq_ends[None, :], 0), axis=1)
        position = own_at - begin
        key_at = [own_at]
        for step in range(1, behind + 1):
            there = packed_of(jnp.maximum(my_ctx - step, 0))
            key_at.append(jnp.where(my_ctx >= step, there, far_away))
        frequency = rope_base ** (-(jnp.arange(half_dim, dtype=f32) * 2.0) / HD)
        angles = position.astype(f32)[:, None] * frequency[None, :]
        cosine, sine = jnp.cos(angles), jnp.sin(angles)
        return (
            begin[:, None],
            own_at[:, None],
            jnp.concatenate(key_at)[None, :],
            jnp.concatenate([cosine, cosine], axis=1),
            jnp.concatenate([-sine, sine], axis=1),
        )

    index = my_fsdp.astype(jnp.int32).reshape(1)
    ctx = my_ctx.astype(jnp.int32).reshape(1)
    feed_in = [packed(0)]
    mine_tokens, other_tokens = run(arrange, tokens)
    feed_in.append(packed(1))
    far = qkv_h.turn()
    out_h = Pieces(run, out_cast, far)
    feed_in += [packed(i) for i in range(2, PARTS)]
    feed_w = [lax.all_gather(after(v, far), "fsdp") for v in feed_in]
    low, high, key_at, cos_table, sin_table = run(places, lengths, span_order)
    qkv_h.finish()

    def in_order(pieces, axis, cut=None):
        if shard % LANES == 0:
            return pieces
        order = fsdp_order(n_fsdp)
        blocks = [pieces[order.index(i)] for i in range(n_fsdp)]
        blocks = [b if cut is None else b[:cut] for b in blocks]
        return [jnp.concatenate(xor_blocks(blocks, my_fsdp, n_fsdp), axis=axis)]

    gains, bias = run(lambda i, p: vectors(i, p, all_heads), index, qkv_h.pieces())
    qkv_w = in_order(qkv_h.pieces(), 0, shard)

    queries, kv_own, normed = run(
        lambda *a: project(*a, q_width),
        index, mine_tokens, other_tokens, gains, bias, cos_table, sin_table, qkv_w,
    )
    kv_parts = [kv_own] + [shift(kv_own, "context", step) for step in range(1, behind + 1)]
    grads_own = run.pin(grads_own)
    grads = (grads_own, swap(grads_own, "tensor", 1))
    normed_rel = run(lambda v: to_relative(v, my_fsdp, n_fsdp), normed)
    out_h.turn()
    kv_parts = [kv_own] + list(run.pin(tuple(kv_parts[1:])))
    out_h.finish()
    out_w = in_order(out_h.pieces(), 1)
    branch_mine, attended, branch_other = run(
        lambda *a: (lambda o, m, s: (m, o, s))(*attend(*a)),
        index, queries, low, high, key_at, out_w, kv_parts,
    )
    branch_other = swap(branch_other, "tensor", 1)
    sent = run(lambda a, b: jnp.concatenate([a, b[:, D // 2 :]], axis=1), attended, normed_rel)
    early_beside = swap(sent, "fsdp", 1)
    grads = run.pin(grads)
    middle, normed_two = run(
        middle_norm, mine_tokens, branch_mine, branch_other, gains
    )
    lines = Rows(normed_two)
    early_beside = run.pin(early_beside)
    attended_beside, normed_beside = early_beside[:, :q_width], early_beside[:, q_width:]
    lines.turn()
    lines.pin_team()

    limits = [limit.reshape(1)] + [jnp.zeros((1,), jnp.int32)] * (PARTS - 1)
    acts, acts_beside = {}, {}
    total_rows = n_ctx * rows

    def feed_team(index, carry, last=False, every=False):
        rows_in = lines.team() + lines.rest() if every else lines.team()
        results = run(
            lambda *a: feed(*a[:5], total_rows, True, a[5], last),
            limits[index], ctx, rows_in, grads, feed_w[index], carry,
        )
        acts[index] = tuple(results[:3])
        if every:
            acts_beside[index] = tuple(swap(a, "fsdp", 1) for a in acts[index])
        return tuple(results[3:])

    def feed_rest(index):
        acts[index] = run(
            lambda *a: feed(*a[:5], total_rows, False, act=a[5]),
            limits[index], ctx, lines.rest(), grads, feed_w[index], acts[index],
        )
        acts_beside[index] = tuple(swap(a, "fsdp", 1) for a in acts[index])

    waiting, reduced, other_parts = {}, {}, {}

    def grads_of(index):
        far, near = run(
            lambda *a: weight_grads(*a)[::-1],
            turned, turned_beside, acts[index], acts_beside[index],
        )
        bits = bits_of(n_fsdp)[1:]
        for bit in bits[:-1]:
            total = near.astype(f32) + swap(far, "fsdp", bit).astype(f32)
            cut = total.shape[1] // 2
            far, near = total[:, cut:].astype(bf16), total[:, :cut].astype(bf16)
        waiting[index] = (near, swap(far, "fsdp", bits[-1]))

    def give(near, arrived):
        return (near.astype(f32) + arrived.astype(f32)).astype(bf16)

    def add_far(index):
        reduced[index] = run(give, *waiting[index])
        other_parts[index] = swap(reduced[index], "context", 1)

    carry = feed_team(0, ())
    lines.across_rest()
    carry = feed_team(1, carry)
    lines.pin_rest()
    turned, turned_sent = run(
        lambda *a: turn_rows(*a, n_fsdp), index, ctx, lines.team() + lines.rest(), grads
    )
    turned_beside = swap(turned_sent, "fsdp", 1)
    feed_rest(0)
    feed_rest(1)
    grads_of(0)
    given = feed_team(2, carry, True)
    d_near, d_beside, d_far, out_near, out_beside, out_far = given
    d_far = swap(d_far, "tensor", 1)
    feed_rest(2)
    grads_of(1)
    d_beside = swap(run(lambda a, b: give(a, b[half:]), d_beside, d_far), "context", 1)
    add_far(0)
    d_middle, d_branch, grad_gain_two = run(
        lambda a, b, *c: middle_back(a, b[:half], *c),
        d_near, d_far, d_beside, middle, gains, grad_mine,
    )
    d_branch_other = swap(d_branch, "tensor", 1)
    grads_of(2)
    d_branch_other = run.pin(d_branch_other)
    d_all = run(lambda *a: to_relative(stack(*a), my_fsdp, n_fsdp), d_branch, d_branch_other)
    d_all_beside = swap(d_all[:, D // 2 :], "fsdp", 1)
    d_all_beside = run.pin(d_all_beside)
    dq_low, *dkv_parts = run(
        attend_back,
        index, queries, low, high, key_at, cos_table, sin_table,
        (d_branch, d_branch_other), out_w, kv_parts,
    )
    dkv_parts = [dkv_parts[0]] + [
        shift(p, "context", -step - 1) for step, p in enumerate(dkv_parts[1:])
    ]
    other_parts[0] = run.pin(other_parts[0])
    reduced[1] = run(give, *waiting[1])

    def halves(values, axis):
        cut = values.shape[axis] // 2
        return (
            lax.slice_in_dim(values, 0, cut, axis=axis),
            lax.slice_in_dim(values, cut, 2 * cut, axis=axis),
        )

    class Reduce:
        def __init__(self, axis, full, full_beside, split, split_beside):
            self.axis, self.other = axis, 1 - axis
            self.full, self.full_beside = full, full_beside
            self.kept, self.kept_beside = split[:, : D // 2], split_beside
            self.todo = [("fsdp", bit) for bit in bits_of(n_fsdp)[1:]]
            self.todo += [("context", bit) for bit in bits_of(n_ctx)]
            self.back = [bit for bit in reversed(bits_of(n_ctx))]
            self.value = None

        def cut(self, total):
            name, bit = self.todo[0]
            if name == "fsdp":
                keep, send = halves(total, self.axis)
                return keep, send.astype(bf16)
            first, second = halves(total, self.other)
            on = (my_ctx & bit) != 0
            return jnp.where(on, second, first), jnp.where(on, first, second).astype(bf16)

        def send(self, pair):
            name, bit = self.todo.pop(0)
            self.keep, sent = pair
            self.sent = swap(sent, name, bit)

        def first(self):
            def product(full, kept, full_beside, kept_beside):
                left, right = stack(kept, kept_beside), stack(full, full_beside)
                if self.axis == 1:
                    left, right = right, left
                return self.cut(dot_rows(left, right))

            self.send(run(product, self.full, self.kept, self.full_beside, self.kept_beside))

        def step(self):
            if self.todo:
                self.send(run(lambda a, b: self.cut(a + b.astype(f32)), self.keep, self.sent))
                return
            if self.value is None:
                self.value = run(give, self.keep, self.sent)
            else:
                self.value = self.join()
            self.bit = self.back.pop(0)
            self.sent = swap(self.value, "context", self.bit)

        def join(self):
            on = (my_ctx & self.bit) != 0

            def both(mine, other):
                return jnp.concatenate(
                    [jnp.where(on, other, mine), jnp.where(on, mine, other)], axis=self.other
                )

            return run(both, self.value, self.sent)

    def place_part(index, placed):
        return run(
            lambda m, a, b, c: place(m, a, b, index, starts, fresh, ff_local, c),
            member.reshape(1), reduced[index], other_parts[index], placed,
        )

    def smalls(gain_rows, gain_other, grad_bias):
        gain_rows = jnp.pad(gain_rows + gain_other, ((0, 6), (0, 0)))
        biases = jnp.pad(grad_bias.reshape(all_heads, HD), ((0, 0), (0, D - HD)))
        return stack(gain_rows, biases)

    steps = [("fsdp", bit) for bit in bits_of(n_fsdp)] + [("context", bit) for bit in bits_of(n_ctx)]

    def small_step(small):
        name, bit = steps.pop(0)
        return run(jnp.add, small, swap(small, name, bit))

    reduce_o = Reduce(1, attended, attended_beside, d_all, d_all_beside)
    reduce_o.first()
    dkv_parts = dkv_parts[:1] + list(run.pin(tuple(dkv_parts[1:])))
    other_parts[1] = swap(after(reduced[1], dkv_parts[-1]), "context", 1)
    d_qkv, dn_mine, dn_other, grad_bias = run(
        project_back, index, dq_low, cos_table, sin_table, qkv_w, dkv_parts
    )
    d_qkv_beside = swap(d_qkv, "fsdp", 1)
    dn_other = swap(dn_other, "tensor", 1)
    placed = place_part(0, ())
    reduce_qkv = Reduce(0, d_qkv, d_qkv_beside, normed_rel, normed_beside)
    reduce_qkv.first()
    d_inputs, grad_gain_one = run(
        input_back, dn_mine, dn_other, mine_tokens, gains, d_middle
    )
    d_inputs_other = swap(d_inputs, "tensor", 1)
    add_far(2)
    d_inputs_other = run.pin(d_inputs_other)
    other_parts[1] = run.pin(other_parts[1])
    reduce_o.step()
    gain_rows = run(stack, grad_gain_one, grad_gain_two)
    gain_other = swap(gain_rows, "tensor", 1)
    out_far = swap(after(out_far, other_parts[1]), "tensor", 1)
    reduce_qkv.step()
    small = run(smalls, gain_rows, gain_other, grad_bias)
    placed = place_part(1, placed)
    out_mine, out_beside = run(
        lambda a, b, c: (a + c[:half].astype(f32), give(b, c[half:])), out_near, out_beside, out_far
    )
    small = small_step(small)
    small = small_step(small)
    reduce_o.step()
    reduce_qkv.step()
    out_beside = swap(out_beside, "context", 1)
    other_parts[2] = run.pin(other_parts[2])
    reduce_o.step()
    reduce_qkv.step()
    small = small_step(small)
    reduce_o.step()
    out_half = run(
        lambda a, b, c: (a + b + c.astype(f32)).astype(bf16), middle, out_mine, out_beside
    )
    out_half_other = swap(out_half, "tensor", 1)
    reduce_qkv.step()
    small = small_step(small)
    placed = place_part(2, placed)
    while reduce_o.back:
        reduce_o.step()
        reduce_qkv.step()
    while steps:
        small = small_step(small)
    grad_gate, grad_up, grad_down = placed
    grad_o = reduce_o.join().astype(f32)
    grad_qkv = reduce_qkv.join().astype(f32)
    grad_biases = small[8 : 8 + all_heads, :bias_cols]
    small_gains = small[:2, :shard]
    for f in range(1, n_fsdp):
        there = small[8 : 8 + all_heads, f * bias_cols : (f + 1) * bias_cols]
        grad_biases = jnp.where(my_fsdp == f, there, grad_biases)
        small_gains = jnp.where(my_fsdp == f, small[:2, f * shard : (f + 1) * shard], small_gains)
    def restore(low_half, other_half):
        both = mine_first(stack(low_half, other_half))
        return both.astype(f32)

    return (
        restore(out_half, out_half_other),
        restore(d_inputs, d_inputs_other),
        small_gains[0],
        grad_qkv[:, :q_width],
        grad_biases[:heads_local],
        grad_qkv[:, q_width : q_width + kv_width],
        grad_biases[heads_local : heads_local + 1],
        grad_qkv[:, q_width + kv_width :],
        grad_biases[heads_local + 1 :],
        grad_o,
        small_gains[1],
        grad_gate,
        grad_up,
        grad_down,
    )


def solution(mesh):
    in_specs = (
        P(("fsdp", "context"), None),
        P(("fsdp", "context"), None),
        P("fsdp", None),
        P("fsdp", None, None),
        P("fsdp"),
        P("fsdp", "tensor"),
        P("tensor", "fsdp"),
        P("fsdp", "tensor"),
        P("tensor", "fsdp"),
        P("fsdp", "tensor"),
        P("tensor", "fsdp"),
        P("tensor", "fsdp"),
        P("fsdp"),
        P("fsdp", "tensor"),
        P("fsdp", "tensor"),
        P("tensor", "fsdp"),
    )
    out_specs = (
        P(("fsdp", "context"), None),
        P(("fsdp", "context"), None),
        P("fsdp"),
        P("fsdp", "tensor"),
        P("tensor", "fsdp"),
        P("fsdp", "tensor"),
        P("tensor", "fsdp"),
        P("fsdp", "tensor"),
        P("tensor", "fsdp"),
        P("tensor", "fsdp"),
        P("fsdp"),
        P("fsdp", "tensor"),
        P("fsdp", "tensor"),
        P("tensor", "fsdp"),
    )
    return jax.shard_map(
        per_device, mesh=mesh, in_specs=in_specs, out_specs=out_specs, check_vma=False
    )
```

```python
import functools

import jax
import jax.numpy as jnp
from jax import lax
from jax.experimental import pallas as pl
from jax.experimental.pallas import tpu as pltpu
from jax.sharding import PartitionSpec as P

D = 1536
HD = 128
LANES = 128
TEAM = 2
PARTS = 3
WIDE = 256
SHARED_PARTS = 1

epsilon = 1e-06
rope_base = 10000.0
neg_big = -1e30
far_away = 1 << 29
bf16 = jnp.bfloat16
f32 = jnp.float32


def dot_plain(left_op, right_op):
    return jnp.dot(left_op, right_op, preferred_element_type=f32)


def dot_rows(left_op, right_op):
    return lax.dot_general(
        left_op, right_op, (((0,), (0,)), ((), ())), preferred_element_type=f32
    )


def dot_cols(left_op, right_op):
    return lax.dot_general(
        left_op, right_op, (((1,), (1,)), ((), ())), preferred_element_type=f32
    )


def swap(values, axis_name, bit):
    size = lax.axis_size(axis_name)
    return lax.ppermute(values, axis_name, [(i, i ^ bit) for i in range(size)])


def shift(values, axis_name, step):
    size = lax.axis_size(axis_name)
    pairs = [(i, i + step) for i in range(size) if 0 <= i + step < size]
    return lax.ppermute(values, axis_name, pairs)


def bits_of(size):
    found = []
    bit = 1
    while bit < size:
        found.append(bit)
        bit *= 2
    return found


def fsdp_order(size):
    order = [0]
    for bit in reversed(bits_of(size)):
        order = order + [held ^ bit for held in order]
    return order


def gather_pieces(piece):
    pieces = [piece]
    for bit in reversed(bits_of(lax.axis_size("fsdp"))):
        pieces = pieces + [swap(held, "fsdp", bit) for held in pieces]
    return pieces


def xor_blocks(blocks, index, size):
    for bit in bits_of(size):
        on = (index & bit) != 0
        blocks = [jnp.where(on, blocks[i ^ bit], blocks[i]) for i in range(size)]
    return blocks


def to_relative(values, index, size):
    width = values.shape[-1] // size
    blocks = [values[..., i * width : (i + 1) * width] for i in range(size)]
    blocks = xor_blocks(blocks, index, size)
    return jnp.concatenate([blocks[i] for i in fsdp_order(size)], axis=-1)


def from_relative(values, index, size):
    width = values.shape[-1] // size
    order = fsdp_order(size)
    blocks = [None] * size
    for place, i in enumerate(order):
        blocks[i] = values[..., place * width : (place + 1) * width]
    return jnp.concatenate(xor_blocks(blocks, index, size), axis=-1)


def reduce_fsdp(values, axis):
    for bit in bits_of(lax.axis_size("fsdp")):
        half = values.shape[axis] // 2
        kept = lax.slice_in_dim(values, 0, half, axis=axis)
        sent = lax.slice_in_dim(values, half, 2 * half, axis=axis).astype(bf16)
        values = kept.astype(f32) + swap(sent, "fsdp", bit).astype(f32)
    return values


def sum_context(values):
    index = lax.axis_index("context")
    bits = bits_of(lax.axis_size("context"))
    for bit in bits:
        half = values.shape[0] // 2
        on = (index & bit) != 0
        kept = jnp.where(on, values[half:], values[:half])
        sent = jnp.where(on, values[:half], values[half:]).astype(bf16)
        values = kept + swap(sent, "context", bit).astype(f32)
    values = values.astype(bf16)
    for bit in reversed(bits):
        on = (index & bit) != 0
        other = swap(values, "context", bit)
        values = jnp.concatenate(
            [jnp.where(on, other, values), jnp.where(on, values, other)], axis=0
        )
    return values.astype(f32)


def whole(array):
    return pl.BlockSpec(array.shape, lambda *ids: (0,) * array.ndim)


def wide_enough(pieces, axis):
    if pieces[0].shape[axis] % LANES:
        return [jnp.concatenate(pieces, axis=axis)]
    return pieces


SCALE = 0.4


def cost(us=1):
    return pl.CostEstimate(
        flops=int(us * SCALE * 1.1e9), bytes_accessed=int(us * SCALE * 3.6e6), transcendentals=0
    )


def joined(refs, index_ref, axis, cut=None):
    blocks = [r[...] if cut is None else r[cut] for r in refs]
    if len(blocks) > 1:
        order = fsdp_order(len(blocks))
        blocks = [blocks[order.index(i)] for i in range(len(blocks))]
        blocks = xor_blocks(blocks, index_ref[0], len(blocks))
    return jnp.concatenate(blocks, axis=axis)


def params(mib):
    return pltpu.CompilerParams(vmem_limit_bytes=mib << 20)


def pack_body(count, start_ref, *refs):
    out_ref = refs[-1]
    for i in range(count):
        at = slice(i * LANES, (i + 1) * LANES)
        out_ref[0, :, at] = refs[i][...].astype(bf16)
        out_ref[1, :, at] = refs[count + i][...].astype(bf16)
        out_ref[2, :, at] = refs[2 * count + i][...].T.astype(bf16)


def pack(w_gate, w_up, w_down, start, width):
    shard = w_gate.shape[0]
    count = width // LANES
    columns = [pl.BlockSpec((shard, LANES), lambda j, s, i=i: (0, s[0] + i)) for i in range(count)]
    lines = [pl.BlockSpec((LANES, shard), lambda j, s, i=i: (s[0] + i, 0)) for i in range(count)]
    spec = pltpu.PrefetchScalarGridSpec(
        num_scalar_prefetch=1,
        grid=(1,),
        in_specs=columns + columns + lines,
        out_specs=pl.BlockSpec((3, shard, width), lambda j, s: (0, 0, 0)),
    )
    return pl.pallas_call(
        functools.partial(pack_body, count),
        out_shape=jax.ShapeDtypeStruct((3, shard, width), bf16),
        grid_spec=spec,
        cost_estimate=cost(),
        compiler_params=params(60),
    )(start, *[w_gate] * count, *[w_up] * count, *[w_down] * count)


def qkv_pack_body(index_ref, g1_ref, g2_ref, bq_ref, bk_ref, bv_ref, wq_ref, wk_ref, wv_ref, out_ref):
    shard, at = wq_ref.shape[0], 0
    for ref in (wq_ref, wk_ref, wv_ref):
        out_ref[:shard, at : at + ref.shape[1]] = ref[...].astype(bf16)
        at += ref.shape[1]
    row = lax.broadcasted_iota(jnp.int32, (16, shard), 0)
    first, second = g1_ref[...][None, :], g2_ref[...][None, :]
    gains = jnp.where(row == 0, first, jnp.where(row == 1, second, 0.0))
    columns = bq_ref.shape[1]
    from_column = lax.broadcasted_iota(jnp.int32, (columns, HD), 0)
    to_column = lax.broadcasted_iota(jnp.int32, (columns, HD), 1)
    spread = (to_column == from_column + columns * index_ref[0]).astype(bf16)
    biases, at = 0.0, 8
    for ref in (bq_ref, bk_ref, bv_ref):
        heads = ref.shape[0]
        to_row = lax.broadcasted_iota(jnp.int32, (16, heads), 0)
        from_row = lax.broadcasted_iota(jnp.int32, (16, heads), 1) + at
        wide = dot_plain(ref[...].astype(bf16), spread).astype(bf16)
        if heads == 1:
            row = lax.broadcasted_iota(jnp.int32, (16, HD), 0)
            biases = biases + jnp.where(row == at, wide.astype(f32), 0.0)
        else:
            biases = biases + dot_plain((to_row == from_row).astype(bf16), wide)
        at += heads
    out_ref[shard:, :] = jnp.zeros((16, out_ref.shape[1]), bf16)
    out_ref[shard:, :HD] = (gains[:, :HD] + biases).astype(bf16)
    out_ref[shard:, HD:shard] = gains[:, HD:].astype(bf16)


def qkv_pack(index, g1, g2, b_q, b_k, b_v, w_q, w_k, w_v):
    width = w_q.shape[1] + w_k.shape[1] + w_v.shape[1]
    inputs = (g1, g2, b_q, b_k, b_v, w_q, w_k, w_v)
    return pl.pallas_call(
        qkv_pack_body,
        out_shape=jax.ShapeDtypeStruct((w_q.shape[0] + 16, width), bf16),
        in_specs=[pl.BlockSpec(memory_space=pltpu.SMEM)] + [pl.BlockSpec(memory_space=pltpu.VMEM)] * len(inputs),
        cost_estimate=cost(2),
        compiler_params=params(60),
    )(index, *inputs)


def vectors_body(count, heads, index_ref, *refs):
    gain_ref, bias_ref = refs[count:]
    width = D // count
    gain_ref[...] = joined(refs[:count], index_ref, 1, (slice(0, 2), slice(0, width)))
    bias_ref[...] = sum(r[8 : 8 + heads, :HD].astype(f32) for r in refs[:count])


def vectors(index, pieces, heads):
    shard = D // len(pieces)
    if shard % LANES:
        order = fsdp_order(len(pieces))
        blocks = [pieces[order.index(i)][shard : shard + 2, :shard] for i in range(len(pieces))]
        gains = jnp.concatenate(xor_blocks(blocks, index[0], len(pieces)), axis=1)
        return gains, sum(p[shard + 8 : shard + 8 + heads, :HD].astype(f32) for p in pieces)
    rows = pl.BlockSpec((16, pieces[0].shape[1]), lambda i: (shard // 16, 0))
    outs = (jax.ShapeDtypeStruct((2, D), bf16), jax.ShapeDtypeStruct((heads, HD), f32))
    return pl.pallas_call(
        functools.partial(vectors_body, len(pieces), heads),
        out_shape=outs,
        grid=(1,),
        in_specs=[pl.BlockSpec(memory_space=pltpu.SMEM)] + [rows] * len(pieces),
        out_specs=tuple(whole(a) for a in outs),
        cost_estimate=cost(),
        compiler_params=params(60),
    )(index, *pieces)


def project_body(count, q_width, index_ref, a_ref, b_ref, gain_ref, bias_ref, cos_ref, sin_ref, *refs):
    w_refs, (q_ref, kv_ref, h_ref) = refs[:count], refs[count:]
    x = jnp.concatenate([a_ref[...], b_ref[...]], axis=0).astype(f32)
    scale = lax.rsqrt(jnp.mean(x * x, axis=-1, keepdims=True) + epsilon)
    normed = (x * scale * gain_ref[0:1].astype(f32)).astype(bf16)
    h_ref[...] = normed
    total = w_refs[0].shape[1]
    depth = D // count
    for at in range(0, total, WIDE):
        weights = joined(w_refs, index_ref, 0, (slice(0, depth), slice(at, at + WIDE)))
        both = dot_plain(normed, weights)
        for inner in range(0, WIDE, HD):
            place = at + inner
            head = place // HD
            values = both[:, inner : inner + HD] + bias_ref[head : head + 1]
            if place < total - HD:
                turned = pltpu.roll(values, HD // 2, 1)
                values = values * cos_ref[...] + turned * sin_ref[...]
            if place < q_width:
                q_ref[:, place : place + HD] = values.astype(bf16)
            else:
                kv_ref[:, place - q_width : place - q_width + HD] = values.astype(bf16)


def project(index, first, second, gain, bias, cos_table, sin_table, weights, q_width):
    rows = 2 * first.shape[0]
    total = weights[0].shape[1]
    return pl.pallas_call(
        functools.partial(project_body, len(weights), q_width),
        out_shape=(
            jax.ShapeDtypeStruct((rows, q_width), bf16),
            jax.ShapeDtypeStruct((rows, total - q_width), bf16),
            jax.ShapeDtypeStruct((rows, D), bf16),
        ),
        in_specs=[pl.BlockSpec(memory_space=pltpu.SMEM)] + [pl.BlockSpec(memory_space=pltpu.VMEM)] * (6 + len(weights)),
        cost_estimate=cost(4),
        compiler_params=params(60),
    )(index, first, second, gain, bias, cos_table, sin_table, *weights)


def masked_weights(queries, keys, low_ref, high_ref, key_ref):
    scores = dot_cols(queries, keys) * HD ** (-0.5)
    key_at = key_ref[...]
    allowed = (key_at >= low_ref[...]) & (key_at <= high_ref[...])
    scores = jnp.where(allowed, scores, neg_big)
    top = jnp.max(scores, axis=-1, keepdims=True)
    raised = jnp.exp(scores - top)
    return raised * (1.0 / jnp.sum(raised, axis=-1, keepdims=True))


def attend_body(count, ahead, index_ref, q_ref, low_ref, high_ref, key_ref, *refs):
    w_refs, kv_refs = refs[:count], refs[count : count + ahead]
    o_ref, mine_ref, other_ref = refs[count + ahead :]
    keys = jnp.concatenate([kv[:, :HD] for kv in kv_refs], axis=0)
    values = jnp.concatenate([kv[:, HD:] for kv in kv_refs], axis=0)
    weights = masked_weights(q_ref[...], keys, low_ref, high_ref, key_ref)
    head = pl.program_id(0)
    out = dot_plain(weights.astype(bf16), values).astype(bf16)
    o_ref[:, pl.ds(pl.multiple_of(head * HD, HD), HD)] = out

    @pl.when(head == pl.num_programs(0) - 1)
    def _():
        half = mine_ref.shape[0]
        out_w = joined(w_refs, index_ref, 1)
        branch = dot_plain(o_ref[...], out_w)
        mine_ref[...] = branch[:half]
        other_ref[...] = branch[half:].astype(bf16)


def attend(index, queries, low, high, key_at, weights, kv_parts):
    rows, width = queries.shape
    head = pl.BlockSpec((rows, HD), lambda h: (0, h))
    keys = key_at.shape[1]
    rest = (low, high, key_at, *weights, *kv_parts)
    outs = (
        jax.ShapeDtypeStruct(queries.shape, bf16),
        jax.ShapeDtypeStruct((rows // 2, D), f32),
        jax.ShapeDtypeStruct((rows // 2, D), bf16),
    )
    return pl.pallas_call(
        functools.partial(attend_body, len(weights), len(kv_parts)),
        out_shape=outs,
        grid=(width // HD,),
        in_specs=[pl.BlockSpec(memory_space=pltpu.SMEM), head] + [whole(a) for a in rest],
        out_specs=tuple(whole(a) for a in outs),
        compiler_params=params(60),
        cost_estimate=cost(8),
    )(index, queries, *rest)


def middle_body(x_ref, mine_ref, other_ref, gain_ref, mid_ref, h_ref):
    middle = x_ref[...].astype(f32) + mine_ref[...] + other_ref[...].astype(f32)
    scale = lax.rsqrt(jnp.mean(middle * middle, axis=-1, keepdims=True) + epsilon)
    mid_ref[...] = middle
    h_ref[...] = (middle * scale * gain_ref[1:2].astype(f32)).astype(bf16)


def middle_norm(x, mine, other, gain):
    return pl.pallas_call(
        middle_body,
        out_shape=(jax.ShapeDtypeStruct(mine.shape, f32), jax.ShapeDtypeStruct(mine.shape, bf16)),
        cost_estimate=cost(),
        compiler_params=params(60),
    )(x, mine, other, gain)


def feed_body(
    count, bases, back, carried, last, filled, at_row, limit_ref, ctx_ref, *refs
):
    h_refs, refs = refs[: 2 * len(bases)], refs[2 * len(bases) :]
    (g_own, g_across, w_hbm), refs = refs[:3], refs[3:]
    carry, refs = refs[: 2 * carried], refs[2 * carried + filled :]
    bufs = None
    if carried:
        outs, (w_ref, act_ref, sems, bufs) = refs[:-4], refs[-4:]
    else:
        outs, (w_ref, act_ref, sems) = refs[:-3], refs[-3:]
    rows, width = act_ref.shape[1:]
    tiles = 3
    loads = [
        pltpu.make_async_copy(w_hbm.at[:, k], w_ref.at[:, k], sems.at[k]) for k in range(tiles)
    ]
    carries = [
        pltpu.make_async_copy(ref, bufs.at[k], sems.at[tiles + k]) for k, ref in enumerate(carry)
    ]
    for copy in loads + carries:
        copy.start()
    half = g_own.shape[1]
    chunk = 2 * half
    lane = lax.broadcasted_iota(jnp.int32, (1, width), 1)
    shown = lane >= limit_ref[0]

    def weights(k):
        return jnp.concatenate([w_ref[i, k] for i in range(count)], axis=0)

    at = 0
    for which, h_ref in enumerate(h_refs):
        base, g_ref = bases[which // 2], (g_own, g_across)[which % 2]
        for j in range(h_ref.shape[0] // chunk):
            rows_in = h_ref[j * chunk : (j + 1) * chunk]
            grads_in = jnp.concatenate(
                [g_ref[ctx_ref[0] ^ (base + 2 * j + k)] for k in range(2)], axis=0
            )
            if at == 0:
                loads[0].wait()
            gate = dot_plain(rows_in, weights(0))
            if at == 0:
                loads[1].wait()
            up = dot_plain(rows_in, weights(1))
            if at == 0:
                loads[2].wait()
            d_hidden = dot_plain(grads_in, weights(2))
            gate_sig = jax.nn.sigmoid(gate)
            activated = gate * gate_sig
            hidden = activated * up
            d_gate = d_hidden * up * gate_sig * (1.0 + gate * (1.0 - gate_sig))
            d_up = d_hidden * activated
            act_ref[0, at : at + chunk] = jnp.where(shown, d_gate, 0.0).astype(bf16)
            act_ref[1, at : at + chunk] = jnp.where(shown, d_up, 0.0).astype(bf16)
            act_ref[2, at : at + chunk] = jnp.where(shown, hidden, 0.0).astype(bf16)
            at += chunk
    at = tiles + len(carries)
    copies = [
        pltpu.make_async_copy(act_ref.at[k], outs[k].at[pl.ds(at_row, rows)], sems.at[at + k])
        for k in range(3)
    ]
    for copy in copies:
        copy.start()
    if back:
        team = slice(0, 4 * half)
        d_rows = dot_cols(act_ref[0, team], weights(0)) + dot_cols(act_ref[1, team], weights(1))
        out_rows = dot_cols(act_ref[2, team], weights(2))
        for copy in carries:
            copy.wait()
        if carried:
            d_rows = d_rows + bufs[0]
            out_rows = out_rows + bufs[1]
        if last:
            cuts = ((0, half), (half, 2 * half), (2 * half, 4 * half))
            for group, total in ((outs[3:6], d_rows), (outs[6:], out_rows)):
                for ref, (low, high) in zip(group, cuts):
                    ref[...] = total[low:high].astype(ref.dtype)
        else:
            outs[3][...] = d_rows
            outs[4][...] = out_rows
    for copy in copies:
        copy.wait()


def feed(limit, ctx, rows_in, grads_in, weights, total, back, carry=(), last=False, act=None):
    some = sum(r.shape[0] for r in rows_in)
    width = weights.shape[3]
    outs = [jax.ShapeDtypeStruct((total, width), bf16)] * 3
    half = grads_in[0].shape[1]
    if back and last:
        group = [jax.ShapeDtypeStruct((half, D), f32)] * 2
        outs += (group + [jax.ShapeDtypeStruct((2 * half, D), bf16)]) * 2
    elif back:
        outs += [jax.ShapeDtypeStruct((4 * half, D), f32)] * 2
    vmem = pl.BlockSpec(memory_space=pltpu.VMEM)
    smem = pl.BlockSpec(memory_space=pltpu.SMEM)
    hbm = pl.BlockSpec(memory_space=pl.ANY)
    inputs = (*rows_in, *grads_in)
    filled = () if act is None else tuple(act)
    scratch = [
        pltpu.VMEM(weights.shape, bf16),
        pltpu.VMEM((3, some, width), bf16),
        pltpu.SemaphoreType.DMA((6 + len(carry),)),
    ]
    if carry:
        scratch.append(pltpu.VMEM((2, 4 * half, D), f32))
    first = 3 + len(inputs) + len(carry)
    return pl.pallas_call(
        functools.partial(
            feed_body, weights.shape[0],
            ((0,) if back else ()) + ((TEAM,) if some == total or not back else ()),
            back, len(carry) // 2, last, len(filled), 0 if back else total - some,
        ),
        out_shape=tuple(outs),
        in_specs=[smem, smem] + [vmem] * len(inputs) + [hbm] * (1 + len(carry) + len(filled)),
        out_specs=tuple([hbm] * 3 + [vmem] * (len(outs) - 3)),
        scratch_shapes=scratch,
        input_output_aliases={first + k: k for k in range(len(filled))},
        compiler_params=params(60),
        cost_estimate=cost((6 if back else 0) + 9 * some / 512),
    )(limit, ctx, *inputs, weights, *carry, *filled)


def turn_body(blocks, dynamic, contexts, index_ref, ctx_ref, *refs):
    kept_ref, sent_ref = refs[-2:]
    width = D // blocks
    order = fsdp_order(blocks)
    values = [(ref, None) for ref in refs[:-2]]
    if contexts:
        groups = (range(TEAM), range(TEAM, contexts))
        values = [(ref, ctx_ref[0] ^ k) for group in groups for ref in refs[:-2] for k in group]
    at = 0
    for ref, which in values:
        value = ref[...] if which is None else ref[which]
        here = slice(at, at + value.shape[0])
        at += value.shape[0]
        parts = [value[:, i * width : (i + 1) * width] for i in range(blocks)]
        if dynamic:
            parts = xor_blocks(parts, index_ref[0], blocks)
            parts = [parts[i] for i in order]
        for spot in range(blocks // 2):
            lines_at = slice(spot * width, (spot + 1) * width)
            kept_ref[lines_at, here] = parts[spot].T
            sent_ref[lines_at, here] = parts[blocks // 2 + spot].T


def turn_rows(index, ctx, rows, n_fsdp):
    total = sum(r.size for r in rows) // D
    contexts = rows[0].shape[0] if rows[0].ndim == 3 else 0
    blocks = n_fsdp
    if D // n_fsdp % LANES:
        blocks = 2
        rows = [to_relative(v, index[0], n_fsdp) for v in rows]
    return pl.pallas_call(
        functools.partial(turn_body, blocks, blocks == n_fsdp, contexts),
        out_shape=(jax.ShapeDtypeStruct((D // 2, total), bf16),) * 2,
        in_specs=[pl.BlockSpec(memory_space=pltpu.SMEM), pl.BlockSpec(memory_space=pltpu.SMEM)] + [pl.BlockSpec(memory_space=pltpu.VMEM)] * len(rows),
        cost_estimate=cost(4),
        compiler_params=params(60),
    )(index, ctx, *rows)


def weight_body(*refs):
    own, beside, acts = refs[:2], refs[2:4], refs[4:7]
    acts_beside, (near_ref, far_ref) = refs[7:10], refs[10:]
    cut = near_ref.shape[1]
    for k in range(3):
        value = dot_plain(own[k // 2][...], acts[k][...])
        value = value + dot_plain(beside[k // 2][...], acts_beside[k][...])
        near_ref[k] = value[:cut].astype(bf16)
        far_ref[k] = value[cut:].astype(bf16)


def weight_grads(own, beside, acts, acts_beside):
    total, width = acts[0].shape
    left = pl.BlockSpec(own[0].shape, lambda j: (0, 0), pipeline_mode=pl.Buffered(1))
    right = pl.BlockSpec((total, WIDE), lambda j: (0, j))
    out = pl.BlockSpec((3, D // 4, WIDE), lambda j: (0, 0, j))
    return pl.pallas_call(
        weight_body,
        out_shape=(jax.ShapeDtypeStruct((3, D // 4, width), bf16),) * 2,
        grid=(width // WIDE,),
        in_specs=[left] * 4 + [right] * 6,
        out_specs=(out, out),
        compiler_params=params(60),
        cost_estimate=cost(12),
    )(*own, *beside, *acts, *acts_beside)


def middle_back_body(
    near_ref, across_ref, far_ref, mid_ref, gain_ref, g_ref, d_ref, low_ref, gain_out
):
    d_normed = near_ref[...] + across_ref[...].astype(f32) + far_ref[...].astype(f32)
    middle = mid_ref[...]
    scale = lax.rsqrt(jnp.mean(middle * middle, axis=-1, keepdims=True) + epsilon)
    gain_out[...] = jnp.sum(d_normed * middle * scale, axis=0, keepdims=True)
    weighted = d_normed * gain_ref[1:2].astype(f32)
    inner = jnp.mean(weighted * middle, axis=-1, keepdims=True)
    d_middle = g_ref[...].astype(f32) + scale * weighted - middle * scale**3 * inner
    d_ref[...] = d_middle
    low_ref[...] = d_middle.astype(bf16)


def middle_back(near, across, far, middle, gain, grads):
    return pl.pallas_call(
        middle_back_body,
        out_shape=(
            jax.ShapeDtypeStruct(near.shape, f32),
            jax.ShapeDtypeStruct(near.shape, bf16),
            jax.ShapeDtypeStruct((1, D), f32),
        ),
        cost_estimate=cost(),
        compiler_params=params(60),
    )(near, across, far, middle, gain, grads)


def attend_back_body(count, ahead, index_ref, q_ref, low_ref, high_ref, key_ref, cos_ref, sin_ref, *refs):
    scale = HD ** (-0.5)
    mine_ref, other_ref = refs[:2]
    w_refs, kv_refs = refs[2 : 2 + count], refs[2 + count : 2 + count + ahead]
    outs = refs[2 + count + ahead :]
    dq_ref, dkv_refs, (d_o, sums) = outs[0], outs[1 : 1 + ahead], outs[1 + ahead :]
    head = pl.program_id(0)

    @pl.when(head == 0)
    def _():
        d_branch = jnp.concatenate([mine_ref[...], other_ref[...]], axis=0)
        out_w = joined(w_refs, index_ref, 1)
        d_o[...] = dot_cols(d_branch, out_w).astype(bf16)
        sums[...] = jnp.zeros_like(sums)

    queries = q_ref[...]
    grad = d_o[:, pl.ds(pl.multiple_of(head * HD, HD), HD)]
    keys = jnp.concatenate([kv[:, :HD] for kv in kv_refs], axis=0)
    values = jnp.concatenate([kv[:, HD:] for kv in kv_refs], axis=0)
    weights = masked_weights(queries, keys, low_ref, high_ref, key_ref)
    dweights = dot_cols(grad, values)
    delta = jnp.sum(weights * dweights, axis=-1, keepdims=True)
    dscores = (weights * (dweights - delta)).astype(bf16)
    dq_rot = dot_plain(dscores, keys) * scale
    turned = pltpu.roll(dq_rot, HD // 2, 1)
    dq_ref[...] = (dq_rot * cos_ref[...] - turned * sin_ref[...]).astype(bf16)
    sums[:, :HD] += dot_rows(dscores, queries) * scale
    sums[:, HD:] += dot_rows(weights.astype(bf16), grad)

    @pl.when(head == pl.num_programs(0) - 1)
    def _():
        rows = q_ref.shape[0]
        for i, out in enumerate(dkv_refs):
            out[...] = sums[i * rows : (i + 1) * rows].astype(out.dtype)


def attend_back(index, queries, low, high, key_at, cos_table, sin_table, grads, weights, kv_parts):
    rows, width = queries.shape
    head = pl.BlockSpec((rows, HD), lambda h: (0, h))
    keys = key_at.shape[1]
    rest = (low, high, key_at, cos_table, sin_table, *grads, *weights, *kv_parts)
    outs = [jax.ShapeDtypeStruct(queries.shape, bf16)]
    outs += [
        jax.ShapeDtypeStruct(kv.shape, bf16 if i else f32) for i, kv in enumerate(kv_parts)
    ]
    return pl.pallas_call(
        functools.partial(attend_back_body, len(weights), len(kv_parts)),
        out_shape=tuple(outs),
        grid=(width // HD,),
        in_specs=[pl.BlockSpec(memory_space=pltpu.SMEM), head] + [whole(a) for a in rest],
        out_specs=tuple([head] + [whole(a) for a in outs[1:]]),
        scratch_shapes=[pltpu.VMEM((rows, width), bf16), pltpu.VMEM((keys, 2 * HD), f32)],
        compiler_params=params(60),
        cost_estimate=cost(10),
    )(index, queries, *rest)


def project_back_body(count, ahead, index_ref, dq_ref, cos_ref, sin_ref, *refs):
    w_refs, dkv_refs = refs[:count], refs[count : count + ahead]
    d_ref, mine_ref, other_ref, bias_ref = refs[count + ahead :]
    total = dkv_refs[0][...]
    for extra in dkv_refs[1:]:
        total = total + extra[...].astype(f32)
    dk = total[:, :HD]
    dk = dk * cos_ref[...] - pltpu.roll(dk, HD // 2, 1) * sin_ref[...]
    d_low = jnp.concatenate([dq_ref[...], dk.astype(bf16), total[:, HD:].astype(bf16)], axis=1)
    d_ref[...] = d_low
    bias_ref[...] = jnp.sum(d_low.astype(f32), axis=0, keepdims=True)
    weights = joined(w_refs, index_ref, 0, slice(0, D // count))
    d_normed = dot_cols(d_low, weights)
    half = mine_ref.shape[0]
    mine_ref[...] = d_normed[:half]
    other_ref[...] = d_normed[half:].astype(bf16)


def project_back(index, dq, cos_table, sin_table, weights, dkv_parts):
    rows = dq.shape[0]
    total = weights[0].shape[1]
    return pl.pallas_call(
        functools.partial(project_back_body, len(weights), len(dkv_parts)),
        out_shape=(
            jax.ShapeDtypeStruct((rows, total), bf16),
            jax.ShapeDtypeStruct((rows // 2, D), f32),
            jax.ShapeDtypeStruct((rows // 2, D), bf16),
            jax.ShapeDtypeStruct((1, total), f32),
        ),
        in_specs=[pl.BlockSpec(memory_space=pltpu.SMEM)] + [pl.BlockSpec(memory_space=pltpu.VMEM)] * (3 + len(weights) + len(dkv_parts)),
        cost_estimate=cost(4),
        compiler_params=params(60),
    )(index, dq, cos_table, sin_table, *weights, *dkv_parts)


def input_back_body(mine_ref, other_ref, x_ref, gain_ref, mid_ref, d_ref, gain_out):
    d_normed = mine_ref[...] + other_ref[...].astype(f32)
    x = x_ref[...].astype(f32)
    scale = lax.rsqrt(jnp.mean(x * x, axis=-1, keepdims=True) + epsilon)
    gain_out[...] = jnp.sum(d_normed * x * scale, axis=0, keepdims=True)
    weighted = d_normed * gain_ref[0:1].astype(f32)
    inner = jnp.mean(weighted * x, axis=-1, keepdims=True)
    d_ref[...] = (mid_ref[...] + scale * weighted - x * scale**3 * inner).astype(bf16)


def input_back(mine, other, x, gain, d_middle):
    return pl.pallas_call(
        input_back_body,
        out_shape=(jax.ShapeDtypeStruct(mine.shape, bf16), jax.ShapeDtypeStruct((1, D), f32)),
        cost_estimate=cost(),
        compiler_params=params(60),
    )(mine, other, x, gain, d_middle)


def place_body(plan, carried, member_ref, *refs):
    own_ref, other_ref, refs = refs[0], refs[1], refs[2:]
    outs = refs[carried : carried + 3]
    wide_buf, tall_buf, sems = refs[carried + 3 :]
    width = own_ref.shape[2]

    def copies(team):
        skip, at = plan[team]
        size = width - skip
        for k in range(2):
            yield pltpu.make_async_copy(
                wide_buf.at[team, k, :, pl.ds(skip, size)],
                outs[k].at[:, pl.ds(at + skip, size)],
                sems.at[team, k],
            )
        yield pltpu.make_async_copy(
            tall_buf.at[team, pl.ds(skip, size)],
            outs[2].at[pl.ds(at + skip, size)],
            sems.at[team, 2],
        )

    for team in range(len(plan)):
        def put(ref, team=team):
            wide_buf[team, 0] = ref[0].astype(f32)
            wide_buf[team, 1] = ref[1].astype(f32)
            tall_buf[team] = ref[2].astype(f32).T

        @pl.when(member_ref[0] == team)
        def _():
            put(own_ref)

        @pl.when(member_ref[0] != team)
        def _():
            put(other_ref)

        for copy in copies(team):
            copy.start()
    for team in range(len(plan)):
        for copy in copies(team):
            copy.wait()


def place(member, own, other, index, starts, fresh, ff_local, carry):
    shard, width = own.shape[1:]
    plan = tuple(
        (min(max(fresh[s] - index * width, 0), width), starts[s] + index * width)
        for s in range(TEAM)
    )
    hbm = pl.BlockSpec(memory_space=pl.ANY)
    vmem = pl.BlockSpec(memory_space=pltpu.VMEM)
    return pl.pallas_call(
        functools.partial(place_body, plan, len(carry)),
        out_shape=(
            jax.ShapeDtypeStruct((shard, ff_local), f32),
            jax.ShapeDtypeStruct((shard, ff_local), f32),
            jax.ShapeDtypeStruct((ff_local, shard), f32),
        ),
        in_specs=[pl.BlockSpec(memory_space=pltpu.SMEM)] + [vmem] * 2 + [hbm] * len(carry),
        out_specs=(hbm, hbm, hbm),
        scratch_shapes=[
            pltpu.VMEM((TEAM, 2, shard, width), f32),
            pltpu.VMEM((TEAM, width, shard), f32),
            pltpu.SemaphoreType.DMA((TEAM, 3)),
        ],
        input_output_aliases={3 + i: i for i in range(len(carry))},
        cost_estimate=cost(),
        compiler_params=params(60),
    )(member, own, other, *carry)


def after(values, *first):
    return lax.optimization_barrier((values, first))[0]


class Order:
    def __init__(self):
        self.last = ()

    def __call__(self, step, *args):
        args, _ = lax.optimization_barrier((args, self.last))
        result = step(*args)
        self.last = (jax.tree.leaves(result)[0],)
        return result

    def pin(self, values):
        values, _ = lax.optimization_barrier((values, self.last))
        self.last = (jax.tree.leaves(values)[0],)
        return values


def stack(*pieces):
    return jnp.concatenate(pieces, axis=0)


class Pieces:
    def __init__(self, run, full, *first):
        bits = list(reversed(bits_of(lax.axis_size("fsdp"))))
        self.run, self.near = run, bits[-1]
        self.held = [full]
        gate = after(full, *first)
        for bit in bits[:-1]:
            self.held = self.held + [swap(p, "fsdp", bit) for p in [gate] + self.held[1:]]

    def turn(self):
        self.held = self.held[:1] + list(self.run.pin(tuple(self.held[1:])))
        self.sent = swap(self.run(lambda *a: jnp.stack(a), *self.held), "fsdp", self.near)
        return self.held[-1]

    def finish(self):
        self.sent = self.run.pin(self.sent)

    def pieces(self):
        return self.held + [self.sent[i] for i in range(len(self.held))]


def per_device(
    tokens,
    cotangent,
    lengths,
    span_order,
    attn_gain,
    w_q,
    b_q,
    w_k,
    b_k,
    w_v,
    b_v,
    w_o,
    mlp_gain,
    w_gate,
    w_up,
    w_down,
):
    n_fsdp = lax.axis_size("fsdp")
    n_ctx = lax.axis_size("context")
    my_fsdp = lax.axis_index("fsdp")
    my_ctx = lax.axis_index("context")
    my_tensor = lax.axis_index("tensor")
    member = my_ctx % TEAM
    rows = tokens.shape[0]
    half = rows // 2
    piece_rows = rows // n_ctx
    shard = D // n_fsdp
    q_width = w_q.shape[1]
    kv_width = w_k.shape[1]
    qkv_width = q_width + 2 * kv_width
    heads_local = q_width // HD
    all_heads = qkv_width // HD
    flipped = my_tensor != 0
    run = Order()
    sharing = n_fsdp == 4 and n_ctx % 2 == 0

    def mine_first(values):
        first, second = values[:half], values[half:]
        return stack(jnp.where(flipped, second, first), jnp.where(flipped, first, second))

    bias_cols = HD // n_fsdp

    index = my_fsdp.astype(jnp.int32).reshape(1)
    qkv_h = Pieces(
        run, run(qkv_pack, index, attn_gain, mlp_gain, b_q, b_k, b_v, w_q, w_k, w_v)
    )
    out_cast = run(lambda w: w.astype(bf16), w_o)

    def arrange(values):
        both = mine_first(values)
        return both[:half], both[half:]

    class Rows:
        def __init__(self, mine):
            self.mine = mine
            self.beside = swap(mine, "context", 1)

        def turn(self):
            self.beside = run.pin(self.beside)
            self.held = run(stack, self.mine, self.beside)
            self.held_across = swap(self.held, "tensor", 1)
            held, others = self.held, []
            for bit in bits_of(n_ctx)[1:]:
                there = swap(held, "context", bit)
                others.append(there)
                held = stack(held, there)
            self.remote = others[0] if len(others) == 1 else stack(*others)

        def across_rest(self):
            self.remote = run.pin(self.remote)
            self.remote_across = swap(self.remote, "tensor", 1)

        def pin_team(self):
            self.held_across = run.pin(self.held_across)

        def pin_rest(self):
            self.remote_across = run.pin(self.remote_across)

        def team(self):
            return (self.held, self.held_across)

        def rest(self):
            return (self.remote, self.remote_across)

    grad_mine, _ = run(arrange, cotangent)
    grads_own = lax.all_gather(grad_mine, "context")

    ff_local = w_gate.shape[1]
    tiles = ff_local // LANES
    unit = PARTS * WIDE // LANES
    slice_tiles = -(-tiles // (TEAM * unit)) * unit
    part = slice_tiles // PARTS * LANES
    starts = [min(s * slice_tiles, tiles - slice_tiles) * LANES for s in range(TEAM)]
    fresh = [s * slice_tiles * LANES - starts[s] for s in range(TEAM)]
    my_start = jnp.int32(starts[0] // LANES)
    limit = jnp.int32(fresh[0])
    for s in range(1, TEAM):
        my_start = jnp.where(member == s, starts[s] // LANES, my_start)
        limit = jnp.where(member == s, fresh[s], limit)

    def packed(index):
        start = (my_start + index * (part // LANES)).reshape(1)
        return run(lambda *a: pack(*a, part), w_gate, w_up, w_down, start)

    longest = 3 * n_ctx * rows // 8
    behind = min(n_ctx - 1, (longest - 1 + rows - 1) // rows)
    half_dim = HD // 2

    def places(lengths, span_order):
        seq_ends = jnp.cumsum(lengths[0])
        row = jnp.arange(rows, dtype=jnp.int32)
        stored = jnp.where(flipped, (row + half) % rows, row)

        def packed_of(context):
            owner = lax.dynamic_index_in_dim(span_order[0], context, 0, keepdims=False)
            span = stored // piece_rows
            hot = span[:, None] == jnp.arange(n_ctx, dtype=jnp.int32)[None, :]
            spot = jnp.sum(jnp.where(hot, owner[None, :], 0), axis=1)
            return context * rows + spot * piece_rows + stored % piece_rows

        own_at = packed_of(my_ctx)
        passed = own_at[:, None] >= seq_ends[None, :]
        begin = jnp.max(jnp.where(passed, seq_ends[None, :], 0), axis=1)
        position = own_at - begin
        key_at = [own_at]
        for step in range(1, behind + 1):
            there = packed_of(jnp.maximum(my_ctx - step, 0))
            key_at.append(jnp.where(my_ctx >= step, there, far_away))
        frequency = rope_base ** (-(jnp.arange(half_dim, dtype=f32) * 2.0) / HD)
        angles = position.astype(f32)[:, None] * frequency[None, :]
        cosine, sine = jnp.cos(angles), jnp.sin(angles)
        return (
            begin[:, None],
            own_at[:, None],
            jnp.concatenate(key_at)[None, :],
            jnp.concatenate([cosine, cosine], axis=1),
            jnp.concatenate([-sine, sine], axis=1),
        )

    ctx = my_ctx.astype(jnp.int32).reshape(1)
    feed_in = [packed(0)]
    mine_tokens, other_tokens = run(arrange, tokens)
    feed_in.append(packed(1))
    far = qkv_h.turn()
    out_h = Pieces(run, out_cast, far)
    feed_in += [packed(i) for i in range(2, PARTS)]
    feed_w = [lax.all_gather(after(v, far), "fsdp") for v in feed_in]
    low, high, key_at, cos_table, sin_table = run(places, lengths, span_order)
    qkv_h.finish()

    def in_order(pieces, axis, cut=None):
        if shard % LANES == 0:
            return pieces
        order = fsdp_order(n_fsdp)
        blocks = [pieces[order.index(i)] for i in range(n_fsdp)]
        blocks = [b if cut is None else b[:cut] for b in blocks]
        return [jnp.concatenate(xor_blocks(blocks, my_fsdp, n_fsdp), axis=axis)]

    gains, bias = run(lambda i, p: vectors(i, p, all_heads), index, qkv_h.pieces())
    qkv_w = in_order(qkv_h.pieces(), 0, shard)

    queries, kv_own, normed = run(
        lambda *a: project(*a, q_width),
        index, mine_tokens, other_tokens, gains, bias, cos_table, sin_table, qkv_w,
    )
    kv_parts = [kv_own] + [shift(kv_own, "context", step) for step in range(1, behind + 1)]
    grads_own = run.pin(grads_own)
    grads = (grads_own, swap(grads_own, "tensor", 1))
    normed_rel = run(lambda v: to_relative(v, my_fsdp, n_fsdp), normed)
    out_h.turn()
    kv_parts = [kv_own] + list(run.pin(tuple(kv_parts[1:])))
    out_h.finish()
    out_w = in_order(out_h.pieces(), 1)
    branch_mine, attended, branch_other = run(
        lambda *a: (lambda o, m, s: (m, o, s))(*attend(*a)),
        index, queries, low, high, key_at, out_w, kv_parts,
    )
    branch_other = swap(branch_other, "tensor", 1)
    sent = run(lambda a, b: jnp.concatenate([a, b[:, D // 2 :]], axis=1), attended, normed_rel)
    early_beside = swap(sent, "fsdp", 1)
    grads = run.pin(grads)
    middle, normed_two = run(
        middle_norm, mine_tokens, branch_mine, branch_other, gains
    )
    lines = Rows(normed_two)
    early_beside = run.pin(early_beside)
    attended_beside, normed_beside = early_beside[:, :q_width], early_beside[:, q_width:]
    lines.turn()
    lines.pin_team()

    limits = [limit.reshape(1)] + [jnp.zeros((1,), jnp.int32)] * (PARTS - 1)
    acts, acts_beside = {}, {}
    total_rows = n_ctx * rows

    def feed_team(index, carry, last=False, every=False):
        rows_in = lines.team() + lines.rest() if every else lines.team()
        results = run(
            lambda *a: feed(*a[:5], total_rows, True, a[5], last),
            limits[index], ctx, rows_in, grads, feed_w[index], carry,
        )
        acts[index] = tuple(results[:3])
        if every:
            acts_beside[index] = tuple(swap(a, "fsdp", 1) for a in acts[index])
        return tuple(results[3:])

    def feed_rest(index):
        acts[index] = run(
            lambda *a: feed(*a[:5], total_rows, False, act=a[5]),
            limits[index], ctx, lines.rest(), grads, feed_w[index], acts[index],
        )
        acts_beside[index] = tuple(swap(a, "fsdp", 1) for a in acts[index])

    waiting, reduced, other_parts = {}, {}, {}

    def grads_of(index):
        far, near = run(
            lambda *a: weight_grads(*a)[::-1],
            turned, turned_beside, acts[index], acts_beside[index],
        )
        bits = bits_of(n_fsdp)[1:]
        for bit in bits[:-1]:
            total = near.astype(f32) + swap(far, "fsdp", bit).astype(f32)
            cut = total.shape[1] // 2
            far, near = total[:, cut:].astype(bf16), total[:, :cut].astype(bf16)
        waiting[index] = (near, swap(far, "fsdp", bits[-1]))

    def give(near, arrived):
        return (near.astype(f32) + arrived.astype(f32)).astype(bf16)

    def add_far(index):
        reduced[index] = run(give, *waiting[index])
        other_parts[index] = swap(reduced[index], "context", 1)

    carry = feed_team(0, ())
    lines.across_rest()
    turned_grads, grads_sent = run(lambda *a: turn_rows(*a, n_fsdp), index, ctx, grads)
    grads_beside = swap(grads_sent, "fsdp", 1)
    carry = feed_team(1, carry)
    lines.pin_rest()
    turned_lines, lines_sent = run(
        lambda *a: turn_rows(*a, n_fsdp), index, ctx, lines.team() + lines.rest()
    )
    turned = (turned_lines, turned_grads)
    turned_beside = (swap(lines_sent, "fsdp", 1), grads_beside)
    feed_rest(0)
    feed_rest(1)
    grads_of(0)
    given = feed_team(2, carry, True)
    d_near, d_beside, d_far, out_near, out_beside, out_far = given
    d_far = swap(d_far, "tensor", 1)
    feed_rest(2)
    grads_of(1)
    d_beside = swap(run(lambda a, b: give(a, b[half:]), d_beside, d_far), "context", 1)
    add_far(0)
    d_middle, d_branch, grad_gain_two = run(
        lambda a, b, *c: middle_back(a, b[:half], *c),
        d_near, d_far, d_beside, middle, gains, grad_mine,
    )
    d_branch_other = swap(d_branch, "tensor", 1)
    grads_of(2)
    d_branch_other = run.pin(d_branch_other)
    d_all = run(lambda *a: to_relative(stack(*a), my_fsdp, n_fsdp), d_branch, d_branch_other)
    d_all_beside = swap(d_all[:, D // 2 :], "fsdp", 1)
    d_all_beside = run.pin(d_all_beside)
    dq_low, *dkv_parts = run(
        attend_back,
        index, queries, low, high, key_at, cos_table, sin_table,
        (d_branch, d_branch_other), out_w, kv_parts,
    )
    dkv_parts = [dkv_parts[0]] + [
        shift(p, "context", -step - 1) for step, p in enumerate(dkv_parts[1:])
    ]
    other_parts[0] = run.pin(other_parts[0])
    reduced[1] = run(give, *waiting[1])

    def halves(values, axis):
        cut = values.shape[axis] // 2
        return (
            lax.slice_in_dim(values, 0, cut, axis=axis),
            lax.slice_in_dim(values, cut, 2 * cut, axis=axis),
        )

    class Reduce:
        def __init__(self, axis, full, full_beside, split, split_beside):
            self.axis, self.other = axis, 1 - axis
            self.full, self.full_beside = full, full_beside
            self.kept, self.kept_beside = split[:, : D // 2], split_beside
            self.todo = [("fsdp", bit) for bit in bits_of(n_fsdp)[1:]]
            self.todo += [("context", bit) for bit in bits_of(n_ctx)]
            self.back = [bit for bit in reversed(bits_of(n_ctx))]
            self.value = None

        def cut(self, total):
            name, bit = self.todo[0]
            if name == "fsdp":
                keep, send = halves(total, self.axis)
                return keep, send.astype(bf16)
            first, second = halves(total, self.other)
            on = (my_ctx & bit) != 0
            return jnp.where(on, second, first), jnp.where(on, first, second).astype(bf16)

        def send(self, pair):
            name, bit = self.todo.pop(0)
            self.keep, sent = pair
            self.sent = swap(sent, name, bit)

        def first(self):
            def product(full, kept, full_beside, kept_beside):
                left, right = stack(kept, kept_beside), stack(full, full_beside)
                if self.axis == 1:
                    left, right = right, left
                return self.cut(dot_rows(left, right))

            self.send(run(product, self.full, self.kept, self.full_beside, self.kept_beside))

        def step(self):
            if self.todo:
                self.send(run(lambda a, b: self.cut(a + b.astype(f32)), self.keep, self.sent))
                return
            if self.value is None:
                self.value = run(give, self.keep, self.sent)
            else:
                self.value = self.join()
            self.bit = self.back.pop(0)
            self.sent = swap(self.value, "context", self.bit)

        def join(self):
            on = (my_ctx & self.bit) != 0

            def both(mine, other):
                return jnp.concatenate(
                    [jnp.where(on, other, mine), jnp.where(on, mine, other)], axis=self.other
                )

            return run(both, self.value, self.sent)

    def place_part(index, placed):
        return run(
            lambda m, a, b, c: place(m, a, b, index, starts, fresh, ff_local, c),
            member.reshape(1), reduced[index], other_parts[index], placed,
        )

    def smalls(gain_rows, gain_other, grad_bias):
        gain_rows = jnp.pad(gain_rows + gain_other, ((0, 6), (0, 0)))
        biases = jnp.pad(grad_bias.reshape(all_heads, HD), ((0, 0), (0, D - HD)))
        return stack(gain_rows, biases)

    steps = [("fsdp", bit) for bit in bits_of(n_fsdp)] + [("context", bit) for bit in bits_of(n_ctx)]

    def small_step(small):
        name, bit = steps.pop(0)
        return run(jnp.add, small, swap(small, name, bit))

    reduce_o = Reduce(1, attended, attended_beside, d_all, d_all_beside)
    reduce_o.first()
    dkv_parts = dkv_parts[:1] + list(run.pin(tuple(dkv_parts[1:])))
    other_parts[1] = swap(after(reduced[1], dkv_parts[-1]), "context", 1)
    d_qkv, dn_mine, dn_other, grad_bias = run(
        project_back, index, dq_low, cos_table, sin_table, qkv_w, dkv_parts
    )
    d_qkv_beside = swap(d_qkv, "fsdp", 1)
    dn_other = swap(dn_other, "tensor", 1)
    placed = place_part(0, ())
    reduce_qkv = Reduce(0, d_qkv, d_qkv_beside, normed_rel, normed_beside)
    reduce_qkv.first()
    d_inputs, grad_gain_one = run(
        input_back, dn_mine, dn_other, mine_tokens, gains, d_middle
    )
    d_inputs_other = swap(d_inputs, "tensor", 1)
    add_far(2)
    d_inputs_other = run.pin(d_inputs_other)
    other_parts[1] = run.pin(other_parts[1])
    reduce_o.step()
    gain_rows = run(stack, grad_gain_one, grad_gain_two)
    gain_other = swap(gain_rows, "tensor", 1)
    out_far = swap(after(out_far, other_parts[1]), "tensor", 1)
    reduce_qkv.step()
    small = run(smalls, gain_rows, gain_other, grad_bias)
    placed = place_part(1, placed)
    out_mine, out_beside = run(
        lambda a, b, c: (a + c[:half].astype(f32), give(b, c[half:])), out_near, out_beside, out_far
    )
    small = small_step(small)
    small = small_step(small)
    reduce_o.step()
    arrived = reduce_qkv.sent
    reduce_qkv.step()
    out_beside = swap(after(out_beside, arrived), "context", 1)
    other_parts[2] = run.pin(other_parts[2])
    reduce_o.step()
    reduce_qkv.step()
    small = small_step(small)
    reduce_o.step()
    out_half = run(
        lambda a, b, c: (a + b + c.astype(f32)).astype(bf16), middle, out_mine, out_beside
    )
    out_half_other = swap(out_half, "tensor", 1)
    reduce_qkv.step()
    small = small_step(small)
    placed = place_part(2, placed)
    while reduce_o.back:
        reduce_o.step()
        reduce_qkv.step()
    while steps:
        small = small_step(small)
    grad_gate, grad_up, grad_down = placed
    grad_o = reduce_o.join().astype(f32)
    grad_qkv = reduce_qkv.join().astype(f32)
    grad_biases = small[8 : 8 + all_heads, :bias_cols]
    small_gains = small[:2, :shard]
    for f in range(1, n_fsdp):
        there = small[8 : 8 + all_heads, f * bias_cols : (f + 1) * bias_cols]
        grad_biases = jnp.where(my_fsdp == f, there, grad_biases)
        small_gains = jnp.where(my_fsdp == f, small[:2, f * shard : (f + 1) * shard], small_gains)
    def restore(low_half, other_half):
        both = mine_first(stack(low_half, other_half))
        return both.astype(f32)

    return (
        restore(out_half, out_half_other),
        restore(d_inputs, d_inputs_other),
        small_gains[0],
        grad_qkv[:, :q_width],
        grad_biases[:heads_local],
        grad_qkv[:, q_width : q_width + kv_width],
        grad_biases[heads_local : heads_local + 1],
        grad_qkv[:, q_width + kv_width :],
        grad_biases[heads_local + 1 :],
        grad_o,
        small_gains[1],
        grad_gate,
        grad_up,
        grad_down,
    )


def solution(mesh):
    in_specs = (
        P(("fsdp", "context"), None),
        P(("fsdp", "context"), None),
        P("fsdp", None),
        P("fsdp", None, None),
        P("fsdp"),
        P("fsdp", "tensor"),
        P("tensor", "fsdp"),
        P("fsdp", "tensor"),
        P("tensor", "fsdp"),
        P("fsdp", "tensor"),
        P("tensor", "fsdp"),
        P("tensor", "fsdp"),
        P("fsdp"),
        P("fsdp", "tensor"),
        P("fsdp", "tensor"),
        P("tensor", "fsdp"),
    )
    out_specs = (
        P(("fsdp", "context"), None),
        P(("fsdp", "context"), None),
        P("fsdp"),
        P("fsdp", "tensor"),
        P("tensor", "fsdp"),
        P("fsdp", "tensor"),
        P("tensor", "fsdp"),
        P("fsdp", "tensor"),
        P("tensor", "fsdp"),
        P("tensor", "fsdp"),
        P("fsdp"),
        P("fsdp", "tensor"),
        P("fsdp", "tensor"),
        P("tensor", "fsdp"),
    )
    return jax.shard_map(
        per_device, mesh=mesh, in_specs=in_specs, out_specs=out_specs, check_vma=False
    )
```

```python
import functools

import jax
import jax.numpy as jnp
from jax import lax
from jax.experimental import pallas as pl
from jax.experimental.pallas import tpu as pltpu
from jax.sharding import PartitionSpec as P

D = 1536
HD = 128
LANES = 128
TEAM = 2
PARTS = 3
WIDE = 256
SHARED_PARTS = 1

epsilon = 1e-06
rope_base = 10000.0
neg_big = -1e30
far_away = 1 << 29
bf16 = jnp.bfloat16
f32 = jnp.float32


def dot_plain(left_op, right_op):
    return jnp.dot(left_op, right_op, preferred_element_type=f32)


def dot_rows(left_op, right_op):
    return lax.dot_general(
        left_op, right_op, (((0,), (0,)), ((), ())), preferred_element_type=f32
    )


def dot_cols(left_op, right_op):
    return lax.dot_general(
        left_op, right_op, (((1,), (1,)), ((), ())), preferred_element_type=f32
    )


def swap(values, axis_name, bit):
    size = lax.axis_size(axis_name)
    return lax.ppermute(values, axis_name, [(i, i ^ bit) for i in range(size)])


def shift(values, axis_name, step):
    size = lax.axis_size(axis_name)
    pairs = [(i, i + step) for i in range(size) if 0 <= i + step < size]
    return lax.ppermute(values, axis_name, pairs)


def bits_of(size):
    found = []
    bit = 1
    while bit < size:
        found.append(bit)
        bit *= 2
    return found


def fsdp_order(size):
    order = [0]
    for bit in reversed(bits_of(size)):
        order = order + [held ^ bit for held in order]
    return order


def gather_pieces(piece):
    pieces = [piece]
    for bit in reversed(bits_of(lax.axis_size("fsdp"))):
        pieces = pieces + [swap(held, "fsdp", bit) for held in pieces]
    return pieces


def xor_blocks(blocks, index, size):
    for bit in bits_of(size):
        on = (index & bit) != 0
        blocks = [jnp.where(on, blocks[i ^ bit], blocks[i]) for i in range(size)]
    return blocks


def to_relative(values, index, size):
    width = values.shape[-1] // size
    blocks = [values[..., i * width : (i + 1) * width] for i in range(size)]
    blocks = xor_blocks(blocks, index, size)
    return jnp.concatenate([blocks[i] for i in fsdp_order(size)], axis=-1)


def from_relative(values, index, size):
    width = values.shape[-1] // size
    order = fsdp_order(size)
    blocks = [None] * size
    for place, i in enumerate(order):
        blocks[i] = values[..., place * width : (place + 1) * width]
    return jnp.concatenate(xor_blocks(blocks, index, size), axis=-1)


def reduce_fsdp(values, axis):
    for bit in bits_of(lax.axis_size("fsdp")):
        half = values.shape[axis] // 2
        kept = lax.slice_in_dim(values, 0, half, axis=axis)
        sent = lax.slice_in_dim(values, half, 2 * half, axis=axis).astype(bf16)
        values = kept.astype(f32) + swap(sent, "fsdp", bit).astype(f32)
    return values


def sum_context(values):
    index = lax.axis_index("context")
    bits = bits_of(lax.axis_size("context"))
    for bit in bits:
        half = values.shape[0] // 2
        on = (index & bit) != 0
        kept = jnp.where(on, values[half:], values[:half])
        sent = jnp.where(on, values[:half], values[half:]).astype(bf16)
        values = kept + swap(sent, "context", bit).astype(f32)
    values = values.astype(bf16)
    for bit in reversed(bits):
        on = (index & bit) != 0
        other = swap(values, "context", bit)
        values = jnp.concatenate(
            [jnp.where(on, other, values), jnp.where(on, values, other)], axis=0
        )
    return values.astype(f32)


def whole(array):
    return pl.BlockSpec(array.shape, lambda *ids: (0,) * array.ndim)


def wide_enough(pieces, axis):
    if pieces[0].shape[axis] % LANES:
        return [jnp.concatenate(pieces, axis=axis)]
    return pieces


SCALE = 0.2


def cost(us=1):
    return pl.CostEstimate(
        flops=int(us * SCALE * 1.1e9), bytes_accessed=int(us * SCALE * 3.6e6), transcendentals=0
    )


def joined(refs, index_ref, axis, cut=None):
    blocks = [r[...] if cut is None else r[cut] for r in refs]
    if len(blocks) > 1:
        order = fsdp_order(len(blocks))
        blocks = [blocks[order.index(i)] for i in range(len(blocks))]
        blocks = xor_blocks(blocks, index_ref[0], len(blocks))
    return jnp.concatenate(blocks, axis=axis)


def params(mib):
    return pltpu.CompilerParams(vmem_limit_bytes=mib << 20)


def pack_body(count, start_ref, *refs):
    out_ref = refs[-1]
    for i in range(count):
        at = slice(i * LANES, (i + 1) * LANES)
        out_ref[0, :, at] = refs[i][...].astype(bf16)
        out_ref[1, :, at] = refs[count + i][...].astype(bf16)
        out_ref[2, :, at] = refs[2 * count + i][...].T.astype(bf16)


def pack(w_gate, w_up, w_down, start, width):
    shard = w_gate.shape[0]
    count = width // LANES
    columns = [pl.BlockSpec((shard, LANES), lambda j, s, i=i: (0, s[0] + i)) for i in range(count)]
    lines = [pl.BlockSpec((LANES, shard), lambda j, s, i=i: (s[0] + i, 0)) for i in range(count)]
    spec = pltpu.PrefetchScalarGridSpec(
        num_scalar_prefetch=1,
        grid=(1,),
        in_specs=columns + columns + lines,
        out_specs=pl.BlockSpec((3, shard, width), lambda j, s: (0, 0, 0)),
    )
    return pl.pallas_call(
        functools.partial(pack_body, count),
        out_shape=jax.ShapeDtypeStruct((3, shard, width), bf16),
        grid_spec=spec,
        cost_estimate=cost(),
        compiler_params=params(60),
    )(start, *[w_gate] * count, *[w_up] * count, *[w_down] * count)


def qkv_pack_body(index_ref, g1_ref, g2_ref, bq_ref, bk_ref, bv_ref, wq_ref, wk_ref, wv_ref, out_ref):
    shard, at = wq_ref.shape[0], 0
    for ref in (wq_ref, wk_ref, wv_ref):
        out_ref[:shard, at : at + ref.shape[1]] = ref[...].astype(bf16)
        at += ref.shape[1]
    row = lax.broadcasted_iota(jnp.int32, (16, shard), 0)
    first, second = g1_ref[...][None, :], g2_ref[...][None, :]
    gains = jnp.where(row == 0, first, jnp.where(row == 1, second, 0.0))
    columns = bq_ref.shape[1]
    from_column = lax.broadcasted_iota(jnp.int32, (columns, HD), 0)
    to_column = lax.broadcasted_iota(jnp.int32, (columns, HD), 1)
    spread = (to_column == from_column + columns * index_ref[0]).astype(bf16)
    biases, at = 0.0, 8
    for ref in (bq_ref, bk_ref, bv_ref):
        heads = ref.shape[0]
        to_row = lax.broadcasted_iota(jnp.int32, (16, heads), 0)
        from_row = lax.broadcasted_iota(jnp.int32, (16, heads), 1) + at
        wide = dot_plain(ref[...].astype(bf16), spread).astype(bf16)
        if heads == 1:
            row = lax.broadcasted_iota(jnp.int32, (16, HD), 0)
            biases = biases + jnp.where(row == at, wide.astype(f32), 0.0)
        else:
            biases = biases + dot_plain((to_row == from_row).astype(bf16), wide)
        at += heads
    out_ref[shard:, :] = jnp.zeros((16, out_ref.shape[1]), bf16)
    out_ref[shard:, :HD] = (gains[:, :HD] + biases).astype(bf16)
    out_ref[shard:, HD:shard] = gains[:, HD:].astype(bf16)


def qkv_pack(index, g1, g2, b_q, b_k, b_v, w_q, w_k, w_v):
    width = w_q.shape[1] + w_k.shape[1] + w_v.shape[1]
    inputs = (g1, g2, b_q, b_k, b_v, w_q, w_k, w_v)
    return pl.pallas_call(
        qkv_pack_body,
        out_shape=jax.ShapeDtypeStruct((w_q.shape[0] + 16, width), bf16),
        in_specs=[pl.BlockSpec(memory_space=pltpu.SMEM)] + [pl.BlockSpec(memory_space=pltpu.VMEM)] * len(inputs),
        cost_estimate=cost(2),
        compiler_params=params(60),
    )(index, *inputs)


def vectors_body(count, heads, index_ref, *refs):
    gain_ref, bias_ref = refs[count:]
    width = D // count
    gain_ref[...] = joined(refs[:count], index_ref, 1, (slice(0, 2), slice(0, width)))
    bias_ref[...] = sum(r[8 : 8 + heads, :HD].astype(f32) for r in refs[:count])


def vectors(index, pieces, heads):
    shard = D // len(pieces)
    if shard % LANES:
        order = fsdp_order(len(pieces))
        blocks = [pieces[order.index(i)][shard : shard + 2, :shard] for i in range(len(pieces))]
        gains = jnp.concatenate(xor_blocks(blocks, index[0], len(pieces)), axis=1)
        return gains, sum(p[shard + 8 : shard + 8 + heads, :HD].astype(f32) for p in pieces)
    rows = pl.BlockSpec((16, pieces[0].shape[1]), lambda i: (shard // 16, 0))
    outs = (jax.ShapeDtypeStruct((2, D), bf16), jax.ShapeDtypeStruct((heads, HD), f32))
    return pl.pallas_call(
        functools.partial(vectors_body, len(pieces), heads),
        out_shape=outs,
        grid=(1,),
        in_specs=[pl.BlockSpec(memory_space=pltpu.SMEM)] + [rows] * len(pieces),
        out_specs=tuple(whole(a) for a in outs),
        cost_estimate=cost(),
        compiler_params=params(60),
    )(index, *pieces)


def project_body(count, q_width, index_ref, a_ref, b_ref, gain_ref, bias_ref, cos_ref, sin_ref, *refs):
    w_refs, (q_ref, kv_ref, h_ref) = refs[:count], refs[count:]
    x = jnp.concatenate([a_ref[...], b_ref[...]], axis=0).astype(f32)
    scale = lax.rsqrt(jnp.mean(x * x, axis=-1, keepdims=True) + epsilon)
    normed = (x * scale * gain_ref[0:1].astype(f32)).astype(bf16)
    h_ref[...] = normed
    total = w_refs[0].shape[1]
    depth = D // count
    for at in range(0, total, WIDE):
        weights = joined(w_refs, index_ref, 0, (slice(0, depth), slice(at, at + WIDE)))
        both = dot_plain(normed, weights)
        for inner in range(0, WIDE, HD):
            place = at + inner
            head = place // HD
            values = both[:, inner : inner + HD] + bias_ref[head : head + 1]
            if place < total - HD:
                turned = pltpu.roll(values, HD // 2, 1)
                values = values * cos_ref[...] + turned * sin_ref[...]
            if place < q_width:
                q_ref[:, place : place + HD] = values.astype(bf16)
            else:
                kv_ref[:, place - q_width : place - q_width + HD] = values.astype(bf16)


def project(index, first, second, gain, bias, cos_table, sin_table, weights, q_width):
    rows = 2 * first.shape[0]
    total = weights[0].shape[1]
    return pl.pallas_call(
        functools.partial(project_body, len(weights), q_width),
        out_shape=(
            jax.ShapeDtypeStruct((rows, q_width), bf16),
            jax.ShapeDtypeStruct((rows, total - q_width), bf16),
            jax.ShapeDtypeStruct((rows, D), bf16),
        ),
        in_specs=[pl.BlockSpec(memory_space=pltpu.SMEM)] + [pl.BlockSpec(memory_space=pltpu.VMEM)] * (6 + len(weights)),
        cost_estimate=cost(4),
        compiler_params=params(60),
    )(index, first, second, gain, bias, cos_table, sin_table, *weights)


def masked_weights(queries, keys, low_ref, high_ref, key_ref):
    scores = dot_cols(queries, keys) * HD ** (-0.5)
    key_at = key_ref[...]
    allowed = (key_at >= low_ref[...]) & (key_at <= high_ref[...])
    scores = jnp.where(allowed, scores, neg_big)
    top = jnp.max(scores, axis=-1, keepdims=True)
    raised = jnp.exp(scores - top)
    return raised * (1.0 / jnp.sum(raised, axis=-1, keepdims=True))


def attend_body(count, ahead, index_ref, q_ref, low_ref, high_ref, key_ref, *refs):
    w_refs, kv_refs = refs[:count], refs[count : count + ahead]
    o_ref, mine_ref, other_ref = refs[count + ahead :]
    keys = jnp.concatenate([kv[:, :HD] for kv in kv_refs], axis=0)
    values = jnp.concatenate([kv[:, HD:] for kv in kv_refs], axis=0)
    weights = masked_weights(q_ref[...], keys, low_ref, high_ref, key_ref)
    head = pl.program_id(0)
    out = dot_plain(weights.astype(bf16), values).astype(bf16)
    o_ref[:, pl.ds(pl.multiple_of(head * HD, HD), HD)] = out

    @pl.when(head == pl.num_programs(0) - 1)
    def _():
        half = mine_ref.shape[0]
        out_w = joined(w_refs, index_ref, 1)
        branch = dot_plain(o_ref[...], out_w)
        mine_ref[...] = branch[:half]
        other_ref[...] = branch[half:].astype(bf16)


def attend(index, queries, low, high, key_at, weights, kv_parts):
    rows, width = queries.shape
    head = pl.BlockSpec((rows, HD), lambda h: (0, h))
    keys = key_at.shape[1]
    rest = (low, high, key_at, *weights, *kv_parts)
    outs = (
        jax.ShapeDtypeStruct(queries.shape, bf16),
        jax.ShapeDtypeStruct((rows // 2, D), f32),
        jax.ShapeDtypeStruct((rows // 2, D), bf16),
    )
    return pl.pallas_call(
        functools.partial(attend_body, len(weights), len(kv_parts)),
        out_shape=outs,
        grid=(width // HD,),
        in_specs=[pl.BlockSpec(memory_space=pltpu.SMEM), head] + [whole(a) for a in rest],
        out_specs=tuple(whole(a) for a in outs),
        compiler_params=params(60),
        cost_estimate=cost(8),
    )(index, queries, *rest)


def middle_body(x_ref, mine_ref, other_ref, gain_ref, mid_ref, h_ref):
    middle = x_ref[...].astype(f32) + mine_ref[...] + other_ref[...].astype(f32)
    scale = lax.rsqrt(jnp.mean(middle * middle, axis=-1, keepdims=True) + epsilon)
    mid_ref[...] = middle
    h_ref[...] = (middle * scale * gain_ref[1:2].astype(f32)).astype(bf16)


def middle_norm(x, mine, other, gain):
    return pl.pallas_call(
        middle_body,
        out_shape=(jax.ShapeDtypeStruct(mine.shape, f32), jax.ShapeDtypeStruct(mine.shape, bf16)),
        cost_estimate=cost(),
        compiler_params=params(60),
    )(x, mine, other, gain)


def feed_body(
    count, bases, back, carried, last, filled, at_row, limit_ref, ctx_ref, *refs
):
    h_refs, refs = refs[: 2 * len(bases)], refs[2 * len(bases) :]
    (g_own, g_across, w_hbm), refs = refs[:3], refs[3:]
    carry, refs = refs[: 2 * carried], refs[2 * carried + filled :]
    bufs = None
    if carried:
        outs, (w_ref, act_ref, sems, bufs) = refs[:-4], refs[-4:]
    else:
        outs, (w_ref, act_ref, sems) = refs[:-3], refs[-3:]
    rows, width = act_ref.shape[1:]
    tiles = 3
    loads = [
        pltpu.make_async_copy(w_hbm.at[:, k], w_ref.at[:, k], sems.at[k]) for k in range(tiles)
    ]
    carries = [
        pltpu.make_async_copy(ref, bufs.at[k], sems.at[tiles + k]) for k, ref in enumerate(carry)
    ]
    for copy in loads + carries:
        copy.start()
    half = g_own.shape[1]
    chunk = 2 * half
    lane = lax.broadcasted_iota(jnp.int32, (1, width), 1)
    shown = lane >= limit_ref[0]

    def weights(k):
        return jnp.concatenate([w_ref[i, k] for i in range(count)], axis=0)

    at = 0
    for which, h_ref in enumerate(h_refs):
        base, g_ref = bases[which // 2], (g_own, g_across)[which % 2]
        for j in range(h_ref.shape[0] // chunk):
            rows_in = h_ref[j * chunk : (j + 1) * chunk]
            grads_in = jnp.concatenate(
                [g_ref[ctx_ref[0] ^ (base + 2 * j + k)] for k in range(2)], axis=0
            )
            if at == 0:
                loads[0].wait()
            gate = dot_plain(rows_in, weights(0))
            if at == 0:
                loads[1].wait()
            up = dot_plain(rows_in, weights(1))
            if at == 0:
                loads[2].wait()
            d_hidden = dot_plain(grads_in, weights(2))
            gate_sig = jax.nn.sigmoid(gate)
            activated = gate * gate_sig
            hidden = activated * up
            d_gate = d_hidden * up * gate_sig * (1.0 + gate * (1.0 - gate_sig))
            d_up = d_hidden * activated
            act_ref[0, at : at + chunk] = jnp.where(shown, d_gate, 0.0).astype(bf16)
            act_ref[1, at : at + chunk] = jnp.where(shown, d_up, 0.0).astype(bf16)
            act_ref[2, at : at + chunk] = jnp.where(shown, hidden, 0.0).astype(bf16)
            at += chunk
    at = tiles + len(carries)
    copies = [
        pltpu.make_async_copy(act_ref.at[k], outs[k].at[pl.ds(at_row, rows)], sems.at[at + k])
        for k in range(3)
    ]
    for copy in copies:
        copy.start()
    if back:
        team = slice(0, 4 * half)
        d_rows = dot_cols(act_ref[0, team], weights(0)) + dot_cols(act_ref[1, team], weights(1))
        out_rows = dot_cols(act_ref[2, team], weights(2))
        for copy in carries:
            copy.wait()
        if carried:
            d_rows = d_rows + bufs[0]
            out_rows = out_rows + bufs[1]
        if last:
            cuts = ((0, half), (half, 2 * half), (2 * half, 4 * half))
            for group, total in ((outs[3:6], d_rows), (outs[6:], out_rows)):
                for ref, (low, high) in zip(group, cuts):
                    ref[...] = total[low:high].astype(ref.dtype)
        else:
            outs[3][...] = d_rows
            outs[4][...] = out_rows
    for copy in copies:
        copy.wait()


def feed(limit, ctx, rows_in, grads_in, weights, total, back, carry=(), last=False, act=None):
    some = sum(r.shape[0] for r in rows_in)
    width = weights.shape[3]
    outs = [jax.ShapeDtypeStruct((total, width), bf16)] * 3
    half = grads_in[0].shape[1]
    if back and last:
        group = [jax.ShapeDtypeStruct((half, D), f32)] * 2
        outs += (group + [jax.ShapeDtypeStruct((2 * half, D), bf16)]) * 2
    elif back:
        outs += [jax.ShapeDtypeStruct((4 * half, D), f32)] * 2
    vmem = pl.BlockSpec(memory_space=pltpu.VMEM)
    smem = pl.BlockSpec(memory_space=pltpu.SMEM)
    hbm = pl.BlockSpec(memory_space=pl.ANY)
    inputs = (*rows_in, *grads_in)
    filled = () if act is None else tuple(act)
    scratch = [
        pltpu.VMEM(weights.shape, bf16),
        pltpu.VMEM((3, some, width), bf16),
        pltpu.SemaphoreType.DMA((6 + len(carry),)),
    ]
    if carry:
        scratch.append(pltpu.VMEM((2, 4 * half, D), f32))
    first = 3 + len(inputs) + len(carry)
    return pl.pallas_call(
        functools.partial(
            feed_body, weights.shape[0],
            ((0,) if back else ()) + ((TEAM,) if some == total or not back else ()),
            back, len(carry) // 2, last, len(filled), 0 if back else total - some,
        ),
        out_shape=tuple(outs),
        in_specs=[smem, smem] + [vmem] * len(inputs) + [hbm] * (1 + len(carry) + len(filled)),
        out_specs=tuple([hbm] * 3 + [vmem] * (len(outs) - 3)),
        scratch_shapes=scratch,
        input_output_aliases={first + k: k for k in range(len(filled))},
        compiler_params=params(60),
        cost_estimate=cost((6 if back else 0) + 9 * some / 512),
    )(limit, ctx, *inputs, weights, *carry, *filled)


def turn_body(blocks, dynamic, contexts, index_ref, ctx_ref, *refs):
    kept_ref, sent_ref = refs[-2:]
    width = D // blocks
    order = fsdp_order(blocks)
    values = [(ref, None) for ref in refs[:-2]]
    if contexts:
        groups = (range(TEAM), range(TEAM, contexts))
        values = [(ref, ctx_ref[0] ^ k) for group in groups for ref in refs[:-2] for k in group]
    at = 0
    for ref, which in values:
        value = ref[...] if which is None else ref[which]
        here = slice(at, at + value.shape[0])
        at += value.shape[0]
        parts = [value[:, i * width : (i + 1) * width] for i in range(blocks)]
        if dynamic:
            parts = xor_blocks(parts, index_ref[0], blocks)
            parts = [parts[i] for i in order]
        for spot in range(blocks // 2):
            lines_at = slice(spot * width, (spot + 1) * width)
            kept_ref[lines_at, here] = parts[spot].T
            sent_ref[lines_at, here] = parts[blocks // 2 + spot].T


def turn_rows(index, ctx, rows, n_fsdp):
    total = sum(r.size for r in rows) // D
    contexts = rows[0].shape[0] if rows[0].ndim == 3 else 0
    blocks = n_fsdp
    if D // n_fsdp % LANES:
        blocks = 2
        rows = [to_relative(v, index[0], n_fsdp) for v in rows]
    return pl.pallas_call(
        functools.partial(turn_body, blocks, blocks == n_fsdp, contexts),
        out_shape=(jax.ShapeDtypeStruct((D // 2, total), bf16),) * 2,
        in_specs=[pl.BlockSpec(memory_space=pltpu.SMEM), pl.BlockSpec(memory_space=pltpu.SMEM)] + [pl.BlockSpec(memory_space=pltpu.VMEM)] * len(rows),
        cost_estimate=cost(4),
        compiler_params=params(60),
    )(index, ctx, *rows)


def weight_body(*refs):
    own, beside, acts = refs[:2], refs[2:4], refs[4:7]
    acts_beside, (near_ref, far_ref) = refs[7:10], refs[10:]
    cut = near_ref.shape[1]
    for k in range(3):
        value = dot_plain(own[k // 2][...], acts[k][...])
        value = value + dot_plain(beside[k // 2][...], acts_beside[k][...])
        near_ref[k] = value[:cut].astype(bf16)
        far_ref[k] = value[cut:].astype(bf16)


def weight_grads(own, beside, acts, acts_beside):
    total, width = acts[0].shape
    left = pl.BlockSpec(own[0].shape, lambda j: (0, 0), pipeline_mode=pl.Buffered(1))
    right = pl.BlockSpec((total, WIDE), lambda j: (0, j))
    out = pl.BlockSpec((3, D // 4, WIDE), lambda j: (0, 0, j))
    return pl.pallas_call(
        weight_body,
        out_shape=(jax.ShapeDtypeStruct((3, D // 4, width), bf16),) * 2,
        grid=(width // WIDE,),
        in_specs=[left] * 4 + [right] * 6,
        out_specs=(out, out),
        compiler_params=params(60),
        cost_estimate=cost(12),
    )(*own, *beside, *acts, *acts_beside)


def middle_back_body(
    near_ref, across_ref, far_ref, mid_ref, gain_ref, g_ref, d_ref, low_ref, gain_out
):
    d_normed = near_ref[...] + across_ref[...].astype(f32) + far_ref[...].astype(f32)
    middle = mid_ref[...]
    scale = lax.rsqrt(jnp.mean(middle * middle, axis=-1, keepdims=True) + epsilon)
    gain_out[...] = jnp.sum(d_normed * middle * scale, axis=0, keepdims=True)
    weighted = d_normed * gain_ref[1:2].astype(f32)
    inner = jnp.mean(weighted * middle, axis=-1, keepdims=True)
    d_middle = g_ref[...].astype(f32) + scale * weighted - middle * scale**3 * inner
    d_ref[...] = d_middle
    low_ref[...] = d_middle.astype(bf16)


def middle_back(near, across, far, middle, gain, grads):
    return pl.pallas_call(
        middle_back_body,
        out_shape=(
            jax.ShapeDtypeStruct(near.shape, f32),
            jax.ShapeDtypeStruct(near.shape, bf16),
            jax.ShapeDtypeStruct((1, D), f32),
        ),
        cost_estimate=cost(),
        compiler_params=params(60),
    )(near, across, far, middle, gain, grads)


def attend_back_body(count, ahead, index_ref, q_ref, low_ref, high_ref, key_ref, cos_ref, sin_ref, *refs):
    scale = HD ** (-0.5)
    mine_ref, other_ref = refs[:2]
    w_refs, kv_refs = refs[2 : 2 + count], refs[2 + count : 2 + count + ahead]
    outs = refs[2 + count + ahead :]
    dq_ref, dkv_refs, (d_o, sums) = outs[0], outs[1 : 1 + ahead], outs[1 + ahead :]
    head = pl.program_id(0)

    @pl.when(head == 0)
    def _():
        d_branch = jnp.concatenate([mine_ref[...], other_ref[...]], axis=0)
        out_w = joined(w_refs, index_ref, 1)
        d_o[...] = dot_cols(d_branch, out_w).astype(bf16)
        sums[...] = jnp.zeros_like(sums)

    queries = q_ref[...]
    grad = d_o[:, pl.ds(pl.multiple_of(head * HD, HD), HD)]
    keys = jnp.concatenate([kv[:, :HD] for kv in kv_refs], axis=0)
    values = jnp.concatenate([kv[:, HD:] for kv in kv_refs], axis=0)
    weights = masked_weights(queries, keys, low_ref, high_ref, key_ref)
    dweights = dot_cols(grad, values)
    delta = jnp.sum(weights * dweights, axis=-1, keepdims=True)
    dscores = (weights * (dweights - delta)).astype(bf16)
    dq_rot = dot_plain(dscores, keys) * scale
    turned = pltpu.roll(dq_rot, HD // 2, 1)
    dq_ref[...] = (dq_rot * cos_ref[...] - turned * sin_ref[...]).astype(bf16)
    sums[:, :HD] += dot_rows(dscores, queries) * scale
    sums[:, HD:] += dot_rows(weights.astype(bf16), grad)

    @pl.when(head == pl.num_programs(0) - 1)
    def _():
        rows = q_ref.shape[0]
        for i, out in enumerate(dkv_refs):
            out[...] = sums[i * rows : (i + 1) * rows].astype(out.dtype)


def attend_back(index, queries, low, high, key_at, cos_table, sin_table, grads, weights, kv_parts):
    rows, width = queries.shape
    head = pl.BlockSpec((rows, HD), lambda h: (0, h))
    keys = key_at.shape[1]
    rest = (low, high, key_at, cos_table, sin_table, *grads, *weights, *kv_parts)
    outs = [jax.ShapeDtypeStruct(queries.shape, bf16)]
    outs += [
        jax.ShapeDtypeStruct(kv.shape, bf16 if i else f32) for i, kv in enumerate(kv_parts)
    ]
    return pl.pallas_call(
        functools.partial(attend_back_body, len(weights), len(kv_parts)),
        out_shape=tuple(outs),
        grid=(width // HD,),
        in_specs=[pl.BlockSpec(memory_space=pltpu.SMEM), head] + [whole(a) for a in rest],
        out_specs=tuple([head] + [whole(a) for a in outs[1:]]),
        scratch_shapes=[pltpu.VMEM((rows, width), bf16), pltpu.VMEM((keys, 2 * HD), f32)],
        compiler_params=params(60),
        cost_estimate=cost(10),
    )(index, queries, *rest)


def project_back_body(count, ahead, index_ref, dq_ref, cos_ref, sin_ref, *refs):
    w_refs, dkv_refs = refs[:count], refs[count : count + ahead]
    d_ref, mine_ref, other_ref, bias_ref = refs[count + ahead :]
    total = dkv_refs[0][...]
    for extra in dkv_refs[1:]:
        total = total + extra[...].astype(f32)
    dk = total[:, :HD]
    dk = dk * cos_ref[...] - pltpu.roll(dk, HD // 2, 1) * sin_ref[...]
    d_low = jnp.concatenate([dq_ref[...], dk.astype(bf16), total[:, HD:].astype(bf16)], axis=1)
    d_ref[...] = d_low
    bias_ref[...] = jnp.sum(d_low.astype(f32), axis=0, keepdims=True)
    weights = joined(w_refs, index_ref, 0, slice(0, D // count))
    d_normed = dot_cols(d_low, weights)
    half = mine_ref.shape[0]
    mine_ref[...] = d_normed[:half]
    other_ref[...] = d_normed[half:].astype(bf16)


def project_back(index, dq, cos_table, sin_table, weights, dkv_parts):
    rows = dq.shape[0]
    total = weights[0].shape[1]
    return pl.pallas_call(
        functools.partial(project_back_body, len(weights), len(dkv_parts)),
        out_shape=(
            jax.ShapeDtypeStruct((rows, total), bf16),
            jax.ShapeDtypeStruct((rows // 2, D), f32),
            jax.ShapeDtypeStruct((rows // 2, D), bf16),
            jax.ShapeDtypeStruct((1, total), f32),
        ),
        in_specs=[pl.BlockSpec(memory_space=pltpu.SMEM)] + [pl.BlockSpec(memory_space=pltpu.VMEM)] * (3 + len(weights) + len(dkv_parts)),
        cost_estimate=cost(4),
        compiler_params=params(60),
    )(index, dq, cos_table, sin_table, *weights, *dkv_parts)


def input_back_body(mine_ref, other_ref, x_ref, gain_ref, mid_ref, d_ref, gain_out):
    d_normed = mine_ref[...] + other_ref[...].astype(f32)
    x = x_ref[...].astype(f32)
    scale = lax.rsqrt(jnp.mean(x * x, axis=-1, keepdims=True) + epsilon)
    gain_out[...] = jnp.sum(d_normed * x * scale, axis=0, keepdims=True)
    weighted = d_normed * gain_ref[0:1].astype(f32)
    inner = jnp.mean(weighted * x, axis=-1, keepdims=True)
    d_ref[...] = (mid_ref[...] + scale * weighted - x * scale**3 * inner).astype(bf16)


def input_back(mine, other, x, gain, d_middle):
    return pl.pallas_call(
        input_back_body,
        out_shape=(jax.ShapeDtypeStruct(mine.shape, bf16), jax.ShapeDtypeStruct((1, D), f32)),
        cost_estimate=cost(),
        compiler_params=params(60),
    )(mine, other, x, gain, d_middle)


def place_body(plan, carried, member_ref, *refs):
    own_ref, other_ref, refs = refs[0], refs[1], refs[2:]
    outs = refs[carried : carried + 3]
    wide_buf, tall_buf, sems = refs[carried + 3 :]
    width = own_ref.shape[2]

    def copies(team):
        skip, at = plan[team]
        size = width - skip
        for k in range(2):
            yield pltpu.make_async_copy(
                wide_buf.at[team, k, :, pl.ds(skip, size)],
                outs[k].at[:, pl.ds(at + skip, size)],
                sems.at[team, k],
            )
        yield pltpu.make_async_copy(
            tall_buf.at[team, pl.ds(skip, size)],
            outs[2].at[pl.ds(at + skip, size)],
            sems.at[team, 2],
        )

    for team in range(len(plan)):
        def put(ref, team=team):
            wide_buf[team, 0] = ref[0].astype(f32)
            wide_buf[team, 1] = ref[1].astype(f32)
            tall_buf[team] = ref[2].astype(f32).T

        @pl.when(member_ref[0] == team)
        def _():
            put(own_ref)

        @pl.when(member_ref[0] != team)
        def _():
            put(other_ref)

        for copy in copies(team):
            copy.start()
    for team in range(len(plan)):
        for copy in copies(team):
            copy.wait()


def place(member, own, other, index, starts, fresh, ff_local, carry):
    shard, width = own.shape[1:]
    plan = tuple(
        (min(max(fresh[s] - index * width, 0), width), starts[s] + index * width)
        for s in range(TEAM)
    )
    hbm = pl.BlockSpec(memory_space=pl.ANY)
    vmem = pl.BlockSpec(memory_space=pltpu.VMEM)
    return pl.pallas_call(
        functools.partial(place_body, plan, len(carry)),
        out_shape=(
            jax.ShapeDtypeStruct((shard, ff_local), f32),
            jax.ShapeDtypeStruct((shard, ff_local), f32),
            jax.ShapeDtypeStruct((ff_local, shard), f32),
        ),
        in_specs=[pl.BlockSpec(memory_space=pltpu.SMEM)] + [vmem] * 2 + [hbm] * len(carry),
        out_specs=(hbm, hbm, hbm),
        scratch_shapes=[
            pltpu.VMEM((TEAM, 2, shard, width), f32),
            pltpu.VMEM((TEAM, width, shard), f32),
            pltpu.SemaphoreType.DMA((TEAM, 3)),
        ],
        input_output_aliases={3 + i: i for i in range(len(carry))},
        cost_estimate=cost(),
        compiler_params=params(60),
    )(member, own, other, *carry)


def after(values, *first):
    return lax.optimization_barrier((values, first))[0]


class Order:
    def __init__(self):
        self.last = ()

    def __call__(self, step, *args):
        args, _ = lax.optimization_barrier((args, self.last))
        result = step(*args)
        self.last = (jax.tree.leaves(result)[0],)
        return result

    def pin(self, values):
        values, _ = lax.optimization_barrier((values, self.last))
        self.last = (jax.tree.leaves(values)[0],)
        return values


def stack(*pieces):
    return jnp.concatenate(pieces, axis=0)


class Pieces:
    def __init__(self, run, full, *first):
        bits = list(reversed(bits_of(lax.axis_size("fsdp"))))
        self.run, self.near = run, bits[-1]
        self.held = [full]
        gate = after(full, *first)
        for bit in bits[:-1]:
            self.held = self.held + [swap(p, "fsdp", bit) for p in [gate] + self.held[1:]]

    def turn(self):
        self.held = self.held[:1] + list(self.run.pin(tuple(self.held[1:])))
        self.sent = swap(self.run(lambda *a: jnp.stack(a), *self.held), "fsdp", self.near)
        return self.held[-1]

    def finish(self):
        self.sent = self.run.pin(self.sent)

    def pieces(self):
        return self.held + [self.sent[i] for i in range(len(self.held))]


def per_device(
    tokens,
    cotangent,
    lengths,
    span_order,
    attn_gain,
    w_q,
    b_q,
    w_k,
    b_k,
    w_v,
    b_v,
    w_o,
    mlp_gain,
    w_gate,
    w_up,
    w_down,
):
    n_fsdp = lax.axis_size("fsdp")
    n_ctx = lax.axis_size("context")
    my_fsdp = lax.axis_index("fsdp")
    my_ctx = lax.axis_index("context")
    my_tensor = lax.axis_index("tensor")
    member = my_ctx % TEAM
    rows = tokens.shape[0]
    half = rows // 2
    piece_rows = rows // n_ctx
    shard = D // n_fsdp
    q_width = w_q.shape[1]
    kv_width = w_k.shape[1]
    qkv_width = q_width + 2 * kv_width
    heads_local = q_width // HD
    all_heads = qkv_width // HD
    flipped = my_tensor != 0
    run = Order()
    sharing = n_fsdp == 4 and n_ctx % 2 == 0

    def mine_first(values):
        first, second = values[:half], values[half:]
        return stack(jnp.where(flipped, second, first), jnp.where(flipped, first, second))

    bias_cols = HD // n_fsdp

    index = my_fsdp.astype(jnp.int32).reshape(1)
    qkv_h = Pieces(
        run, run(qkv_pack, index, attn_gain, mlp_gain, b_q, b_k, b_v, w_q, w_k, w_v)
    )
    out_cast = run(lambda w: w.astype(bf16), w_o)

    def arrange(values):
        both = mine_first(values)
        return both[:half], both[half:]

    class Rows:
        def __init__(self, mine):
            self.mine = mine
            self.beside = swap(mine, "context", 1)

        def turn(self):
            self.beside = run.pin(self.beside)
            self.held = run(stack, self.mine, self.beside)
            self.held_across = swap(self.held, "tensor", 1)
            held, others = self.held, []
            for bit in bits_of(n_ctx)[1:]:
                there = swap(held, "context", bit)
                others.append(there)
                held = stack(held, there)
            self.remote = others[0] if len(others) == 1 else stack(*others)

        def across_rest(self):
            self.remote = run.pin(self.remote)
            self.remote_across = swap(self.remote, "tensor", 1)

        def pin_team(self):
            self.held_across = run.pin(self.held_across)

        def pin_rest(self):
            self.remote_across = run.pin(self.remote_across)

        def team(self):
            return (self.held, self.held_across)

        def rest(self):
            return (self.remote, self.remote_across)

    grad_mine, _ = run(arrange, cotangent)
    grads_own = lax.all_gather(grad_mine, "context")

    ff_local = w_gate.shape[1]
    tiles = ff_local // LANES
    unit = PARTS * WIDE // LANES
    slice_tiles = -(-tiles // (TEAM * unit)) * unit
    part = slice_tiles // PARTS * LANES
    starts = [min(s * slice_tiles, tiles - slice_tiles) * LANES for s in range(TEAM)]
    fresh = [s * slice_tiles * LANES - starts[s] for s in range(TEAM)]
    my_start = jnp.int32(starts[0] // LANES)
    limit = jnp.int32(fresh[0])
    for s in range(1, TEAM):
        my_start = jnp.where(member == s, starts[s] // LANES, my_start)
        limit = jnp.where(member == s, fresh[s], limit)

    def packed(index):
        start = (my_start + index * (part // LANES)).reshape(1)
        return run(lambda *a: pack(*a, part), w_gate, w_up, w_down, start)

    longest = 3 * n_ctx * rows // 8
    behind = min(n_ctx - 1, (longest - 1 + rows - 1) // rows)
    half_dim = HD // 2

    def places(lengths, span_order):
        seq_ends = jnp.cumsum(lengths[0])
        row = jnp.arange(rows, dtype=jnp.int32)
        stored = jnp.where(flipped, (row + half) % rows, row)

        def packed_of(context):
            owner = lax.dynamic_index_in_dim(span_order[0], context, 0, keepdims=False)
            span = stored // piece_rows
            hot = span[:, None] == jnp.arange(n_ctx, dtype=jnp.int32)[None, :]
            spot = jnp.sum(jnp.where(hot, owner[None, :], 0), axis=1)
            return context * rows + spot * piece_rows + stored % piece_rows

        own_at = packed_of(my_ctx)
        passed = own_at[:, None] >= seq_ends[None, :]
        begin = jnp.max(jnp.where(passed, seq_ends[None, :], 0), axis=1)
        position = own_at - begin
        key_at = [own_at]
        for step in range(1, behind + 1):
            there = packed_of(jnp.maximum(my_ctx - step, 0))
            key_at.append(jnp.where(my_ctx >= step, there, far_away))
        frequency = rope_base ** (-(jnp.arange(half_dim, dtype=f32) * 2.0) / HD)
        angles = position.astype(f32)[:, None] * frequency[None, :]
        cosine, sine = jnp.cos(angles), jnp.sin(angles)
        return (
            begin[:, None],
            own_at[:, None],
            jnp.concatenate(key_at)[None, :],
            jnp.concatenate([cosine, cosine], axis=1),
            jnp.concatenate([-sine, sine], axis=1),
        )

    ctx = my_ctx.astype(jnp.int32).reshape(1)
    feed_in = [packed(0)]
    mine_tokens, other_tokens = run(arrange, tokens)
    feed_in.append(packed(1))
    far = qkv_h.turn()
    out_h = Pieces(run, out_cast, far)
    feed_in += [packed(i) for i in range(2, PARTS)]
    feed_w = [lax.all_gather(after(v, far), "fsdp") for v in feed_in]
    low, high, key_at, cos_table, sin_table = run(places, lengths, span_order)
    qkv_h.finish()

    def in_order(pieces, axis, cut=None):
        if shard % LANES == 0:
            return pieces
        order = fsdp_order(n_fsdp)
        blocks = [pieces[order.index(i)] for i in range(n_fsdp)]
        blocks = [b if cut is None else b[:cut] for b in blocks]
        return [jnp.concatenate(xor_blocks(blocks, my_fsdp, n_fsdp), axis=axis)]

    gains, bias = run(lambda i, p: vectors(i, p, all_heads), index, qkv_h.pieces())
    qkv_w = in_order(qkv_h.pieces(), 0, shard)

    queries, kv_own, normed = run(
        lambda *a: project(*a, q_width),
        index, mine_tokens, other_tokens, gains, bias, cos_table, sin_table, qkv_w,
    )
    kv_parts = [kv_own] + [shift(kv_own, "context", step) for step in range(1, behind + 1)]
    grads_own = run.pin(grads_own)
    grads = (grads_own, swap(grads_own, "tensor", 1))
    normed_rel = run(lambda v: to_relative(v, my_fsdp, n_fsdp), normed)
    out_h.turn()
    kv_parts = [kv_own] + list(run.pin(tuple(kv_parts[1:])))
    out_h.finish()
    out_w = in_order(out_h.pieces(), 1)
    branch_mine, attended, branch_other = run(
        lambda *a: (lambda o, m, s: (m, o, s))(*attend(*a)),
        index, queries, low, high, key_at, out_w, kv_parts,
    )
    branch_other = swap(branch_other, "tensor", 1)
    sent = run(lambda a, b: jnp.concatenate([a, b[:, D // 2 :]], axis=1), attended, normed_rel)
    early_beside = swap(sent, "fsdp", 1)
    grads = run.pin(grads)
    middle, normed_two = run(
        middle_norm, mine_tokens, branch_mine, branch_other, gains
    )
    lines = Rows(normed_two)
    early_beside = run.pin(early_beside)
    attended_beside, normed_beside = early_beside[:, :q_width], early_beside[:, q_width:]
    lines.turn()
    turned_grads, grads_sent = run(lambda *a: turn_rows(*a, n_fsdp), index, ctx, grads)
    grads_beside = swap(grads_sent, "fsdp", 1)
    lines.pin_team()

    limits = [limit.reshape(1)] + [jnp.zeros((1,), jnp.int32)] * (PARTS - 1)
    acts, acts_beside = {}, {}
    total_rows = n_ctx * rows

    def feed_team(index, carry, last=False, every=False):
        rows_in = lines.team() + lines.rest() if every else lines.team()
        results = run(
            lambda *a: feed(*a[:5], total_rows, True, a[5], last),
            limits[index], ctx, rows_in, grads, feed_w[index], carry,
        )
        acts[index] = tuple(results[:3])
        if every:
            acts_beside[index] = tuple(swap(a, "fsdp", 1) for a in acts[index])
        return tuple(results[3:])

    def feed_rest(index):
        acts[index] = run(
            lambda *a: feed(*a[:5], total_rows, False, act=a[5]),
            limits[index], ctx, lines.rest(), grads, feed_w[index], acts[index],
        )
        acts_beside[index] = tuple(swap(a, "fsdp", 1) for a in acts[index])

    waiting, reduced, other_parts = {}, {}, {}

    def grads_of(index):
        far, near = run(
            lambda *a: weight_grads(*a)[::-1],
            turned, turned_beside, acts[index], acts_beside[index],
        )
        bits = bits_of(n_fsdp)[1:]
        for bit in bits[:-1]:
            total = near.astype(f32) + swap(far, "fsdp", bit).astype(f32)
            cut = total.shape[1] // 2
            far, near = total[:, cut:].astype(bf16), total[:, :cut].astype(bf16)
        waiting[index] = (near, swap(far, "fsdp", bits[-1]))

    def give(near, arrived):
        return (near.astype(f32) + arrived.astype(f32)).astype(bf16)

    def add_far(index):
        reduced[index] = run(give, *waiting[index])
        other_parts[index] = swap(reduced[index], "context", 1)

    carry = feed_team(0, ())
    lines.across_rest()
    carry = feed_team(1, carry)
    lines.pin_rest()
    turned_lines, lines_sent = run(
        lambda *a: turn_rows(*a, n_fsdp), index, ctx, lines.team() + lines.rest()
    )
    turned = (turned_lines, turned_grads)
    turned_beside = (swap(lines_sent, "fsdp", 1), grads_beside)
    feed_rest(0)
    feed_rest(1)
    grads_of(0)
    given = feed_team(2, carry, True)
    d_near, d_beside, d_far, out_near, out_beside, out_far = given
    d_far = swap(d_far, "tensor", 1)
    feed_rest(2)
    grads_of(1)
    d_beside = swap(run(lambda a, b: give(a, b[half:]), d_beside, d_far), "context", 1)
    add_far(0)
    d_middle, d_branch, grad_gain_two = run(
        lambda a, b, *c: middle_back(a, b[:half], *c),
        d_near, d_far, d_beside, middle, gains, grad_mine,
    )
    d_branch_other = swap(d_branch, "tensor", 1)
    grads_of(2)
    d_branch_other = run.pin(d_branch_other)
    d_all = run(lambda *a: to_relative(stack(*a), my_fsdp, n_fsdp), d_branch, d_branch_other)
    d_all_beside = swap(d_all[:, D // 2 :], "fsdp", 1)
    d_all_beside = run.pin(d_all_beside)
    dq_low, *dkv_parts = run(
        attend_back,
        index, queries, low, high, key_at, cos_table, sin_table,
        (d_branch, d_branch_other), out_w, kv_parts,
    )
    dkv_parts = [dkv_parts[0]] + [
        shift(p, "context", -step - 1) for step, p in enumerate(dkv_parts[1:])
    ]
    other_parts[0] = run.pin(other_parts[0])
    reduced[1] = run(give, *waiting[1])

    def halves(values, axis):
        cut = values.shape[axis] // 2
        return (
            lax.slice_in_dim(values, 0, cut, axis=axis),
            lax.slice_in_dim(values, cut, 2 * cut, axis=axis),
        )

    class Reduce:
        def __init__(self, axis, full, full_beside, split, split_beside):
            self.axis, self.other = axis, 1 - axis
            self.full, self.full_beside = full, full_beside
            self.kept, self.kept_beside = split[:, : D // 2], split_beside
            self.todo = [("fsdp", bit) for bit in bits_of(n_fsdp)[1:]]
            self.todo += [("context", bit) for bit in bits_of(n_ctx)]
            self.back = [bit for bit in reversed(bits_of(n_ctx))]
            self.value = None

        def cut(self, total):
            name, bit = self.todo[0]
            if name == "fsdp":
                keep, send = halves(total, self.axis)
                return keep, send.astype(bf16)
            first, second = halves(total, self.other)
            on = (my_ctx & bit) != 0
            return jnp.where(on, second, first), jnp.where(on, first, second).astype(bf16)

        def send(self, pair):
            name, bit = self.todo.pop(0)
            self.keep, sent = pair
            self.sent = swap(sent, name, bit)

        def first(self):
            def product(full, kept, full_beside, kept_beside):
                left, right = stack(kept, kept_beside), stack(full, full_beside)
                if self.axis == 1:
                    left, right = right, left
                return self.cut(dot_rows(left, right))

            self.send(run(product, self.full, self.kept, self.full_beside, self.kept_beside))

        def step(self):
            if self.todo:
                self.send(run(lambda a, b: self.cut(a + b.astype(f32)), self.keep, self.sent))
                return
            if self.value is None:
                self.value = run(give, self.keep, self.sent)
            else:
                self.value = self.join()
            self.bit = self.back.pop(0)
            self.sent = swap(self.value, "context", self.bit)

        def join(self):
            on = (my_ctx & self.bit) != 0

            def both(mine, other):
                return jnp.concatenate(
                    [jnp.where(on, other, mine), jnp.where(on, mine, other)], axis=self.other
                )

            return run(both, self.value, self.sent)

    def place_part(index, placed):
        return run(
            lambda m, a, b, c: place(m, a, b, index, starts, fresh, ff_local, c),
            member.reshape(1), reduced[index], other_parts[index], placed,
        )

    def smalls(gain_rows, gain_other, grad_bias):
        gain_rows = jnp.pad(gain_rows + gain_other, ((0, 6), (0, 0)))
        biases = jnp.pad(grad_bias.reshape(all_heads, HD), ((0, 0), (0, D - HD)))
        return stack(gain_rows, biases)

    steps = [("fsdp", bit) for bit in bits_of(n_fsdp)] + [("context", bit) for bit in bits_of(n_ctx)]

    def small_step(small):
        name, bit = steps.pop(0)
        return run(jnp.add, small, swap(small, name, bit))

    reduce_o = Reduce(1, attended, attended_beside, d_all, d_all_beside)
    reduce_o.first()
    dkv_parts = dkv_parts[:1] + list(run.pin(tuple(dkv_parts[1:])))
    other_parts[1] = swap(after(reduced[1], dkv_parts[-1]), "context", 1)
    d_qkv, dn_mine, dn_other, grad_bias = run(
        project_back, index, dq_low, cos_table, sin_table, qkv_w, dkv_parts
    )
    d_qkv_beside = swap(d_qkv, "fsdp", 1)
    dn_other = swap(dn_other, "tensor", 1)
    placed = place_part(0, ())
    reduce_qkv = Reduce(0, d_qkv, d_qkv_beside, normed_rel, normed_beside)
    reduce_qkv.first()
    d_inputs, grad_gain_one = run(
        input_back, dn_mine, dn_other, mine_tokens, gains, d_middle
    )
    d_inputs_other = swap(d_inputs, "tensor", 1)
    add_far(2)
    d_inputs_other = run.pin(d_inputs_other)
    other_parts[1] = run.pin(other_parts[1])
    reduce_o.step()
    gain_rows = run(stack, grad_gain_one, grad_gain_two)
    gain_other = swap(gain_rows, "tensor", 1)
    out_far = swap(after(out_far, other_parts[1]), "tensor", 1)
    reduce_qkv.step()
    small = run(smalls, gain_rows, gain_other, grad_bias)
    placed = place_part(1, placed)
    out_mine, out_beside = run(
        lambda a, b, c: (a + c[:half].astype(f32), give(b, c[half:])), out_near, out_beside, out_far
    )
    small = small_step(small)
    small = small_step(small)
    reduce_o.step()
    arrived = reduce_qkv.sent
    reduce_qkv.step()
    out_beside = swap(after(out_beside, arrived), "context", 1)
    other_parts[2] = run.pin(other_parts[2])
    reduce_o.step()
    reduce_qkv.step()
    small = small_step(small)
    reduce_o.step()
    out_half = run(
        lambda a, b, c: (a + b + c.astype(f32)).astype(bf16), middle, out_mine, out_beside
    )
    out_half_other = swap(out_half, "tensor", 1)
    reduce_qkv.step()
    small = small_step(small)
    placed = place_part(2, placed)
    while reduce_o.back:
        reduce_o.step()
        reduce_qkv.step()
    while steps:
        small = small_step(small)
    grad_gate, grad_up, grad_down = placed
    grad_o = reduce_o.join().astype(f32)
    grad_qkv = reduce_qkv.join().astype(f32)
    grad_biases = small[8 : 8 + all_heads, :bias_cols]
    small_gains = small[:2, :shard]
    for f in range(1, n_fsdp):
        there = small[8 : 8 + all_heads, f * bias_cols : (f + 1) * bias_cols]
        grad_biases = jnp.where(my_fsdp == f, there, grad_biases)
        small_gains = jnp.where(my_fsdp == f, small[:2, f * shard : (f + 1) * shard], small_gains)
    def restore(low_half, other_half):
        both = mine_first(stack(low_half, other_half))
        return both.astype(f32)

    return (
        restore(out_half, out_half_other),
        restore(d_inputs, d_inputs_other),
        small_gains[0],
        grad_qkv[:, :q_width],
        grad_biases[:heads_local],
        grad_qkv[:, q_width : q_width + kv_width],
        grad_biases[heads_local : heads_local + 1],
        grad_qkv[:, q_width + kv_width :],
        grad_biases[heads_local + 1 :],
        grad_o,
        small_gains[1],
        grad_gate,
        grad_up,
        grad_down,
    )


def solution(mesh):
    in_specs = (
        P(("fsdp", "context"), None),
        P(("fsdp", "context"), None),
        P("fsdp", None),
        P("fsdp", None, None),
        P("fsdp"),
        P("fsdp", "tensor"),
        P("tensor", "fsdp"),
        P("fsdp", "tensor"),
        P("tensor", "fsdp"),
        P("fsdp", "tensor"),
        P("tensor", "fsdp"),
        P("tensor", "fsdp"),
        P("fsdp"),
        P("fsdp", "tensor"),
        P("fsdp", "tensor"),
        P("tensor", "fsdp"),
    )
    out_specs = (
        P(("fsdp", "context"), None),
        P(("fsdp", "context"), None),
        P("fsdp"),
        P("fsdp", "tensor"),
        P("tensor", "fsdp"),
        P("fsdp", "tensor"),
        P("tensor", "fsdp"),
        P("fsdp", "tensor"),
        P("tensor", "fsdp"),
        P("tensor", "fsdp"),
        P("fsdp"),
        P("fsdp", "tensor"),
        P("fsdp", "tensor"),
        P("tensor", "fsdp"),
    )
    return jax.shard_map(
        per_device, mesh=mesh, in_specs=in_specs, out_specs=out_specs, check_vma=False
    )
```

```python
import functools

import jax
import jax.numpy as jnp
from jax import lax
from jax.experimental import pallas as pl
from jax.experimental.pallas import tpu as pltpu
from jax.sharding import PartitionSpec as P

D = 1536
HD = 128
LANES = 128
TEAM = 2
PARTS = 3
WIDE = 256
SHARED_PARTS = 1

epsilon = 1e-06
rope_base = 10000.0
neg_big = -1e30
far_away = 1 << 29
bf16 = jnp.bfloat16
f32 = jnp.float32


def dot_plain(left_op, right_op):
    return jnp.dot(left_op, right_op, preferred_element_type=f32)


def dot_rows(left_op, right_op):
    return lax.dot_general(
        left_op, right_op, (((0,), (0,)), ((), ())), preferred_element_type=f32
    )


def dot_cols(left_op, right_op):
    return lax.dot_general(
        left_op, right_op, (((1,), (1,)), ((), ())), preferred_element_type=f32
    )


def swap(values, axis_name, bit):
    size = lax.axis_size(axis_name)
    return lax.ppermute(values, axis_name, [(i, i ^ bit) for i in range(size)])


def shift(values, axis_name, step):
    size = lax.axis_size(axis_name)
    pairs = [(i, i + step) for i in range(size) if 0 <= i + step < size]
    return lax.ppermute(values, axis_name, pairs)


def bits_of(size):
    found = []
    bit = 1
    while bit < size:
        found.append(bit)
        bit *= 2
    return found


def fsdp_order(size):
    order = [0]
    for bit in reversed(bits_of(size)):
        order = order + [held ^ bit for held in order]
    return order


def gather_pieces(piece):
    pieces = [piece]
    for bit in reversed(bits_of(lax.axis_size("fsdp"))):
        pieces = pieces + [swap(held, "fsdp", bit) for held in pieces]
    return pieces


def xor_blocks(blocks, index, size):
    for bit in bits_of(size):
        on = (index & bit) != 0
        blocks = [jnp.where(on, blocks[i ^ bit], blocks[i]) for i in range(size)]
    return blocks


def to_relative(values, index, size):
    width = values.shape[-1] // size
    blocks = [values[..., i * width : (i + 1) * width] for i in range(size)]
    blocks = xor_blocks(blocks, index, size)
    return jnp.concatenate([blocks[i] for i in fsdp_order(size)], axis=-1)


def from_relative(values, index, size):
    width = values.shape[-1] // size
    order = fsdp_order(size)
    blocks = [None] * size
    for place, i in enumerate(order):
        blocks[i] = values[..., place * width : (place + 1) * width]
    return jnp.concatenate(xor_blocks(blocks, index, size), axis=-1)


def reduce_fsdp(values, axis):
    for bit in bits_of(lax.axis_size("fsdp")):
        half = values.shape[axis] // 2
        kept = lax.slice_in_dim(values, 0, half, axis=axis)
        sent = lax.slice_in_dim(values, half, 2 * half, axis=axis).astype(bf16)
        values = kept.astype(f32) + swap(sent, "fsdp", bit).astype(f32)
    return values


def sum_context(values):
    index = lax.axis_index("context")
    bits = bits_of(lax.axis_size("context"))
    for bit in bits:
        half = values.shape[0] // 2
        on = (index & bit) != 0
        kept = jnp.where(on, values[half:], values[:half])
        sent = jnp.where(on, values[:half], values[half:]).astype(bf16)
        values = kept + swap(sent, "context", bit).astype(f32)
    values = values.astype(bf16)
    for bit in reversed(bits):
        on = (index & bit) != 0
        other = swap(values, "context", bit)
        values = jnp.concatenate(
            [jnp.where(on, other, values), jnp.where(on, values, other)], axis=0
        )
    return values.astype(f32)


def whole(array):
    return pl.BlockSpec(array.shape, lambda *ids: (0,) * array.ndim)


def wide_enough(pieces, axis):
    if pieces[0].shape[axis] % LANES:
        return [jnp.concatenate(pieces, axis=axis)]
    return pieces


SCALE = 0.2


def cost(us=1):
    return pl.CostEstimate(
        flops=int(us * SCALE * 1.1e9), bytes_accessed=int(us * SCALE * 3.6e6), transcendentals=0
    )


def joined(refs, index_ref, axis, cut=None):
    blocks = [r[...] if cut is None else r[cut] for r in refs]
    if len(blocks) > 1:
        order = fsdp_order(len(blocks))
        blocks = [blocks[order.index(i)] for i in range(len(blocks))]
        blocks = xor_blocks(blocks, index_ref[0], len(blocks))
    return jnp.concatenate(blocks, axis=axis)


def params(mib):
    return pltpu.CompilerParams(vmem_limit_bytes=mib << 20)


def pack_body(count, start_ref, *refs):
    out_ref = refs[-1]
    for i in range(count):
        at = slice(i * LANES, (i + 1) * LANES)
        out_ref[0, :, at] = refs[i][...].astype(bf16)
        out_ref[1, :, at] = refs[count + i][...].astype(bf16)
        out_ref[2, :, at] = refs[2 * count + i][...].T.astype(bf16)


def pack(w_gate, w_up, w_down, start, width):
    shard = w_gate.shape[0]
    count = width // LANES
    columns = [pl.BlockSpec((shard, LANES), lambda j, s, i=i: (0, s[0] + i)) for i in range(count)]
    lines = [pl.BlockSpec((LANES, shard), lambda j, s, i=i: (s[0] + i, 0)) for i in range(count)]
    spec = pltpu.PrefetchScalarGridSpec(
        num_scalar_prefetch=1,
        grid=(1,),
        in_specs=columns + columns + lines,
        out_specs=pl.BlockSpec((3, shard, width), lambda j, s: (0, 0, 0)),
    )
    return pl.pallas_call(
        functools.partial(pack_body, count),
        out_shape=jax.ShapeDtypeStruct((3, shard, width), bf16),
        grid_spec=spec,
        cost_estimate=cost(),
        compiler_params=params(60),
    )(start, *[w_gate] * count, *[w_up] * count, *[w_down] * count)


def qkv_pack_body(index_ref, g1_ref, g2_ref, bq_ref, bk_ref, bv_ref, wq_ref, wk_ref, wv_ref, out_ref):
    shard, at = wq_ref.shape[0], 0
    for ref in (wq_ref, wk_ref, wv_ref):
        out_ref[:shard, at : at + ref.shape[1]] = ref[...].astype(bf16)
        at += ref.shape[1]
    row = lax.broadcasted_iota(jnp.int32, (16, shard), 0)
    first, second = g1_ref[...][None, :], g2_ref[...][None, :]
    gains = jnp.where(row == 0, first, jnp.where(row == 1, second, 0.0))
    columns = bq_ref.shape[1]
    from_column = lax.broadcasted_iota(jnp.int32, (columns, HD), 0)
    to_column = lax.broadcasted_iota(jnp.int32, (columns, HD), 1)
    spread = (to_column == from_column + columns * index_ref[0]).astype(bf16)
    biases, at = 0.0, 8
    for ref in (bq_ref, bk_ref, bv_ref):
        heads = ref.shape[0]
        to_row = lax.broadcasted_iota(jnp.int32, (16, heads), 0)
        from_row = lax.broadcasted_iota(jnp.int32, (16, heads), 1) + at
        wide = dot_plain(ref[...].astype(bf16), spread).astype(bf16)
        if heads == 1:
            row = lax.broadcasted_iota(jnp.int32, (16, HD), 0)
            biases = biases + jnp.where(row == at, wide.astype(f32), 0.0)
        else:
            biases = biases + dot_plain((to_row == from_row).astype(bf16), wide)
        at += heads
    out_ref[shard:, :] = jnp.zeros((16, out_ref.shape[1]), bf16)
    out_ref[shard:, :HD] = (gains[:, :HD] + biases).astype(bf16)
    out_ref[shard:, HD:shard] = gains[:, HD:].astype(bf16)


def qkv_pack(index, g1, g2, b_q, b_k, b_v, w_q, w_k, w_v):
    width = w_q.shape[1] + w_k.shape[1] + w_v.shape[1]
    inputs = (g1, g2, b_q, b_k, b_v, w_q, w_k, w_v)
    return pl.pallas_call(
        qkv_pack_body,
        out_shape=jax.ShapeDtypeStruct((w_q.shape[0] + 16, width), bf16),
        in_specs=[pl.BlockSpec(memory_space=pltpu.SMEM)] + [pl.BlockSpec(memory_space=pltpu.VMEM)] * len(inputs),
        cost_estimate=cost(2),
        compiler_params=params(60),
    )(index, *inputs)


def vectors_body(count, heads, index_ref, *refs):
    gain_ref, bias_ref = refs[count:]
    width = D // count
    gain_ref[...] = joined(refs[:count], index_ref, 1, (slice(0, 2), slice(0, width)))
    bias_ref[...] = sum(r[8 : 8 + heads, :HD].astype(f32) for r in refs[:count])


def vectors(index, pieces, heads):
    shard = D // len(pieces)
    if shard % LANES:
        order = fsdp_order(len(pieces))
        blocks = [pieces[order.index(i)][shard : shard + 2, :shard] for i in range(len(pieces))]
        gains = jnp.concatenate(xor_blocks(blocks, index[0], len(pieces)), axis=1)
        return gains, sum(p[shard + 8 : shard + 8 + heads, :HD].astype(f32) for p in pieces)
    rows = pl.BlockSpec((16, pieces[0].shape[1]), lambda i: (shard // 16, 0))
    outs = (jax.ShapeDtypeStruct((2, D), bf16), jax.ShapeDtypeStruct((heads, HD), f32))
    return pl.pallas_call(
        functools.partial(vectors_body, len(pieces), heads),
        out_shape=outs,
        grid=(1,),
        in_specs=[pl.BlockSpec(memory_space=pltpu.SMEM)] + [rows] * len(pieces),
        out_specs=tuple(whole(a) for a in outs),
        cost_estimate=cost(),
        compiler_params=params(60),
    )(index, *pieces)


def project_body(count, q_width, index_ref, a_ref, b_ref, gain_ref, bias_ref, cos_ref, sin_ref, *refs):
    w_refs, (q_ref, kv_ref, h_ref) = refs[:count], refs[count:]
    x = jnp.concatenate([a_ref[...], b_ref[...]], axis=0).astype(f32)
    scale = lax.rsqrt(jnp.mean(x * x, axis=-1, keepdims=True) + epsilon)
    normed = (x * scale * gain_ref[0:1].astype(f32)).astype(bf16)
    h_ref[...] = normed
    total = w_refs[0].shape[1]
    depth = D // count
    for at in range(0, total, WIDE):
        weights = joined(w_refs, index_ref, 0, (slice(0, depth), slice(at, at + WIDE)))
        both = dot_plain(normed, weights)
        for inner in range(0, WIDE, HD):
            place = at + inner
            head = place // HD
            values = both[:, inner : inner + HD] + bias_ref[head : head + 1]
            if place < total - HD:
                turned = pltpu.roll(values, HD // 2, 1)
                values = values * cos_ref[...] + turned * sin_ref[...]
            if place < q_width:
                q_ref[:, place : place + HD] = values.astype(bf16)
            else:
                kv_ref[:, place - q_width : place - q_width + HD] = values.astype(bf16)


def project(index, first, second, gain, bias, cos_table, sin_table, weights, q_width):
    rows = 2 * first.shape[0]
    total = weights[0].shape[1]
    return pl.pallas_call(
        functools.partial(project_body, len(weights), q_width),
        out_shape=(
            jax.ShapeDtypeStruct((rows, q_width), bf16),
            jax.ShapeDtypeStruct((rows, total - q_width), bf16),
            jax.ShapeDtypeStruct((rows, D), bf16),
        ),
        in_specs=[pl.BlockSpec(memory_space=pltpu.SMEM)] + [pl.BlockSpec(memory_space=pltpu.VMEM)] * (6 + len(weights)),
        cost_estimate=cost(4),
        compiler_params=params(60),
    )(index, first, second, gain, bias, cos_table, sin_table, *weights)


def masked_weights(queries, keys, low_ref, high_ref, key_ref):
    scores = dot_cols(queries, keys) * HD ** (-0.5)
    key_at = key_ref[...]
    allowed = (key_at >= low_ref[...]) & (key_at <= high_ref[...])
    scores = jnp.where(allowed, scores, neg_big)
    top = jnp.max(scores, axis=-1, keepdims=True)
    raised = jnp.exp(scores - top)
    return raised * (1.0 / jnp.sum(raised, axis=-1, keepdims=True))


def attend_body(count, ahead, index_ref, q_ref, low_ref, high_ref, key_ref, *refs):
    w_refs, kv_refs = refs[:count], refs[count : count + ahead]
    o_ref, mine_ref, other_ref = refs[count + ahead :]
    keys = jnp.concatenate([kv[:, :HD] for kv in kv_refs], axis=0)
    values = jnp.concatenate([kv[:, HD:] for kv in kv_refs], axis=0)
    weights = masked_weights(q_ref[...], keys, low_ref, high_ref, key_ref)
    head = pl.program_id(0)
    out = dot_plain(weights.astype(bf16), values).astype(bf16)
    o_ref[:, pl.ds(pl.multiple_of(head * HD, HD), HD)] = out

    @pl.when(head == pl.num_programs(0) - 1)
    def _():
        half = mine_ref.shape[0]
        out_w = joined(w_refs, index_ref, 1)
        branch = dot_plain(o_ref[...], out_w)
        mine_ref[...] = branch[:half]
        other_ref[...] = branch[half:].astype(bf16)


def attend(index, queries, low, high, key_at, weights, kv_parts):
    rows, width = queries.shape
    head = pl.BlockSpec((rows, HD), lambda h: (0, h))
    keys = key_at.shape[1]
    rest = (low, high, key_at, *weights, *kv_parts)
    outs = (
        jax.ShapeDtypeStruct(queries.shape, bf16),
        jax.ShapeDtypeStruct((rows // 2, D), f32),
        jax.ShapeDtypeStruct((rows // 2, D), bf16),
    )
    return pl.pallas_call(
        functools.partial(attend_body, len(weights), len(kv_parts)),
        out_shape=outs,
        grid=(width // HD,),
        in_specs=[pl.BlockSpec(memory_space=pltpu.SMEM), head] + [whole(a) for a in rest],
        out_specs=tuple(whole(a) for a in outs),
        compiler_params=params(60),
        cost_estimate=cost(8),
    )(index, queries, *rest)


def middle_body(x_ref, mine_ref, other_ref, gain_ref, mid_ref, h_ref):
    middle = x_ref[...].astype(f32) + mine_ref[...] + other_ref[...].astype(f32)
    scale = lax.rsqrt(jnp.mean(middle * middle, axis=-1, keepdims=True) + epsilon)
    mid_ref[...] = middle
    h_ref[...] = (middle * scale * gain_ref[1:2].astype(f32)).astype(bf16)


def middle_norm(x, mine, other, gain):
    return pl.pallas_call(
        middle_body,
        out_shape=(jax.ShapeDtypeStruct(mine.shape, f32), jax.ShapeDtypeStruct(mine.shape, bf16)),
        cost_estimate=cost(),
        compiler_params=params(60),
    )(x, mine, other, gain)


def feed_body(
    count, bases, back, carried, last, filled, at_row, limit_ref, ctx_ref, *refs
):
    h_refs, refs = refs[: 2 * len(bases)], refs[2 * len(bases) :]
    (g_own, g_across, w_hbm), refs = refs[:3], refs[3:]
    carry, refs = refs[: 2 * carried], refs[2 * carried + filled :]
    bufs = None
    if carried:
        outs, (w_ref, act_ref, sems, bufs) = refs[:-4], refs[-4:]
    else:
        outs, (w_ref, act_ref, sems) = refs[:-3], refs[-3:]
    rows, width = act_ref.shape[1:]
    tiles = 3
    loads = [
        pltpu.make_async_copy(w_hbm.at[:, k], w_ref.at[:, k], sems.at[k]) for k in range(tiles)
    ]
    carries = [
        pltpu.make_async_copy(ref, bufs.at[k], sems.at[tiles + k]) for k, ref in enumerate(carry)
    ]
    for copy in loads + carries:
        copy.start()
    half = g_own.shape[1]
    chunk = 2 * half
    lane = lax.broadcasted_iota(jnp.int32, (1, width), 1)
    shown = lane >= limit_ref[0]

    def weights(k):
        return jnp.concatenate([w_ref[i, k] for i in range(count)], axis=0)

    at = 0
    for which, h_ref in enumerate(h_refs):
        base, g_ref = bases[which // 2], (g_own, g_across)[which % 2]
        for j in range(h_ref.shape[0] // chunk):
            rows_in = h_ref[j * chunk : (j + 1) * chunk]
            grads_in = jnp.concatenate(
                [g_ref[ctx_ref[0] ^ (base + 2 * j + k)] for k in range(2)], axis=0
            )
            if at == 0:
                loads[0].wait()
            gate = dot_plain(rows_in, weights(0))
            if at == 0:
                loads[1].wait()
            up = dot_plain(rows_in, weights(1))
            if at == 0:
                loads[2].wait()
            d_hidden = dot_plain(grads_in, weights(2))
            gate_sig = jax.nn.sigmoid(gate)
            activated = gate * gate_sig
            hidden = activated * up
            d_gate = d_hidden * up * gate_sig * (1.0 + gate * (1.0 - gate_sig))
            d_up = d_hidden * activated
            act_ref[0, at : at + chunk] = jnp.where(shown, d_gate, 0.0).astype(bf16)
            act_ref[1, at : at + chunk] = jnp.where(shown, d_up, 0.0).astype(bf16)
            act_ref[2, at : at + chunk] = jnp.where(shown, hidden, 0.0).astype(bf16)
            at += chunk
    at = tiles + len(carries)
    copies = [
        pltpu.make_async_copy(act_ref.at[k], outs[k].at[pl.ds(at_row, rows)], sems.at[at + k])
        for k in range(3)
    ]
    for copy in copies:
        copy.start()
    if back:
        team = slice(0, 4 * half)
        d_rows = dot_cols(act_ref[0, team], weights(0)) + dot_cols(act_ref[1, team], weights(1))
        out_rows = dot_cols(act_ref[2, team], weights(2))
        for copy in carries:
            copy.wait()
        if carried:
            d_rows = d_rows + bufs[0]
            out_rows = out_rows + bufs[1]
        if last:
            cuts = ((0, half), (half, 2 * half), (2 * half, 4 * half))
            for group, total in ((outs[3:6], d_rows), (outs[6:], out_rows)):
                for ref, (low, high) in zip(group, cuts):
                    ref[...] = total[low:high].astype(ref.dtype)
        else:
            outs[3][...] = d_rows
            outs[4][...] = out_rows
    for copy in copies:
        copy.wait()


def feed(limit, ctx, rows_in, grads_in, weights, total, back, carry=(), last=False, act=None):
    some = sum(r.shape[0] for r in rows_in)
    width = weights.shape[3]
    outs = [jax.ShapeDtypeStruct((total, width), bf16)] * 3
    half = grads_in[0].shape[1]
    if back and last:
        group = [jax.ShapeDtypeStruct((half, D), f32)] * 2
        outs += (group + [jax.ShapeDtypeStruct((2 * half, D), bf16)]) * 2
    elif back:
        outs += [jax.ShapeDtypeStruct((4 * half, D), f32)] * 2
    vmem = pl.BlockSpec(memory_space=pltpu.VMEM)
    smem = pl.BlockSpec(memory_space=pltpu.SMEM)
    hbm = pl.BlockSpec(memory_space=pl.ANY)
    inputs = (*rows_in, *grads_in)
    filled = () if act is None else tuple(act)
    scratch = [
        pltpu.VMEM(weights.shape, bf16),
        pltpu.VMEM((3, some, width), bf16),
        pltpu.SemaphoreType.DMA((6 + len(carry),)),
    ]
    if carry:
        scratch.append(pltpu.VMEM((2, 4 * half, D), f32))
    first = 3 + len(inputs) + len(carry)
    return pl.pallas_call(
        functools.partial(
            feed_body, weights.shape[0],
            ((0,) if back else ()) + ((TEAM,) if some == total or not back else ()),
            back, len(carry) // 2, last, len(filled), 0 if back else total - some,
        ),
        out_shape=tuple(outs),
        in_specs=[smem, smem] + [vmem] * len(inputs) + [hbm] * (1 + len(carry) + len(filled)),
        out_specs=tuple([hbm] * 3 + [vmem] * (len(outs) - 3)),
        scratch_shapes=scratch,
        input_output_aliases={first + k: k for k in range(len(filled))},
        compiler_params=params(60),
        cost_estimate=cost((6 if back else 0) + 9 * some / 512),
    )(limit, ctx, *inputs, weights, *carry, *filled)


def turn_body(blocks, dynamic, contexts, index_ref, ctx_ref, *refs):
    kept_ref, sent_ref = refs[-2:]
    width = D // blocks
    order = fsdp_order(blocks)
    values = [(ref, None) for ref in refs[:-2]]
    if contexts:
        groups = (range(TEAM), range(TEAM, contexts))
        values = [(ref, ctx_ref[0] ^ k) for group in groups for ref in refs[:-2] for k in group]
    at = 0
    for ref, which in values:
        value = ref[...] if which is None else ref[which]
        here = slice(at, at + value.shape[0])
        at += value.shape[0]
        parts = [value[:, i * width : (i + 1) * width] for i in range(blocks)]
        if dynamic:
            parts = xor_blocks(parts, index_ref[0], blocks)
            parts = [parts[i] for i in order]
        for spot in range(blocks // 2):
            lines_at = slice(spot * width, (spot + 1) * width)
            kept_ref[lines_at, here] = parts[spot].T
            sent_ref[lines_at, here] = parts[blocks // 2 + spot].T


def turn_rows(index, ctx, rows, n_fsdp):
    total = sum(r.size for r in rows) // D
    contexts = rows[0].shape[0] if rows[0].ndim == 3 else 0
    blocks = n_fsdp
    if D // n_fsdp % LANES:
        blocks = 2
        rows = [to_relative(v, index[0], n_fsdp) for v in rows]
    return pl.pallas_call(
        functools.partial(turn_body, blocks, blocks == n_fsdp, contexts),
        out_shape=(jax.ShapeDtypeStruct((D // 2, total), bf16),) * 2,
        in_specs=[pl.BlockSpec(memory_space=pltpu.SMEM), pl.BlockSpec(memory_space=pltpu.SMEM)] + [pl.BlockSpec(memory_space=pltpu.VMEM)] * len(rows),
        cost_estimate=cost(4),
        compiler_params=params(60),
    )(index, ctx, *rows)


def weight_body(*refs):
    own, beside, acts = refs[:2], refs[2:4], refs[4:7]
    acts_beside, (near_ref, far_ref) = refs[7:10], refs[10:]
    cut = near_ref.shape[1]
    for k in range(3):
        value = dot_plain(own[k // 2][...], acts[k][...])
        value = value + dot_plain(beside[k // 2][...], acts_beside[k][...])
        near_ref[k] = value[:cut].astype(bf16)
        far_ref[k] = value[cut:].astype(bf16)


def weight_grads(own, beside, acts, acts_beside):
    total, width = acts[0].shape
    left = pl.BlockSpec(own[0].shape, lambda j: (0, 0), pipeline_mode=pl.Buffered(1))
    right = pl.BlockSpec((total, WIDE), lambda j: (0, j))
    out = pl.BlockSpec((3, D // 4, WIDE), lambda j: (0, 0, j))
    return pl.pallas_call(
        weight_body,
        out_shape=(jax.ShapeDtypeStruct((3, D // 4, width), bf16),) * 2,
        grid=(width // WIDE,),
        in_specs=[left] * 4 + [right] * 6,
        out_specs=(out, out),
        compiler_params=params(60),
        cost_estimate=cost(12),
    )(*own, *beside, *acts, *acts_beside)


def middle_back_body(
    near_ref, across_ref, far_ref, mid_ref, gain_ref, g_ref, d_ref, low_ref, gain_out
):
    d_normed = near_ref[...] + across_ref[...].astype(f32) + far_ref[...].astype(f32)
    middle = mid_ref[...]
    scale = lax.rsqrt(jnp.mean(middle * middle, axis=-1, keepdims=True) + epsilon)
    gain_out[...] = jnp.sum(d_normed * middle * scale, axis=0, keepdims=True)
    weighted = d_normed * gain_ref[1:2].astype(f32)
    inner = jnp.mean(weighted * middle, axis=-1, keepdims=True)
    d_middle = g_ref[...].astype(f32) + scale * weighted - middle * scale**3 * inner
    d_ref[...] = d_middle
    low_ref[...] = d_middle.astype(bf16)


def middle_back(near, across, far, middle, gain, grads):
    return pl.pallas_call(
        middle_back_body,
        out_shape=(
            jax.ShapeDtypeStruct(near.shape, f32),
            jax.ShapeDtypeStruct(near.shape, bf16),
            jax.ShapeDtypeStruct((1, D), f32),
        ),
        cost_estimate=cost(),
        compiler_params=params(60),
    )(near, across, far, middle, gain, grads)


def attend_back_body(count, ahead, index_ref, q_ref, low_ref, high_ref, key_ref, cos_ref, sin_ref, *refs):
    scale = HD ** (-0.5)
    mine_ref, other_ref = refs[:2]
    w_refs, kv_refs = refs[2 : 2 + count], refs[2 + count : 2 + count + ahead]
    outs = refs[2 + count + ahead :]
    dq_ref, dkv_refs, (d_o, sums) = outs[0], outs[1 : 1 + ahead], outs[1 + ahead :]
    head = pl.program_id(0)

    @pl.when(head == 0)
    def _():
        d_branch = jnp.concatenate([mine_ref[...], other_ref[...]], axis=0)
        out_w = joined(w_refs, index_ref, 1)
        d_o[...] = dot_cols(d_branch, out_w).astype(bf16)
        sums[...] = jnp.zeros_like(sums)

    queries = q_ref[...]
    grad = d_o[:, pl.ds(pl.multiple_of(head * HD, HD), HD)]
    keys = jnp.concatenate([kv[:, :HD] for kv in kv_refs], axis=0)
    values = jnp.concatenate([kv[:, HD:] for kv in kv_refs], axis=0)
    weights = masked_weights(queries, keys, low_ref, high_ref, key_ref)
    dweights = dot_cols(grad, values)
    delta = jnp.sum(weights * dweights, axis=-1, keepdims=True)
    dscores = (weights * (dweights - delta)).astype(bf16)
    dq_rot = dot_plain(dscores, keys) * scale
    turned = pltpu.roll(dq_rot, HD // 2, 1)
    dq_ref[...] = (dq_rot * cos_ref[...] - turned * sin_ref[...]).astype(bf16)
    sums[:, :HD] += dot_rows(dscores, queries) * scale
    sums[:, HD:] += dot_rows(weights.astype(bf16), grad)

    @pl.when(head == pl.num_programs(0) - 1)
    def _():
        rows = q_ref.shape[0]
        for i, out in enumerate(dkv_refs):
            out[...] = sums[i * rows : (i + 1) * rows].astype(out.dtype)


def attend_back(index, queries, low, high, key_at, cos_table, sin_table, grads, weights, kv_parts):
    rows, width = queries.shape
    head = pl.BlockSpec((rows, HD), lambda h: (0, h))
    keys = key_at.shape[1]
    rest = (low, high, key_at, cos_table, sin_table, *grads, *weights, *kv_parts)
    outs = [jax.ShapeDtypeStruct(queries.shape, bf16)]
    outs += [
        jax.ShapeDtypeStruct(kv.shape, bf16 if i else f32) for i, kv in enumerate(kv_parts)
    ]
    return pl.pallas_call(
        functools.partial(attend_back_body, len(weights), len(kv_parts)),
        out_shape=tuple(outs),
        grid=(width // HD,),
        in_specs=[pl.BlockSpec(memory_space=pltpu.SMEM), head] + [whole(a) for a in rest],
        out_specs=tuple([head] + [whole(a) for a in outs[1:]]),
        scratch_shapes=[pltpu.VMEM((rows, width), bf16), pltpu.VMEM((keys, 2 * HD), f32)],
        compiler_params=params(60),
        cost_estimate=cost(10),
    )(index, queries, *rest)


def project_back_body(count, ahead, index_ref, dq_ref, cos_ref, sin_ref, *refs):
    w_refs, dkv_refs = refs[:count], refs[count : count + ahead]
    d_ref, mine_ref, other_ref, bias_ref = refs[count + ahead :]
    total = dkv_refs[0][...]
    for extra in dkv_refs[1:]:
        total = total + extra[...].astype(f32)
    dk = total[:, :HD]
    dk = dk * cos_ref[...] - pltpu.roll(dk, HD // 2, 1) * sin_ref[...]
    d_low = jnp.concatenate([dq_ref[...], dk.astype(bf16), total[:, HD:].astype(bf16)], axis=1)
    d_ref[...] = d_low
    bias_ref[...] = jnp.sum(d_low.astype(f32), axis=0, keepdims=True)
    weights = joined(w_refs, index_ref, 0, slice(0, D // count))
    d_normed = dot_cols(d_low, weights)
    half = mine_ref.shape[0]
    mine_ref[...] = d_normed[:half]
    other_ref[...] = d_normed[half:].astype(bf16)


def project_back(index, dq, cos_table, sin_table, weights, dkv_parts):
    rows = dq.shape[0]
    total = weights[0].shape[1]
    return pl.pallas_call(
        functools.partial(project_back_body, len(weights), len(dkv_parts)),
        out_shape=(
            jax.ShapeDtypeStruct((rows, total), bf16),
            jax.ShapeDtypeStruct((rows // 2, D), f32),
            jax.ShapeDtypeStruct((rows // 2, D), bf16),
            jax.ShapeDtypeStruct((1, total), f32),
        ),
        in_specs=[pl.BlockSpec(memory_space=pltpu.SMEM)] + [pl.BlockSpec(memory_space=pltpu.VMEM)] * (3 + len(weights) + len(dkv_parts)),
        cost_estimate=cost(4),
        compiler_params=params(60),
    )(index, dq, cos_table, sin_table, *weights, *dkv_parts)


def input_back_body(mine_ref, other_ref, x_ref, gain_ref, mid_ref, d_ref, gain_out):
    d_normed = mine_ref[...] + other_ref[...].astype(f32)
    x = x_ref[...].astype(f32)
    scale = lax.rsqrt(jnp.mean(x * x, axis=-1, keepdims=True) + epsilon)
    gain_out[...] = jnp.sum(d_normed * x * scale, axis=0, keepdims=True)
    weighted = d_normed * gain_ref[0:1].astype(f32)
    inner = jnp.mean(weighted * x, axis=-1, keepdims=True)
    d_ref[...] = (mid_ref[...] + scale * weighted - x * scale**3 * inner).astype(bf16)


def input_back(mine, other, x, gain, d_middle):
    return pl.pallas_call(
        input_back_body,
        out_shape=(jax.ShapeDtypeStruct(mine.shape, bf16), jax.ShapeDtypeStruct((1, D), f32)),
        cost_estimate=cost(),
        compiler_params=params(60),
    )(mine, other, x, gain, d_middle)


def place_body(plan, carried, member_ref, *refs):
    own_ref, other_ref, refs = refs[0], refs[1], refs[2:]
    outs = refs[carried : carried + 3]
    wide_buf, tall_buf, sems = refs[carried + 3 :]
    width = own_ref.shape[2]

    def copies(team):
        skip, at = plan[team]
        size = width - skip
        for k in range(2):
            yield pltpu.make_async_copy(
                wide_buf.at[team, k, :, pl.ds(skip, size)],
                outs[k].at[:, pl.ds(at + skip, size)],
                sems.at[team, k],
            )
        yield pltpu.make_async_copy(
            tall_buf.at[team, pl.ds(skip, size)],
            outs[2].at[pl.ds(at + skip, size)],
            sems.at[team, 2],
        )

    for team in range(len(plan)):
        def put(ref, team=team):
            wide_buf[team, 0] = ref[0].astype(f32)
            wide_buf[team, 1] = ref[1].astype(f32)
            tall_buf[team] = ref[2].astype(f32).T

        @pl.when(member_ref[0] == team)
        def _():
            put(own_ref)

        @pl.when(member_ref[0] != team)
        def _():
            put(other_ref)

        for copy in copies(team):
            copy.start()
    for team in range(len(plan)):
        for copy in copies(team):
            copy.wait()


def place(member, own, other, index, starts, fresh, ff_local, carry):
    shard, width = own.shape[1:]
    plan = tuple(
        (min(max(fresh[s] - index * width, 0), width), starts[s] + index * width)
        for s in range(TEAM)
    )
    hbm = pl.BlockSpec(memory_space=pl.ANY)
    vmem = pl.BlockSpec(memory_space=pltpu.VMEM)
    return pl.pallas_call(
        functools.partial(place_body, plan, len(carry)),
        out_shape=(
            jax.ShapeDtypeStruct((shard, ff_local), f32),
            jax.ShapeDtypeStruct((shard, ff_local), f32),
            jax.ShapeDtypeStruct((ff_local, shard), f32),
        ),
        in_specs=[pl.BlockSpec(memory_space=pltpu.SMEM)] + [vmem] * 2 + [hbm] * len(carry),
        out_specs=(hbm, hbm, hbm),
        scratch_shapes=[
            pltpu.VMEM((TEAM, 2, shard, width), f32),
            pltpu.VMEM((TEAM, width, shard), f32),
            pltpu.SemaphoreType.DMA((TEAM, 3)),
        ],
        input_output_aliases={3 + i: i for i in range(len(carry))},
        cost_estimate=cost(),
        compiler_params=params(60),
    )(member, own, other, *carry)


def after(values, *first):
    return lax.optimization_barrier((values, first))[0]


class Order:
    def __init__(self):
        self.last = ()

    def __call__(self, step, *args):
        args, _ = lax.optimization_barrier((args, self.last))
        result = step(*args)
        self.last = (jax.tree.leaves(result)[0],)
        return result

    def pin(self, values):
        values, _ = lax.optimization_barrier((values, self.last))
        self.last = (jax.tree.leaves(values)[0],)
        return values


def stack(*pieces):
    return jnp.concatenate(pieces, axis=0)


class Pieces:
    def __init__(self, run, full, *first):
        bits = list(reversed(bits_of(lax.axis_size("fsdp"))))
        self.run, self.near = run, bits[-1]
        self.held = [full]
        gate = after(full, *first)
        for bit in bits[:-1]:
            self.held = self.held + [swap(p, "fsdp", bit) for p in [gate] + self.held[1:]]

    def turn(self):
        self.held = self.held[:1] + list(self.run.pin(tuple(self.held[1:])))
        self.sent = swap(self.run(lambda *a: jnp.stack(a), *self.held), "fsdp", self.near)
        return self.held[-1]

    def finish(self):
        self.sent = self.run.pin(self.sent)

    def pieces(self):
        return self.held + [self.sent[i] for i in range(len(self.held))]


def per_device(
    tokens,
    cotangent,
    lengths,
    span_order,
    attn_gain,
    w_q,
    b_q,
    w_k,
    b_k,
    w_v,
    b_v,
    w_o,
    mlp_gain,
    w_gate,
    w_up,
    w_down,
):
    n_fsdp = lax.axis_size("fsdp")
    n_ctx = lax.axis_size("context")
    my_fsdp = lax.axis_index("fsdp")
    my_ctx = lax.axis_index("context")
    my_tensor = lax.axis_index("tensor")
    member = my_ctx % TEAM
    rows = tokens.shape[0]
    half = rows // 2
    piece_rows = rows // n_ctx
    shard = D // n_fsdp
    q_width = w_q.shape[1]
    kv_width = w_k.shape[1]
    qkv_width = q_width + 2 * kv_width
    heads_local = q_width // HD
    all_heads = qkv_width // HD
    flipped = my_tensor != 0
    run = Order()
    sharing = n_fsdp == 4 and n_ctx % 2 == 0

    def mine_first(values):
        first, second = values[:half], values[half:]
        return stack(jnp.where(flipped, second, first), jnp.where(flipped, first, second))

    bias_cols = HD // n_fsdp

    index = my_fsdp.astype(jnp.int32).reshape(1)
    qkv_h = Pieces(
        run, run(qkv_pack, index, attn_gain, mlp_gain, b_q, b_k, b_v, w_q, w_k, w_v)
    )
    out_cast = run(lambda w: w.astype(bf16), w_o)

    def arrange(values):
        both = mine_first(values)
        return both[:half], both[half:]

    class Rows:
        def __init__(self, mine):
            self.mine = mine
            self.beside = swap(mine, "context", 1)

        def turn(self):
            self.beside = run.pin(self.beside)
            self.held = run(stack, self.mine, self.beside)
            self.held_across = swap(self.held, "tensor", 1)
            held, others = self.held, []
            for bit in bits_of(n_ctx)[1:]:
                there = swap(held, "context", bit)
                others.append(there)
                held = stack(held, there)
            self.remote = others[0] if len(others) == 1 else stack(*others)

        def across_rest(self):
            self.remote = run.pin(self.remote)
            self.remote_across = swap(self.remote, "tensor", 1)

        def pin_team(self):
            self.held_across = run.pin(self.held_across)

        def pin_rest(self):
            self.remote_across = run.pin(self.remote_across)

        def team(self):
            return (self.held, self.held_across)

        def rest(self):
            return (self.remote, self.remote_across)

    grad_mine, _ = run(arrange, cotangent)
    grads_own = lax.all_gather(grad_mine, "context")

    ff_local = w_gate.shape[1]
    tiles = ff_local // LANES
    unit = PARTS * WIDE // LANES
    slice_tiles = -(-tiles // (TEAM * unit)) * unit
    part = slice_tiles // PARTS * LANES
    starts = [min(s * slice_tiles, tiles - slice_tiles) * LANES for s in range(TEAM)]
    fresh = [s * slice_tiles * LANES - starts[s] for s in range(TEAM)]
    my_start = jnp.int32(starts[0] // LANES)
    limit = jnp.int32(fresh[0])
    for s in range(1, TEAM):
        my_start = jnp.where(member == s, starts[s] // LANES, my_start)
        limit = jnp.where(member == s, fresh[s], limit)

    def packed(index):
        start = (my_start + index * (part // LANES)).reshape(1)
        return run(lambda *a: pack(*a, part), w_gate, w_up, w_down, start)

    longest = 3 * n_ctx * rows // 8
    behind = min(n_ctx - 1, (longest - 1 + rows - 1) // rows)
    half_dim = HD // 2

    def places(lengths, span_order):
        seq_ends = jnp.cumsum(lengths[0])
        row = jnp.arange(rows, dtype=jnp.int32)
        stored = jnp.where(flipped, (row + half) % rows, row)

        def packed_of(context):
            owner = lax.dynamic_index_in_dim(span_order[0], context, 0, keepdims=False)
            span = stored // piece_rows
            hot = span[:, None] == jnp.arange(n_ctx, dtype=jnp.int32)[None, :]
            spot = jnp.sum(jnp.where(hot, owner[None, :], 0), axis=1)
            return context * rows + spot * piece_rows + stored % piece_rows

        own_at = packed_of(my_ctx)
        passed = own_at[:, None] >= seq_ends[None, :]
        begin = jnp.max(jnp.where(passed, seq_ends[None, :], 0), axis=1)
        position = own_at - begin
        key_at = [own_at]
        for step in range(1, behind + 1):
            there = packed_of(jnp.maximum(my_ctx - step, 0))
            key_at.append(jnp.where(my_ctx >= step, there, far_away))
        frequency = rope_base ** (-(jnp.arange(half_dim, dtype=f32) * 2.0) / HD)
        angles = position.astype(f32)[:, None] * frequency[None, :]
        cosine, sine = jnp.cos(angles), jnp.sin(angles)
        return (
            begin[:, None],
            own_at[:, None],
            jnp.concatenate(key_at)[None, :],
            jnp.concatenate([cosine, cosine], axis=1),
            jnp.concatenate([-sine, sine], axis=1),
        )

    ctx = my_ctx.astype(jnp.int32).reshape(1)
    feed_in = [packed(0)]
    mine_tokens, other_tokens = run(arrange, tokens)
    feed_in.append(packed(1))
    far = qkv_h.turn()
    out_h = Pieces(run, out_cast, far)
    feed_in += [packed(i) for i in range(2, PARTS)]
    feed_w = [lax.all_gather(after(v, far), "fsdp") for v in feed_in]
    low, high, key_at, cos_table, sin_table = run(places, lengths, span_order)
    qkv_h.finish()

    def in_order(pieces, axis, cut=None):
        if shard % LANES == 0:
            return pieces
        order = fsdp_order(n_fsdp)
        blocks = [pieces[order.index(i)] for i in range(n_fsdp)]
        blocks = [b if cut is None else b[:cut] for b in blocks]
        return [jnp.concatenate(xor_blocks(blocks, my_fsdp, n_fsdp), axis=axis)]

    gains, bias = run(lambda i, p: vectors(i, p, all_heads), index, qkv_h.pieces())
    qkv_w = in_order(qkv_h.pieces(), 0, shard)

    queries, kv_own, normed = run(
        lambda *a: project(*a, q_width),
        index, mine_tokens, other_tokens, gains, bias, cos_table, sin_table, qkv_w,
    )
    kv_parts = [kv_own] + [shift(kv_own, "context", step) for step in range(1, behind + 1)]
    grads_own = run.pin(grads_own)
    grads = (grads_own, swap(grads_own, "tensor", 1))
    normed_rel = run(lambda v: to_relative(v, my_fsdp, n_fsdp), normed)
    out_h.turn()
    kv_parts = [kv_own] + list(run.pin(tuple(kv_parts[1:])))
    out_h.finish()
    out_w = in_order(out_h.pieces(), 1)
    branch_mine, attended, branch_other = run(
        lambda *a: (lambda o, m, s: (m, o, s))(*attend(*a)),
        index, queries, low, high, key_at, out_w, kv_parts,
    )
    branch_other = swap(branch_other, "tensor", 1)
    sent = run(lambda a, b: jnp.concatenate([a, b[:, D // 2 :]], axis=1), attended, normed_rel)
    early_beside = swap(sent, "fsdp", 1)
    grads = run.pin(grads)
    middle, normed_two = run(
        middle_norm, mine_tokens, branch_mine, branch_other, gains
    )
    lines = Rows(normed_two)
    early_beside = run.pin(early_beside)
    attended_beside, normed_beside = early_beside[:, :q_width], early_beside[:, q_width:]
    lines.turn()
    turned_grads, grads_sent = run(lambda *a: turn_rows(*a, n_fsdp), index, ctx, grads)
    grads_beside = swap(grads_sent, "fsdp", 1)
    lines.pin_team()

    limits = [limit.reshape(1)] + [jnp.zeros((1,), jnp.int32)] * (PARTS - 1)
    acts, acts_beside = {}, {}
    total_rows = n_ctx * rows

    def feed_team(index, carry, last=False, every=False):
        rows_in = lines.team() + lines.rest() if every else lines.team()
        results = run(
            lambda *a: feed(*a[:5], total_rows, True, a[5], last),
            limits[index], ctx, rows_in, grads, feed_w[index], carry,
        )
        acts[index] = tuple(results[:3])
        if every:
            acts_beside[index] = tuple(swap(a, "fsdp", 1) for a in acts[index])
        return tuple(results[3:])

    def feed_rest(index):
        acts[index] = run(
            lambda *a: feed(*a[:5], total_rows, False, act=a[5]),
            limits[index], ctx, lines.rest(), grads, feed_w[index], acts[index],
        )
        acts_beside[index] = tuple(swap(a, "fsdp", 1) for a in acts[index])

    waiting, reduced, other_parts = {}, {}, {}

    def grads_of(index):
        far, near = run(
            lambda *a: weight_grads(*a)[::-1],
            turned, turned_beside, acts[index], acts_beside[index],
        )
        bits = bits_of(n_fsdp)[1:]
        for bit in bits[:-1]:
            total = near.astype(f32) + swap(far, "fsdp", bit).astype(f32)
            cut = total.shape[1] // 2
            far, near = total[:, cut:].astype(bf16), total[:, :cut].astype(bf16)
        waiting[index] = (near, swap(far, "fsdp", bits[-1]))

    def give(near, arrived):
        return (near.astype(f32) + arrived.astype(f32)).astype(bf16)

    def add_far(index):
        reduced[index] = run(give, *waiting[index])
        other_parts[index] = swap(reduced[index], "context", 1)

    carry = feed_team(0, ())
    lines.across_rest()
    carry = feed_team(1, carry)
    lines.pin_rest()
    turned_lines, lines_sent = run(
        lambda *a: turn_rows(*a, n_fsdp), index, ctx, lines.team() + lines.rest()
    )
    turned = (turned_lines, turned_grads)
    turned_beside = (swap(lines_sent, "fsdp", 1), grads_beside)
    feed_rest(0)
    feed_rest(1)
    grads_of(0)
    given = feed_team(2, carry, True)
    d_near, d_beside, d_far, out_near, out_beside, out_far = given
    d_far = swap(d_far, "tensor", 1)
    feed_rest(2)
    grads_of(1)
    d_beside = swap(run(lambda a, b: give(a, b[half:]), d_beside, d_far), "context", 1)
    add_far(0)
    d_middle, d_branch, grad_gain_two = run(
        lambda a, b, *c: middle_back(a, b[:half], *c),
        d_near, d_far, d_beside, middle, gains, grad_mine,
    )
    d_branch_other = swap(d_branch, "tensor", 1)
    grads_of(2)
    d_branch_other = run.pin(d_branch_other)
    d_all = run(lambda *a: to_relative(stack(*a), my_fsdp, n_fsdp), d_branch, d_branch_other)
    d_all_beside = swap(d_all[:, D // 2 :], "fsdp", 1)
    d_all_beside = run.pin(d_all_beside)
    dq_low, *dkv_parts = run(
        attend_back,
        index, queries, low, high, key_at, cos_table, sin_table,
        (d_branch, d_branch_other), out_w, kv_parts,
    )
    dkv_parts = [dkv_parts[0]] + [
        shift(p, "context", -step - 1) for step, p in enumerate(dkv_parts[1:])
    ]
    other_parts[0] = run.pin(other_parts[0])
    reduced[1] = run(give, *waiting[1])

    def halves(values, axis):
        cut = values.shape[axis] // 2
        return (
            lax.slice_in_dim(values, 0, cut, axis=axis),
            lax.slice_in_dim(values, cut, 2 * cut, axis=axis),
        )

    class Reduce:
        def __init__(self, axis, full, full_beside, split, split_beside):
            self.axis, self.other = axis, 1 - axis
            self.full, self.full_beside = full, full_beside
            self.kept, self.kept_beside = split[:, : D // 2], split_beside
            self.todo = [("fsdp", bit) for bit in bits_of(n_fsdp)[1:]]
            self.todo += [("context", bit) for bit in bits_of(n_ctx)]
            self.back = [bit for bit in reversed(bits_of(n_ctx))]
            self.value = None

        def cut(self, total):
            name, bit = self.todo[0]
            if name == "fsdp":
                keep, send = halves(total, self.axis)
                return keep, send.astype(bf16)
            first, second = halves(total, self.other)
            on = (my_ctx & bit) != 0
            return jnp.where(on, second, first), jnp.where(on, first, second).astype(bf16)

        def send(self, pair):
            name, bit = self.todo.pop(0)
            self.keep, sent = pair
            self.sent = swap(sent, name, bit)

        def first(self):
            def product(full, kept, full_beside, kept_beside):
                left, right = stack(kept, kept_beside), stack(full, full_beside)
                if self.axis == 1:
                    left, right = right, left
                return self.cut(dot_rows(left, right))

            self.send(run(product, self.full, self.kept, self.full_beside, self.kept_beside))

        def step(self):
            if self.todo:
                self.send(run(lambda a, b: self.cut(a + b.astype(f32)), self.keep, self.sent))
                return
            if self.value is None:
                self.value = run(give, self.keep, self.sent)
            else:
                self.value = self.join()
            self.bit = self.back.pop(0)
            self.sent = swap(self.value, "context", self.bit)

        def join(self):
            on = (my_ctx & self.bit) != 0

            def both(mine, other):
                return jnp.concatenate(
                    [jnp.where(on, other, mine), jnp.where(on, mine, other)], axis=self.other
                )

            return run(both, self.value, self.sent)

    def place_part(index, placed):
        return run(
            lambda m, a, b, c: place(m, a, b, index, starts, fresh, ff_local, c),
            member.reshape(1), reduced[index], other_parts[index], placed,
        )

    def smalls(gain_rows, gain_other, grad_bias):
        gain_rows = jnp.pad(gain_rows + gain_other, ((0, 6), (0, 0)))
        biases = jnp.pad(grad_bias.reshape(all_heads, HD), ((0, 0), (0, D - HD)))
        return stack(gain_rows, biases)

    steps = [("fsdp", bit) for bit in bits_of(n_fsdp)] + [("context", bit) for bit in bits_of(n_ctx)]

    def small_step(small):
        name, bit = steps.pop(0)
        return run(jnp.add, small, swap(small, name, bit))

    reduce_o = Reduce(1, attended, attended_beside, d_all, d_all_beside)
    reduce_o.first()
    dkv_parts = dkv_parts[:1] + list(run.pin(tuple(dkv_parts[1:])))
    other_parts[1] = swap(after(reduced[1], dkv_parts[-1]), "context", 1)
    d_qkv, dn_mine, dn_other, grad_bias = run(
        project_back, index, dq_low, cos_table, sin_table, qkv_w, dkv_parts
    )
    d_qkv_beside = swap(d_qkv, "fsdp", 1)
    dn_other = swap(dn_other, "tensor", 1)
    reduce_qkv = Reduce(0, d_qkv, d_qkv_beside, normed_rel, normed_beside)
    reduce_qkv.first()
    d_inputs, grad_gain_one = run(
        input_back, dn_mine, dn_other, mine_tokens, gains, d_middle
    )
    d_inputs_other = swap(d_inputs, "tensor", 1)
    add_far(2)
    d_inputs_other = run.pin(d_inputs_other)
    placed = place_part(0, ())
    other_parts[1] = run.pin(other_parts[1])
    reduce_o.step()
    gain_rows = run(stack, grad_gain_one, grad_gain_two)
    gain_other = swap(gain_rows, "tensor", 1)
    out_far = swap(after(out_far, other_parts[1]), "tensor", 1)
    reduce_qkv.step()
    small = run(smalls, gain_rows, gain_other, grad_bias)
    placed = place_part(1, placed)
    out_mine, out_beside = run(
        lambda a, b, c: (a + c[:half].astype(f32), give(b, c[half:])), out_near, out_beside, out_far
    )
    small = small_step(small)
    small = small_step(small)
    reduce_o.step()
    arrived = reduce_qkv.sent
    reduce_qkv.step()
    out_beside = swap(after(out_beside, arrived), "context", 1)
    other_parts[2] = run.pin(other_parts[2])
    reduce_o.step()
    reduce_qkv.step()
    small = small_step(small)
    reduce_o.step()
    out_half = run(
        lambda a, b, c: (a + b + c.astype(f32)).astype(bf16), middle, out_mine, out_beside
    )
    out_half_other = swap(out_half, "tensor", 1)
    reduce_qkv.step()
    small = small_step(small)
    placed = place_part(2, placed)
    while reduce_o.back:
        reduce_o.step()
        reduce_qkv.step()
    while steps:
        small = small_step(small)
    grad_gate, grad_up, grad_down = placed
    grad_o = reduce_o.join().astype(f32)
    grad_qkv = reduce_qkv.join().astype(f32)
    grad_biases = small[8 : 8 + all_heads, :bias_cols]
    small_gains = small[:2, :shard]
    for f in range(1, n_fsdp):
        there = small[8 : 8 + all_heads, f * bias_cols : (f + 1) * bias_cols]
        grad_biases = jnp.where(my_fsdp == f, there, grad_biases)
        small_gains = jnp.where(my_fsdp == f, small[:2, f * shard : (f + 1) * shard], small_gains)
    def restore(low_half, other_half):
        both = mine_first(stack(low_half, other_half))
        return both.astype(f32)

    return (
        restore(out_half, out_half_other),
        restore(d_inputs, d_inputs_other),
        small_gains[0],
        grad_qkv[:, :q_width],
        grad_biases[:heads_local],
        grad_qkv[:, q_width : q_width + kv_width],
        grad_biases[heads_local : heads_local + 1],
        grad_qkv[:, q_width + kv_width :],
        grad_biases[heads_local + 1 :],
        grad_o,
        small_gains[1],
        grad_gate,
        grad_up,
        grad_down,
    )


def solution(mesh):
    in_specs = (
        P(("fsdp", "context"), None),
        P(("fsdp", "context"), None),
        P("fsdp", None),
        P("fsdp", None, None),
        P("fsdp"),
        P("fsdp", "tensor"),
        P("tensor", "fsdp"),
        P("fsdp", "tensor"),
        P("tensor", "fsdp"),
        P("fsdp", "tensor"),
        P("tensor", "fsdp"),
        P("tensor", "fsdp"),
        P("fsdp"),
        P("fsdp", "tensor"),
        P("fsdp", "tensor"),
        P("tensor", "fsdp"),
    )
    out_specs = (
        P(("fsdp", "context"), None),
        P(("fsdp", "context"), None),
        P("fsdp"),
        P("fsdp", "tensor"),
        P("tensor", "fsdp"),
        P("fsdp", "tensor"),
        P("tensor", "fsdp"),
        P("fsdp", "tensor"),
        P("tensor", "fsdp"),
        P("tensor", "fsdp"),
        P("fsdp"),
        P("fsdp", "tensor"),
        P("fsdp", "tensor"),
        P("tensor", "fsdp"),
    )
    return jax.shard_map(
        per_device, mesh=mesh, in_specs=in_specs, out_specs=out_specs, check_vma=False
    )
```
